768 devices in a mesh: lat: 48 (over y_hi, z, core), lon: 16 (over x, y_lo).
Axes of the slice: x: 4, y: 8 (y_hi: 2, y_lo: 4; y = y_hi * 4 + y_lo), z: 12, core: 2. Of those that a mesh axis runs over, the one named last changes fastest.
Arguments:
- fields: bfloat16 [288, 384, 384], P('lat', 'lon'), may hold values from -6 to 6
- norm_gain: float32 [192], replicated, may hold values from 0.1 to 1.9
- project_in: bfloat16 [192, 576], replicated, may hold values from -0.4375 to 0.4375
- project_out: bfloat16 [192, 192], replicated, may hold values from -0.4375 to 0.4375
- bias_table: float32 [48, 6, 144, 23], P('lat', None, 'lon'), may hold values from -4 to 400, as said below
- pad_rows: int32 [288], replicated, may hold values from 0 to 1, as said below
- cotangent: bfloat16 [288, 384, 384], P('lat', 'lon'), may hold values from -6 to 6
Outputs:
- out_fields: bfloat16 [288, 384, 384], P('lat', 'lon')
- field_grads: bfloat16 [288, 384, 384], P('lat', 'lon')
- table_grads: float32 [48, 6, 144, 23], P('lat', None, 'lon')
The draws below stay inside these ranges and needn't reach their ends.
Inputs may be any that keep to these rules, and one draw needn't show every extreme that they name: `bias_table`: entries of order one; some heads and position pairs may carry large entries. `pad_rows`: every row is 1 except the last one or two rows of the grid, which are 0.
All inputs are finite; a program needn't handle non-finite values.
Results may differ from the reference program's by a relative error of at most 0.0095.
Values may be sent and summed in bfloat16 or wider, within the bound.
A program may use at most 64 MiB of HBM per device.

```python
import jax
import jax.numpy as jnp
from jax import lax

WIDTH = 192
HEADS = 6
HEAD_DIM = 32
LEVELS = 2
WIN_LAT = 6
WIN_LON = 12
TOKENS_WIN = 144
OFFSETS = 23
PAIRS = 144
NLAT = 288
NLON = 384
LAT_WINDOWS = 48


def draw_bias_table(key, part):
    shape = (LAT_WINDOWS, HEADS, PAIRS, OFFSETS)
    first = jax.random.fold_in(key, 0)
    return jnp.clip(jax.random.normal(first, shape, jnp.float32), -4.0, 4.0)


def draw_pad_rows(key, part):
    padded = jax.random.randint(key, (), 1, 3)
    return (jnp.arange(NLAT) < NLAT - padded).astype(jnp.int32)


def levels(own_key, shape, cuts, low, high):
    loudness, own = 1.0, jax.random.fold_in(own_key, 6)
    for position, blocks in cuts:
        heights = jnp.exp(jax.random.uniform(jax.random.fold_in(own, position), (blocks,), jnp.float32, low / len(cuts), high / len(cuts)))
        loudness = loudness * jnp.repeat(heights, shape[position] // blocks).reshape([-1 if axis == position else 1 for axis in range(len(shape))])
    return loudness


def noise(key, extent, scale, reach, cuts=(), kind=jnp.bfloat16):
    values = scale * jax.random.normal(key, extent, jnp.float32)
    if cuts:
        values = values * levels(key, extent, cuts, -0.22, 0.18)
    return jnp.clip(values, -reach, reach).astype(kind)


def setup_inputs(seed: int = 0) -> dict:
    arg_keys = jax.random.split(jax.random.key(seed), 8)
    return {
        "fields": noise(arg_keys[0], (NLAT, NLON, LEVELS * WIDTH), 1.0, 6.0, ((0, 48), (1, 16))),
        "norm_gain": jnp.clip(1.0 + 0.18 * jax.random.normal(arg_keys[1], (WIDTH,), jnp.float32), 0.1, 1.9),
        "project_in": noise(arg_keys[2], (WIDTH, 3 * WIDTH), WIDTH ** -0.5, 0.4375),
        "project_out": noise(arg_keys[3], (WIDTH, WIDTH), WIDTH ** -0.5, 0.4375),
        "bias_table": draw_bias_table(jax.random.fold_in(arg_keys[7], 71), 0),
        "pad_rows": draw_pad_rows(jax.random.fold_in(arg_keys[7], 71), 0),
        "cotangent": noise(arg_keys[6], (NLAT, NLON, LEVELS * WIDTH), 1.0, 6.0, ((0, 48), (1, 16))),
    }


epsilon_norm = 1e-05
masked_score = -1e+30

def norm_parts(inputs, norm_gain):
    wide_in = inputs.astype(jnp.float32)
    center = wide_in - lax.optimization_barrier(jnp.mean(wide_in, axis=-1, keepdims=True))
    inverse_spread = lax.rsqrt(lax.optimization_barrier(jnp.mean(center * center, axis=-1, keepdims=True)) + epsilon_norm)
    normed = center * inverse_spread
    return (wide_in, normed, inverse_spread, (normed * norm_gain).astype(jnp.bfloat16))

def offset_selector():
    positions = jnp.arange(WIN_LON, dtype=jnp.int32)
    offsets_flat = (positions[:, None] - positions[None, :] + WIN_LON - 1).reshape(-1)
    return (jnp.arange(OFFSETS, dtype=jnp.int32)[:, None] == offsets_flat[None, :]).astype(jnp.float32)

def expand_bias(table_rows):
    count = table_rows.shape[0]
    zone = LEVELS * WIN_LAT
    spread = jnp.einsum('rhpo,oq->rhpq', table_rows, offset_selector(), precision=lax.Precision.HIGHEST)
    spread = spread.reshape(count, HEADS, zone, zone, WIN_LON, WIN_LON).transpose(0, 1, 2, 4, 3, 5)
    return spread.reshape(count, HEADS, TOKENS_WIN, TOKENS_WIN)

def reduce_bias(grad_sums):
    count = grad_sums.shape[0]
    zone = LEVELS * WIN_LAT
    folded = grad_sums.reshape(count, HEADS, zone, WIN_LON, zone, WIN_LON).transpose(0, 1, 2, 4, 3, 5)
    folded = folded.reshape(count, HEADS, PAIRS, WIN_LON * WIN_LON)
    return jnp.einsum('rhpq,oq->rhpo', folded, offset_selector(), precision=lax.Precision.HIGHEST)

def attend_core(inputs, norm_gain, project_in, bias_block, allowed):
    wide_in, normed, inverse_spread, norm_fields = norm_parts(inputs, norm_gain)
    window_count, token_count = (inputs.shape[0], inputs.shape[1])
    projected = jnp.dot(norm_fields.reshape(-1, WIDTH), project_in, preferred_element_type=jnp.float32).astype(jnp.bfloat16)
    heads_split = projected.reshape(window_count, token_count, 3, HEADS, HEAD_DIM)
    queries = heads_split[:, :, 0]
    key_rows = heads_split[:, :, 1]
    values = heads_split[:, :, 2]
    score_scale = HEAD_DIM ** (-0.5)
    scores = jnp.einsum('bqhd,bkhd->bhqk', queries.astype(jnp.float32), key_rows.astype(jnp.float32)) * score_scale + bias_block[None]
    scores = jnp.where(allowed[None, None], scores, masked_score)
    row_max = lax.optimization_barrier(jnp.max(scores, axis=-1, keepdims=True))
    raised = jnp.exp(scores - row_max)
    weights_full = raised / lax.optimization_barrier(jnp.sum(raised, axis=-1, keepdims=True))
    weights_low = weights_full.astype(jnp.bfloat16)
    mixed = jnp.einsum('bhqk,bkhd->bqhd', weights_low.astype(jnp.float32), values.astype(jnp.float32))
    mixed = mixed.astype(jnp.bfloat16).reshape(window_count, token_count, WIDTH)
    return (wide_in, mixed, (normed, inverse_spread, queries, key_rows, values, weights_full, weights_low))

def finish_output(wide_in, mixed, project_out):
    added = jnp.dot(mixed.reshape(-1, WIDTH), project_out, preferred_element_type=jnp.float32).reshape(wide_in.shape)
    return (wide_in + added).astype(jnp.bfloat16)

def backprop(grads_out, norm_gain, project_in, project_out, saved):
    normed, inverse_spread, queries, key_rows, values, weights_full, weights_low = saved
    window_count, token_count = (grads_out.shape[0], grads_out.shape[1])
    score_scale = HEAD_DIM ** (-0.5)
    grad_mixed = jnp.dot(grads_out.reshape(-1, WIDTH), project_out.T, preferred_element_type=jnp.float32).astype(jnp.bfloat16)
    grad_mixed = grad_mixed.reshape(window_count, token_count, HEADS, HEAD_DIM)
    grad_weights = jnp.einsum('bqhd,bkhd->bhqk', grad_mixed.astype(jnp.float32), values.astype(jnp.float32))
    grad_scores = weights_full * (grad_weights - lax.optimization_barrier(jnp.sum(weights_full * grad_weights, axis=-1, keepdims=True)))
    grad_low = grad_scores.astype(jnp.bfloat16)
    grad_query = jnp.einsum('bhqk,bkhd->bqhd', grad_low.astype(jnp.float32), key_rows.astype(jnp.float32)) * score_scale
    grad_key = jnp.einsum('bhqk,bqhd->bkhd', grad_low.astype(jnp.float32), queries.astype(jnp.float32)) * score_scale
    grad_value = jnp.einsum('bhqk,bqhd->bkhd', weights_low.astype(jnp.float32), grad_mixed.astype(jnp.float32))
    grad_project = jnp.stack([grad_query, grad_key, grad_value], axis=2).reshape(-1, 3 * WIDTH).astype(jnp.bfloat16)
    grad_norm = jnp.dot(grad_project, project_in.T, preferred_element_type=jnp.float32).reshape(window_count, token_count, WIDTH)
    scaled_grad = grad_norm * norm_gain
    centered_grad = scaled_grad - lax.optimization_barrier(jnp.mean(scaled_grad, axis=-1, keepdims=True)) - normed * lax.optimization_barrier(jnp.mean(scaled_grad * normed, axis=-1, keepdims=True))
    grad_input = (grads_out.astype(jnp.float32) + inverse_spread * centered_grad).astype(jnp.bfloat16)
    return (grad_input, grad_scores)

def reference(fields, norm_gain, project_in, project_out, bias_table, pad_rows, cotangent):
    rim_rows = WIN_LAT // 2
    rim_cols = WIN_LON // 2
    rolled = jnp.roll(fields, (-rim_rows, -rim_cols), (0, 1))
    rolled_grads = jnp.roll(cotangent, (-rim_rows, -rim_cols), (0, 1))
    lon_windows = NLON // WIN_LON
    token_band = jnp.arange(TOKENS_WIN, dtype=jnp.int32) // WIN_LON % WIN_LAT

    def to_tokens(block):
        shaped = block.reshape(WIN_LAT, lon_windows, WIN_LON, LEVELS, WIDTH).transpose(1, 3, 0, 2, 4)
        return shaped.reshape(lon_windows, TOKENS_WIN, WIDTH)

    def to_cells(block):
        shaped = block.reshape(lon_windows, LEVELS, WIN_LAT, WIN_LON, WIDTH).transpose(2, 0, 3, 1, 4)
        return shaped.reshape(WIN_LAT, NLON, LEVELS * WIDTH)

    def one_row(window_row):
        first_row = (window_row * WIN_LAT).astype(jnp.int32)
        inputs = to_tokens(lax.dynamic_slice_in_dim(rolled, first_row, WIN_LAT, 0))
        grads_out = to_tokens(lax.dynamic_slice_in_dim(rolled_grads, first_row, WIN_LAT, 0))
        token_rows = ((first_row + rim_rows + token_band) % NLAT).astype(jnp.int32)
        token_valid = pad_rows[token_rows]
        allowed = (jnp.abs(token_rows[:, None] - token_rows[None, :]) < WIN_LAT) & (token_valid[None, :] == 1)
        bias_block = expand_bias(lax.dynamic_slice_in_dim(bias_table, window_row.astype(jnp.int32), 1, 0))[0]
        wide_in, mixed, saved = attend_core(inputs, norm_gain, project_in, bias_block, allowed)
        outputs = finish_output(wide_in, mixed, project_out)
        grad_input, grad_scores = backprop(grads_out, norm_gain, project_in, project_out, saved)
        table_part = reduce_bias(lax.optimization_barrier(jnp.sum(grad_scores, axis=0))[None])[0]
        return (to_cells(outputs), to_cells(grad_input), table_part)
    out_rows, grad_rows, table_grads = lax.map(one_row, jnp.arange(LAT_WINDOWS, dtype=jnp.int32))
    out_fields = jnp.roll(out_rows.reshape(NLAT, NLON, LEVELS * WIDTH), (rim_rows, rim_cols), (0, 1))
    field_grads = jnp.roll(grad_rows.reshape(NLAT, NLON, LEVELS * WIDTH), (rim_rows, rim_cols), (0, 1))
    return (out_fields, field_grads, table_grads)
```

```python
import functools

import jax
import jax.numpy as jnp
from jax import lax
from jax.experimental import pallas as pl
from jax.experimental.pallas import tpu as pltpu
from jax.sharding import PartitionSpec as P

WIDTH = 192
HEADS = 6
HEAD_DIM = 32
LEVELS = 2
WIN_LAT = 6
WIN_LON = 12
ZONE = LEVELS * WIN_LAT
CELLS = WIN_LAT * WIN_LON
TOKENS = LEVELS * CELLS
OFFSETS = 23
SLOT = 24
PAIRS = ZONE * ZONE
RIM_R = WIN_LAT // 2
RIM_C = WIN_LON // 2
WINDOWS = 2
COLS = WINDOWS * WIN_LON
FEATS = LEVELS * WIDTH
BAND = 384
DOWN = 56
SIDE = 24
SCALE = HEAD_DIM**-0.5
EPS = 1e-05
MASKED = -1e30
MESH = pl.DeviceIdType.MESH
F32 = jnp.float32
BF16 = jnp.bfloat16


def dot_nn(a, b):
    return lax.dot_general(a, b, (((1,), (0,)), ((), ())), preferred_element_type=F32)


def dot_nt(a, b):
    return lax.dot_general(a, b, (((1,), (1,)), ((), ())), preferred_element_type=F32)


def dot_tn(a, b):
    return lax.dot_general(a, b, (((0,), (0,)), ((), ())), preferred_element_type=F32)


def kernel(
    lat_size,
    lon_size,
    pairs_here,
    fields_hbm,
    gain_hbm,
    win_hbm,
    wout_hbm,
    bias_hbm,
    pad_hbm,
    cot_hbm,
    out_ref,
    grads_ref,
    table_ref,
    f_in,
    c_in,
    w_in,
    wo_in,
    bias_in,
    gain_ref,
    pad_ref,
    raw,
    xw,
    cw,
    tmp,
    send_down,
    send_side,
    recv_down,
    recv_side,
    bias_msg,
    bias_recv,
    spread,
    bias_flat,
    bias_full,
    w_t,
    xtok,
    ctok,
    xhat,
    spread_inv,
    proj_t,
    k_nat,
    v_nat,
    gmix_t,
    mixed_t,
    gproj_t,
    gflat,
    cells,
    table_msg,
    table_recv,
    in_sem,
    halo_send,
    halo_recv,
    bias_send,
    bias_rsem,
    table_send,
    table_rsem,
):
    lat = lax.axis_index("lat")
    lon = lax.axis_index("lon")
    up = lax.rem(lat + lat_size - 1, lat_size)
    dn = lax.rem(lat + 1, lat_size)
    lf = lax.rem(lon + lon_size - 1, lon_size)
    rt = lax.rem(lon + 1, lon_size)

    barrier = pltpu.get_barrier_semaphore()
    for dev in ((up, lon), (up, lf), (dn, lon), (dn, rt)):
        pl.semaphore_signal(barrier, inc=1, device_id=dev, device_id_type=MESH)

    def greet(s, carry):
        peer = lax.rem(lon + s, lon_size)
        pl.semaphore_signal(barrier, inc=1, device_id=(lat, peer), device_id_type=MESH)
        return carry

    lax.fori_loop(1, lon_size, greet, 0)

    loads = [
        pltpu.make_async_copy(src, dst, in_sem.at[n])
        for n, (src, dst) in enumerate(
            (
                (fields_hbm, f_in),
                (cot_hbm, c_in),
                (bias_hbm, bias_in),
                (win_hbm, w_in),
                (wout_hbm, wo_in),
                (gain_hbm, gain_ref),
                (pad_hbm, pad_ref),
            )
        )
    ]
    for load in loads:
        load.start()

    def halo_copy(kind, piece):
        inward = kind < 2
        row_dev, col_dev = (up, lf) if inward else (dn, rt)
        dev = ((row_dev, lon), (lat, col_dev), (row_dev, col_dev))[piece]
        if piece == 0:
            src, dst = send_down.at[kind], recv_down.at[kind]
        else:
            src, dst = send_side.at[kind, piece - 1], recv_side.at[kind, piece - 1]
        return pltpu.make_async_remote_copy(
            src_ref=src,
            dst_ref=dst,
            send_sem=halo_send.at[kind, piece],
            recv_sem=halo_recv.at[kind, piece],
            device_id=dev,
            device_id_type=MESH,
        )

    def pack_in(src, kind, windows):
        for r in range(WIN_LAT):
            raw[r * COLS : (r + 1) * COLS, :] = src[r].astype(F32)
        for r in range(RIM_R):
            base = r * COLS
            tmp[r * 12 : r * 12 + 12, :] = raw[base + 6 : base + 18, :]
            tmp[36 + r * 6 : 42 + r * 6, :] = raw[base + 18 : base + 24, :]
            tmp[88 + r * 6 : 94 + r * 6, :] = raw[base : base + 6, :]
            below = (r + RIM_R) * COLS
            tmp[64 + r * 6 : 70 + r * 6, :] = raw[below : below + 6, :]
            windows[r * 12 : r * 12 + 12, :] = raw[below + 6 : below + 18, :]
            windows[CELLS + r * 12 : CELLS + r * 12 + 6, :] = raw[below + 18 : below + 24, :]
        send_down[kind] = tmp[0:DOWN, :].astype(BF16)
        send_side[kind, 0] = tmp[64 : 64 + SIDE, :].astype(BF16)
        send_side[kind, 1] = tmp[88 : 88 + SIDE, :].astype(BF16)

    def unpack_in(kind, windows):
        tmp[0:DOWN, :] = recv_down[kind].astype(F32)
        tmp[64 : 64 + SIDE, :] = recv_side[kind, 0].astype(F32)
        tmp[88 : 88 + SIDE, :] = recv_side[kind, 1].astype(F32)
        windows[36:72, :] = tmp[0:36, :]
        for r in range(RIM_R):
            top = CELLS + r * 12
            low = CELLS + (r + RIM_R) * 12
            windows[low : low + 6, :] = tmp[36 + r * 6 : 42 + r * 6, :]
            windows[top + 6 : top + 12, :] = tmp[64 + r * 6 : 70 + r * 6, :]
            windows[low + 6 : low + 12, :] = tmp[88 + r * 6 : 94 + r * 6, :]

    tmp[...] = jnp.zeros_like(tmp)
    loads[0].wait()
    pack_in(f_in, 0, xw)
    loads[2].wait()
    bias_msg[...] = jnp.zeros_like(bias_msg)
    for r in range(pairs_here):
        for h in range(HEADS):
            bias_msg[h : h + 1, r * SLOT : r * SLOT + OFFSETS] = bias_in[h, r]
    bias_recv[lon] = bias_msg[...]
    loads[1].wait()
    pack_in(c_in, 1, cw)

    pl.semaphore_wait(barrier, lon_size + 3)

    def bias_copy(s):
        peer = lax.rem(lon + s, lon_size)
        return pltpu.make_async_remote_copy(
            src_ref=bias_msg,
            dst_ref=bias_recv.at[lon],
            send_sem=bias_send.at[s],
            recv_sem=bias_rsem.at[lon],
            device_id=(lat, peer),
            device_id_type=MESH,
        )

    def bias_arrival(s):
        source = lax.rem(lon + s, lon_size)
        return pltpu.make_async_remote_copy(
            src_ref=bias_msg,
            dst_ref=bias_recv.at[source],
            send_sem=bias_send.at[s],
            recv_sem=bias_rsem.at[source],
            device_id=(lat, source),
            device_id_type=MESH,
        )

    for piece in (0, 2, 1):
        halo_copy(0, piece).start()

    def send_bias(s, carry):
        bias_copy(s).start()
        return carry

    lax.fori_loop(1, lon_size, send_bias, 0)
    for piece in (0, 2, 1):
        halo_copy(1, piece).start()

    gflat[...] = jnp.zeros_like(gflat)
    table_msg[...] = jnp.zeros_like(table_msg)
    spread[...] = jnp.zeros_like(spread)
    lane = lax.broadcasted_iota(jnp.int32, (BAND, TOKENS), 0)
    query = lax.broadcasted_iota(jnp.int32, (BAND, TOKENS), 1)
    picked = (query // WIN_LON) * SLOT + query % WIN_LON + WIN_LON - 1
    selector = (lane == picked).astype(F32).astype(BF16)
    loads[3].wait()
    loads[4].wait()
    loads[5].wait()
    loads[6].wait()
    w_t[...] = w_in[...].astype(F32).T.astype(BF16)

    total_rows = lat_size * WIN_LAT
    first_row = lat * WIN_LAT + RIM_R
    key_band = (lax.broadcasted_iota(jnp.int32, (TOKENS, TOKENS), 0) // WIN_LON) % WIN_LAT
    query_band = (lax.broadcasted_iota(jnp.int32, (TOKENS, TOKENS), 1) // WIN_LON) % WIN_LAT
    key_row = lax.rem(first_row + key_band, total_rows)
    query_row = lax.rem(first_row + query_band, total_rows)
    real = jnp.zeros((TOKENS, TOKENS), jnp.int32)
    for a in range(WIN_LAT):
        real = jnp.where(key_band == a, pad_ref[lax.rem(first_row + a, total_rows)], real)
    allowed = (jnp.abs(query_row - key_row) < WIN_LAT) & (real == 1)

    def wait_bias(s, carry):
        bias_arrival(s).wait_recv()
        return carry

    lax.fori_loop(1, lon_size, wait_bias, 0)
    for p in range(PAIRS):
        owner, r = p // pairs_here, p % pairs_here
        zq, zt = p // ZONE, p % ZONE
        spread[zt * 8 : zt * 8 + 8, zq * SLOT : (zq + 1) * SLOT] = bias_recv[
            owner, :, r * SLOT : (r + 1) * SLOT
        ]
    for b in range(WIN_LON):
        table = spread[...]
        if b:
            table = pltpu.roll(table, b, 1)
        high = table.astype(BF16)
        rest = table - high.astype(F32)
        middle = rest.astype(BF16)
        low = (rest - middle.astype(F32)).astype(BF16)
        wide = dot_nn(high, selector) + (dot_nn(middle, selector) + dot_nn(low, selector))
        for zt in range(ZONE):
            row = (zt * WIN_LON + b) * 8
            bias_flat[0, row : row + 8, :] = wide[zt * 8 : zt * 8 + 8, 0:128]
            bias_flat[1, row : row + 8, 0 : TOKENS - 128] = wide[zt * 8 : zt * 8 + 8, 128:TOKENS]
    for h in range(HEADS):
        left = bias_flat[0, pl.ds(h, TOKENS, stride=8), :]
        right = bias_flat[1, pl.ds(h, TOKENS, stride=8), :]
        whole = jnp.concatenate([left, right[:, 0 : TOKENS - 128]], axis=1)
        bias_full[h] = jnp.where(allowed, whole, MASKED)

    gain = gain_ref[...]
    for piece in range(3):
        halo_copy(0, piece).wait_recv()
    unpack_in(0, xw)
    for w in range(WINDOWS):
        block = xw[w * CELLS : (w + 1) * CELLS, :]
        x = jnp.concatenate([block[:, :WIDTH], block[:, WIDTH:]], axis=0)
        xtok[w] = x
        center = x - jnp.mean(x, axis=1, keepdims=True)
        inverse = lax.rsqrt(jnp.mean(center * center, axis=1, keepdims=True) + EPS)
        normed = center * inverse
        xhat[w] = normed
        spread_inv[w] = inverse
        x_n = (normed * gain).astype(BF16)
        proj_t[w] = dot_nt(w_t[...], x_n).astype(BF16)
        kv = dot_nn(x_n, w_in[:, WIDTH:]).astype(BF16)
        for h in range(HEADS):
            k_nat[w, h] = kv[:, h * HEAD_DIM : (h + 1) * HEAD_DIM]
            v_nat[w, h] = kv[:, WIDTH + h * HEAD_DIM : WIDTH + (h + 1) * HEAD_DIM]
    for piece in range(3):
        halo_copy(1, piece).wait_recv()
    unpack_in(1, cw)
    for w in range(WINDOWS):
        block = cw[w * CELLS : (w + 1) * CELLS, :]
        c = jnp.concatenate([block[:, :WIDTH], block[:, WIDTH:]], axis=0)
        ctok[w] = c
        gmix_t[w] = dot_nt(wo_in[...], c.astype(BF16)).astype(BF16)

    def one_head(h, carry):
        at_q = pl.ds(pl.multiple_of(h * HEAD_DIM, HEAD_DIM), HEAD_DIM)
        at_k = pl.ds(pl.multiple_of(WIDTH + h * HEAD_DIM, HEAD_DIM), HEAD_DIM)
        at_v = pl.ds(pl.multiple_of(2 * WIDTH + h * HEAD_DIM, HEAD_DIM), HEAD_DIM)
        bias = bias_full[h]
        summed = None
        for w in range(WINDOWS):
            q_t = proj_t[w, at_q, :]
            g_t = gmix_t[w, at_q, :]
            scores = dot_nn(k_nat[w, h], q_t) * SCALE + bias
            raised = jnp.exp(scores - jnp.max(scores, axis=0, keepdims=True))
            weights = raised * (1.0 / jnp.sum(raised, axis=0, keepdims=True))
            weights_low = weights.astype(BF16)
            mixed_t[w, at_q, :] = dot_nn(proj_t[w, at_v, :], weights_low).astype(BF16)
            grad_w = dot_nn(v_nat[w, h], g_t)
            grad_s = weights * (grad_w - jnp.sum(weights * grad_w, axis=0, keepdims=True))
            grad_low = grad_s.astype(BF16)
            gproj_t[w, at_q, :] = (dot_nn(proj_t[w, at_k, :], grad_low) * SCALE).astype(BF16)
            gproj_t[w, at_k, :] = (dot_nt(q_t, grad_low) * SCALE).astype(BF16)
            gproj_t[w, at_v, :] = dot_nt(g_t, weights_low).astype(BF16)
            summed = grad_s if summed is None else summed + grad_s
        gflat[0, pl.ds(h, TOKENS, stride=8), :] = summed[:, 0:128]
        gflat[1, pl.ds(h, TOKENS, stride=8), 0 : TOKENS - 128] = summed[:, 128:TOKENS]
        return carry

    for h in range(HEADS):
        one_head(h, 0)

    def give_back(kind, tokens):
        for w in range(WINDOWS):
            cells[w * CELLS : (w + 1) * CELLS, 0:WIDTH] = tokens[w][0:CELLS]
            cells[w * CELLS : (w + 1) * CELLS, WIDTH:] = tokens[w][CELLS:]
        tmp[0:36, :] = cells[36:72, :]
        for r in range(RIM_R):
            top = CELLS + r * 12
            low = CELLS + (r + RIM_R) * 12
            tmp[36 + r * 6 : 42 + r * 6, :] = cells[low : low + 6, :]
            tmp[64 + r * 6 : 70 + r * 6, :] = cells[top + 6 : top + 12, :]
            tmp[88 + r * 6 : 94 + r * 6, :] = cells[low + 6 : low + 12, :]
        send_down[kind] = tmp[0:DOWN, :].astype(BF16)
        send_side[kind, 0] = tmp[64 : 64 + SIDE, :].astype(BF16)
        send_side[kind, 1] = tmp[88 : 88 + SIDE, :].astype(BF16)
        for piece in (0, 2, 1):
            halo_copy(kind, piece).start()
        own = raw if kind == 2 else xw
        for r in range(RIM_R):
            below = (r + RIM_R) * COLS
            own[below + 6 : below + 18, :] = cells[r * 12 : r * 12 + 12, :]
            own[below + 18 : below + 24, :] = cells[CELLS + r * 12 : CELLS + r * 12 + 6, :]

    def take_back(kind, dst):
        own = raw if kind == 2 else xw
        for piece in range(3):
            halo_copy(kind, piece).wait_recv()
        tmp[0:DOWN, :] = recv_down[kind].astype(F32)
        tmp[64 : 64 + SIDE, :] = recv_side[kind, 0].astype(F32)
        tmp[88 : 88 + SIDE, :] = recv_side[kind, 1].astype(F32)
        for r in range(RIM_R):
            base = r * COLS
            below = (r + RIM_R) * COLS
            own[base + 6 : base + 18, :] = tmp[r * 12 : r * 12 + 12, :]
            own[base + 18 : base + 24, :] = tmp[36 + r * 6 : 42 + r * 6, :]
            own[base : base + 6, :] = tmp[88 + r * 6 : 94 + r * 6, :]
            own[below : below + 6, :] = tmp[64 + r * 6 : 70 + r * 6, :]
        for r in range(WIN_LAT):
            dst[r] = own[r * COLS : (r + 1) * COLS, :].astype(BF16)

    give_back(2, [xtok[w] + dot_tn(mixed_t[w], wo_in[...]) for w in range(WINDOWS)])

    grads = []
    for w in range(WINDOWS):
        scaled = dot_tn(gproj_t[w], w_t[...]) * gain
        normed = xhat[w]
        centered = (
            scaled
            - jnp.mean(scaled, axis=1, keepdims=True)
            - normed * jnp.mean(scaled * normed, axis=1, keepdims=True)
        )
        grads.append(ctok[w] + spread_inv[w] * centered)
    give_back(3, grads)

    total = jnp.zeros((ZONE * 8, BAND), F32)
    for b in range(WIN_LON):
        picked_rows = []
        for zt in range(ZONE):
            row = (zt * WIN_LON + b) * 8
            picked_rows.append(
                jnp.concatenate(
                    [
                        gflat[0, row : row + 8, :],
                        gflat[1, row : row + 8, 0 : TOKENS - 128],
                    ],
                    axis=1,
                )
            )
        part = jnp.concatenate(picked_rows, axis=0)
        high = part.astype(BF16)
        low = (part - high.astype(F32)).astype(BF16)
        placed = dot_nt(high, selector) + dot_nt(low, selector)
        if b:
            placed = pltpu.roll(placed, BAND - b, 1)
        total = total + placed
    spread[...] = total
    for p in range(PAIRS):
        owner, r = p // pairs_here, p % pairs_here
        zq, zt = p // ZONE, p % ZONE
        table_msg[owner, :, r * SLOT : (r + 1) * SLOT] = spread[
            zt * 8 : zt * 8 + 8, zq * SLOT : (zq + 1) * SLOT
        ]

    def table_copy(s):
        peer = lax.rem(lon + s, lon_size)
        return pltpu.make_async_remote_copy(
            src_ref=table_msg.at[peer],
            dst_ref=table_recv.at[lon],
            send_sem=table_send.at[s],
            recv_sem=table_rsem.at[lon],
            device_id=(lat, peer),
            device_id_type=MESH,
        )

    def table_arrival(s):
        source = lax.rem(lon + s, lon_size)
        return pltpu.make_async_remote_copy(
            src_ref=table_msg.at[source],
            dst_ref=table_recv.at[source],
            send_sem=table_send.at[s],
            recv_sem=table_rsem.at[source],
            device_id=(lat, source),
            device_id_type=MESH,
        )

    def send_table(s, carry):
        table_copy(s).start()
        return carry

    lax.fori_loop(1, lon_size, send_table, 0)
    table_recv[lon] = table_msg[lon]

    take_back(2, out_ref)
    take_back(3, grads_ref)

    def wait_table(s, carry):
        table_arrival(s).wait_recv()
        return carry

    lax.fori_loop(1, lon_size, wait_table, 0)
    added = table_recv[0]
    for j in range(1, lon_size):
        added = added + table_recv[j]
    bias_msg_out = added
    for r in range(pairs_here):
        piece = bias_msg_out[:, r * SLOT : r * SLOT + OFFSETS]
        for h in range(HEADS):
            table_ref[h, r] = piece[h : h + 1, :]

    for kind in range(4):
        for piece in range(3):
            halo_copy(kind, piece).wait_send()

    def drain(s, carry):
        bias_copy(s).wait_send()
        table_copy(s).wait_send()
        return carry

    lax.fori_loop(1, lon_size, drain, 0)


def solution(mesh):
    lat_size, lon_size = mesh.shape["lat"], mesh.shape["lon"]
    pairs_here = PAIRS // lon_size
    lanes = -(-pairs_here * SLOT // 128) * 128

    def per_device(fields, norm_gain, project_in, project_out, bias_table, pad_rows, cotangent):
        hbm_spec = pl.BlockSpec(memory_space=pltpu.HBM)
        vmem_spec = pl.BlockSpec(memory_space=pltpu.VMEM)
        out_fields, field_grads, table_grads = pl.pallas_call(
            functools.partial(kernel, lat_size, lon_size, pairs_here),
            out_shape=(
                jax.ShapeDtypeStruct(fields.shape, BF16),
                jax.ShapeDtypeStruct(fields.shape, BF16),
                jax.ShapeDtypeStruct((HEADS, pairs_here, 1, OFFSETS), F32),
            ),
            in_specs=[hbm_spec] * 7,
            out_specs=(vmem_spec, vmem_spec, vmem_spec),
            scratch_shapes=[
                pltpu.VMEM(fields.shape, BF16),
                pltpu.VMEM(fields.shape, BF16),
                pltpu.VMEM(project_in.shape, BF16),
                pltpu.VMEM(project_out.shape, BF16),
                pltpu.VMEM((HEADS, pairs_here, 1, OFFSETS), F32),
                pltpu.VMEM((1, WIDTH), F32),
                pltpu.SMEM(pad_rows.shape, jnp.int32),
                pltpu.VMEM((WIN_LAT * COLS, FEATS), F32),
                pltpu.VMEM((WINDOWS * CELLS, FEATS), F32),
                pltpu.VMEM((WINDOWS * CELLS, FEATS), F32),
                pltpu.VMEM((112, FEATS), F32),
                pltpu.VMEM((4, DOWN, FEATS), BF16),
                pltpu.VMEM((4, 2, SIDE, FEATS), BF16),
                pltpu.VMEM((4, DOWN, FEATS), BF16),
                pltpu.VMEM((4, 2, SIDE, FEATS), BF16),
                pltpu.VMEM((8, lanes), F32),
                pltpu.VMEM((lon_size, 8, lanes), F32),
                pltpu.VMEM((ZONE * 8, BAND), F32),
                pltpu.VMEM((2, TOKENS * 8, 128), F32),
                pltpu.VMEM((HEADS, TOKENS, TOKENS), F32),
                pltpu.VMEM((3 * WIDTH, WIDTH), BF16),
                pltpu.VMEM((WINDOWS, TOKENS, WIDTH), F32),
                pltpu.VMEM((WINDOWS, TOKENS, WIDTH), F32),
                pltpu.VMEM((WINDOWS, TOKENS, WIDTH), F32),
                pltpu.VMEM((WINDOWS, TOKENS, 1), F32),
                pltpu.VMEM((WINDOWS, 3 * WIDTH, TOKENS), BF16),
                pltpu.VMEM((WINDOWS, HEADS, TOKENS, HEAD_DIM), BF16),
                pltpu.VMEM((WINDOWS, HEADS, TOKENS, HEAD_DIM), BF16),
                pltpu.VMEM((WINDOWS, WIDTH, TOKENS), BF16),
                pltpu.VMEM((WINDOWS, WIDTH, TOKENS), BF16),
                pltpu.VMEM((WINDOWS, 3 * WIDTH, TOKENS), BF16),
                pltpu.VMEM((2, TOKENS * 8, 128), F32),
                pltpu.VMEM((WINDOWS * CELLS, FEATS), F32),
                pltpu.VMEM((lon_size, 8, lanes), F32),
                pltpu.VMEM((lon_size, 8, lanes), F32),
                pltpu.SemaphoreType.DMA((7,)),
                pltpu.SemaphoreType.DMA((4, 3)),
                pltpu.SemaphoreType.DMA((4, 3)),
                pltpu.SemaphoreType.DMA((lon_size,)),
                pltpu.SemaphoreType.DMA((lon_size,)),
                pltpu.SemaphoreType.DMA((lon_size,)),
                pltpu.SemaphoreType.DMA((lon_size,)),
            ],
            compiler_params=pltpu.CompilerParams(
                collective_id=0, has_side_effects=True, vmem_limit_bytes=48 << 20
            ),
        )(
            *(
                pltpu.with_memory_space_constraint(x, pltpu.HBM)
                for x in (
                    fields,
                    norm_gain.reshape(1, WIDTH),
                    project_in,
                    project_out,
                    bias_table.reshape(HEADS, pairs_here, 1, OFFSETS),
                    pad_rows,
                    cotangent,
                )
            )
        )
        return out_fields, field_grads, table_grads.reshape(bias_table.shape)

    in_specs = (
        P("lat", "lon", None),
        P(),
        P(),
        P(),
        P("lat", None, "lon", None),
        P(),
        P("lat", "lon", None),
    )
    out_specs = (P("lat", "lon", None), P("lat", "lon", None), P("lat", None, "lon", None))
    return jax.shard_map(
        per_device, mesh=mesh, in_specs=in_specs, out_specs=out_specs, check_vma=False
    )
```

```python
import functools

import jax
import jax.numpy as jnp
from jax import lax
from jax.experimental import pallas as pl
from jax.experimental.pallas import tpu as pltpu
from jax.sharding import PartitionSpec as P

WIDTH = 192
HEADS = 6
HEAD_DIM = 32
LEVELS = 2
WIN_LAT = 6
WIN_LON = 12
ZONE = LEVELS * WIN_LAT
CELLS = WIN_LAT * WIN_LON
TOKENS = LEVELS * CELLS
OFFSETS = 23
SLOT = 24
PAIRS = ZONE * ZONE
RIM_R = WIN_LAT // 2
RIM_C = WIN_LON // 2
WINDOWS = 2
COLS = WINDOWS * WIN_LON
FEATS = LEVELS * WIDTH
BAND = 384
BIG = 56
SMALL = 24
SCALE = HEAD_DIM**-0.5
EPS = 1e-05
MASKED = -1e30
MESH = pl.DeviceIdType.MESH
F32 = jnp.float32
BF16 = jnp.bfloat16


def dot_nn(a, b):
    return lax.dot_general(a, b, (((1,), (0,)), ((), ())), preferred_element_type=F32)


def dot_nt(a, b):
    return lax.dot_general(a, b, (((1,), (1,)), ((), ())), preferred_element_type=F32)


def dot_tn(a, b):
    return lax.dot_general(a, b, (((0,), (0,)), ((), ())), preferred_element_type=F32)


def kernel(
    lat_size,
    lon_size,
    pairs_here,
    fields_hbm,
    gain_hbm,
    win_hbm,
    wout_hbm,
    bias_hbm,
    pad_hbm,
    cot_hbm,
    out_ref,
    grads_ref,
    table_ref,
    f_in,
    c_in,
    w_in,
    wo_in,
    bias_in,
    gain_ref,
    pad_ref,
    raw,
    xw,
    tmp,
    send_big,
    send_small,
    in_big,
    in_small,
    res_big,
    res_small,
    back_big,
    back_small,
    bias_msg,
    bias_recv,
    spread,
    bias_flat,
    bias_full,
    w_t,
    xtok,
    ctok,
    xhat,
    spread_inv,
    proj_t,
    k_nat,
    v_nat,
    gmix_t,
    mixed_t,
    gproj_t,
    gflat,
    cells,
    table_msg,
    table_recv,
    selector,
    load_sem,
    halo_send,
    halo_recv,
    back_send,
    back_recv,
    bias_send,
    bias_rsem,
    table_send,
    table_rsem,
    ready_sem,
):
    lat = lax.axis_index("lat")
    lon = lax.axis_index("lon")
    up = lax.rem(lat + lat_size - 1, lat_size)
    dn = lax.rem(lat + 1, lat_size)
    lf = lax.rem(lon + lon_size - 1, lon_size)
    rt = lax.rem(lon + 1, lon_size)
    group = lat_size // 2
    place = lax.rem(lat, group)
    is_first = place == 0
    is_last = place == group - 1
    before_last = place == group - 2
    one_if_last = jnp.where(is_last, 1, 0)
    one_if_first = jnp.where(is_first, 1, 0)
    below = jnp.where(is_last, dn, lat)
    above = jnp.where(is_first, lat, up)

    barrier = pltpu.get_barrier_semaphore()

    def signal(dev):
        pl.semaphore_signal(barrier, inc=1, device_id=dev, device_id_type=MESH)

    def greet_seam(s, carry):
        signal((up, lax.rem(lon + s, lon_size)))
        return carry

    def greet(s, carry):
        signal((lat, lax.rem(lon + s, lon_size)))
        return carry

    @pl.when(is_first)
    def _():
        lax.fori_loop(0, lon_size, greet_seam, 0)

    @pl.when(jnp.logical_not(is_first))
    def _():
        signal((up, lon))
        signal((up, lf))

    @pl.when(jnp.logical_not(is_last))
    def _():
        signal((dn, lon))
        lax.fori_loop(1, lon_size, greet, 0)

    @pl.when(jnp.logical_not(is_last | before_last))
    def _():
        signal((dn, rt))

    loads = [
        pltpu.make_async_copy(src, dst, load_sem.at[n])
        for n, (src, dst) in enumerate(
            (
                (fields_hbm, f_in),
                (cot_hbm, c_in),
                (bias_hbm, bias_in),
                (win_hbm, w_in),
                (wout_hbm, wo_in),
                (gain_hbm, gain_ref),
                (pad_hbm, pad_ref),
            )
        )
    ]
    for load in loads:
        load.start()

    def remote(src, dst, send, recv, dev):
        return pltpu.make_async_remote_copy(
            src_ref=src,
            dst_ref=dst,
            send_sem=send,
            recv_sem=recv,
            device_id=dev,
            device_id_type=MESH,
        )

    def big_last(kind):
        return remote(
            send_big.at[kind, 0],
            in_big.at[kind, 1, 0],
            halo_send.at[kind, 0],
            halo_recv.at[kind, 1, 0],
            (dn, lon),
        )

    def big_up(kind):
        return remote(
            send_big.at[kind, 1],
            in_big.at[kind, 0, 1],
            halo_send.at[kind, 1],
            halo_recv.at[kind, 0, 0],
            (up, lon),
        )

    def small_low(kind):
        return remote(
            send_small.at[kind, 0],
            in_small.at[kind, one_if_last, 0],
            halo_send.at[kind, 2],
            halo_recv.at[kind, one_if_last, 1],
            (below, lf),
        )

    def small_top(kind):
        return remote(
            send_small.at[kind, 1],
            in_small.at[kind, one_if_first, 1],
            halo_send.at[kind, 3],
            halo_recv.at[kind, one_if_first, 2],
            (above, lf),
        )

    def wait_halo(kind, slot):
        remote(
            send_big.at[kind, 0],
            in_big.at[kind, slot, 1 - slot],
            halo_send.at[kind, 0],
            halo_recv.at[kind, slot, 0],
            (dn, lon),
        ).wait_recv()
        for half in range(2):
            remote(
                send_small.at[kind, half],
                in_small.at[kind, slot, half],
                halo_send.at[kind, 2],
                halo_recv.at[kind, slot, 1 + half],
                (dn, lon),
            ).wait_recv()

    def pack_in(src, kind):
        for r in range(WIN_LAT):
            raw[r * COLS : (r + 1) * COLS, :] = src[r].astype(F32)
        for half, first in ((0, RIM_R), (1, 0)):
            base, side = half * 88, 64 + half * 88
            for r in range(RIM_R):
                row = (first + r) * COLS
                tmp[base + r * 12 : base + r * 12 + 12, :] = raw[row + 6 : row + 18, :]
                tmp[base + 36 + r * 6 : base + 42 + r * 6, :] = raw[row + 18 : row + 24, :]
                tmp[side + r * 6 : side + 6 + r * 6, :] = raw[row : row + 6, :]
            piece = tmp[base : base + BIG, :].astype(BF16)
            send_big[kind, half] = piece
            in_big[kind, half, half] = piece
            send_small[kind, half] = tmp[side : side + SMALL, :].astype(BF16)

    def unpack_in(kind, slot):
        for half in range(2):
            base, side = half * 88, 64 + half * 88
            tmp[base : base + BIG, :] = in_big[kind, slot, half].astype(F32)
            tmp[side : side + SMALL, :] = in_small[kind, slot, half].astype(F32)
            xw[36 * half : 36 * half + 36, :] = tmp[base : base + 36, :]
            for r in range(RIM_R):
                row = CELLS + (RIM_R * half + r) * 12
                xw[row : row + 6, :] = tmp[base + 36 + r * 6 : base + 42 + r * 6, :]
                xw[row + 6 : row + 12, :] = tmp[side + r * 6 : side + 6 + r * 6, :]

    tmp[...] = jnp.zeros_like(tmp)
    loads[0].wait()
    pack_in(f_in, 0)
    loads[2].wait()
    bias_msg[...] = jnp.zeros_like(bias_msg)
    for r in range(pairs_here):
        for h in range(HEADS):
            bias_msg[h : h + 1, r * SLOT : r * SLOT + OFFSETS] = bias_in[h, r]
    bias_recv[0, lon] = bias_msg[...]
    loads[1].wait()
    pack_in(c_in, 1)

    pl.semaphore_wait(barrier, jnp.where(is_first | is_last, lon_size + 1, lon_size + 3))

    @pl.when(before_last)
    def _():
        pl.semaphore_signal(ready_sem, inc=1, device_id=(dn, rt), device_id_type=MESH)

    def bias_copy(s):
        return remote(
            bias_msg,
            bias_recv.at[one_if_last, lon],
            bias_send.at[s],
            bias_rsem.at[one_if_last, lon],
            (below, lax.rem(lon + s, lon_size)),
        )

    def bias_arrival(slot, s):
        source = lax.rem(lon + s, lon_size)
        return remote(
            bias_msg,
            bias_recv.at[slot, source],
            bias_send.at[s],
            bias_rsem.at[slot, source],
            (dn, lon),
        )

    def send_bias(s, carry):
        bias_copy(s).start()
        return carry

    for kind in range(2):

        @pl.when(is_last)
        def _():
            big_last(kind).start()

        small_low(kind).start()

        @pl.when(jnp.logical_not(is_first))
        def _():
            big_up(kind).start()

        @pl.when(jnp.logical_not(is_last))
        def _():
            small_top(kind).start()

        if kind == 0:
            lax.fori_loop(1 - one_if_last, lon_size, send_bias, 0)

    @pl.when(is_last)
    def _():
        pl.semaphore_wait(ready_sem, 1)
        for kind in range(2):
            small_top(kind).start()

    gflat[...] = jnp.zeros_like(gflat)
    table_msg[...] = jnp.zeros_like(table_msg)
    spread[...] = jnp.zeros_like(spread)
    lane = lax.broadcasted_iota(jnp.int32, (BAND, TOKENS), 0)
    query = lax.broadcasted_iota(jnp.int32, (BAND, TOKENS), 1)
    picked = (query // WIN_LON) * SLOT + query % WIN_LON + WIN_LON - 1
    selector[...] = (lane == picked).astype(F32).astype(BF16)
    loads[3].wait()
    loads[4].wait()
    loads[5].wait()
    loads[6].wait()
    w_t[...] = w_in[...].astype(F32).T.astype(BF16)
    total_rows = lat_size * WIN_LAT
    key_band = (lax.broadcasted_iota(jnp.int32, (TOKENS, TOKENS), 0) // WIN_LON) % WIN_LAT
    query_band = (lax.broadcasted_iota(jnp.int32, (TOKENS, TOKENS), 1) // WIN_LON) % WIN_LAT

    def back_copy_big(kind, slot):
        return remote(
            res_big.at[kind, slot, 1 - slot],
            back_big.at[kind, 1 - slot],
            back_send.at[kind, slot, 0],
            back_recv.at[kind, 1 - slot],
            (jnp.where(slot == 0, dn, up), lon),
        )

    def back_copy_small(kind, slot, half):
        owner = lax.rem(lat + half - slot + lat_size, lat_size)
        return remote(
            res_small.at[kind, slot, half],
            back_small.at[kind, half],
            back_send.at[kind, slot, 1 + half],
            back_recv.at[kind, 2 + half],
            (owner, rt),
        )

    def give_back(kind, slot, tokens):
        for w in range(WINDOWS):
            cells[w * CELLS : (w + 1) * CELLS, 0:WIDTH] = tokens[w][0:CELLS]
            cells[w * CELLS : (w + 1) * CELLS, WIDTH:] = tokens[w][CELLS:]
        for half in range(2):
            base, side = half * 88, 64 + half * 88
            tmp[base : base + 36, :] = cells[36 * half : 36 * half + 36, :]
            for r in range(RIM_R):
                row = CELLS + (RIM_R * half + r) * 12
                tmp[base + 36 + r * 6 : base + 42 + r * 6, :] = cells[row : row + 6, :]
                tmp[side + r * 6 : side + 6 + r * 6, :] = cells[row + 6 : row + 12, :]
            res_big[kind, slot, half] = tmp[base : base + BIG, :].astype(BF16)
            res_small[kind, slot, half] = tmp[side : side + SMALL, :].astype(BF16)
        for half in range(2):
            back_copy_small(kind, slot, half).start()
        back_copy_big(kind, slot).start()
        back_big[kind, slot] = res_big[kind, slot, slot]

    def table_copy(slot, s):
        peer = lax.rem(lon + s, lon_size)
        return remote(
            table_msg.at[slot, peer],
            table_recv.at[lon],
            table_send.at[slot, s],
            table_rsem.at[lon],
            (jnp.where(slot == 0, lat, up), peer),
        )

    def table_arrival(s):
        source = lax.rem(lon + s, lon_size)
        return remote(
            table_msg.at[0, source],
            table_recv.at[source],
            table_send.at[0, s],
            table_rsem.at[source],
            (lat, source),
        )

    def window_row(slot, carry):
        gain = gain_ref[...]
        wait_halo(0, slot)
        unpack_in(0, slot)
        for w in range(WINDOWS):
            block = xw[w * CELLS : (w + 1) * CELLS, :]
            x = jnp.concatenate([block[:, :WIDTH], block[:, WIDTH:]], axis=0)
            xtok[w] = x
            center = x - jnp.mean(x, axis=1, keepdims=True)
            inverse = lax.rsqrt(jnp.mean(center * center, axis=1, keepdims=True) + EPS)
            normed = center * inverse
            xhat[w] = normed
            spread_inv[w] = inverse
            x_n = (normed * gain).astype(BF16)
            proj_t[w] = dot_nt(w_t[...], x_n).astype(BF16)
            kv = dot_nn(x_n, w_in[:, WIDTH:]).astype(BF16)
            for h in range(HEADS):
                k_nat[w, h] = kv[:, h * HEAD_DIM : (h + 1) * HEAD_DIM]
                v_nat[w, h] = kv[:, WIDTH + h * HEAD_DIM : WIDTH + (h + 1) * HEAD_DIM]
        wait_halo(1, slot)
        unpack_in(1, slot)
        for w in range(WINDOWS):
            block = xw[w * CELLS : (w + 1) * CELLS, :]
            c = jnp.concatenate([block[:, :WIDTH], block[:, WIDTH:]], axis=0)
            ctok[w] = c
            gmix_t[w] = dot_nt(wo_in[...], c.astype(BF16)).astype(BF16)

        first_row = jnp.where(slot == 0, lat, up) * WIN_LAT + RIM_R
        key_row = lax.rem(first_row + key_band, total_rows)
        query_row = lax.rem(first_row + query_band, total_rows)
        real = jnp.zeros((TOKENS, TOKENS), jnp.int32)
        for a in range(WIN_LAT):
            real = jnp.where(key_band == a, pad_ref[lax.rem(first_row + a, total_rows)], real)
        allowed = (jnp.abs(query_row - key_row) < WIN_LAT) & (real == 1)

        def wait_bias(s, inner):
            bias_arrival(slot, s).wait_recv()
            return inner

        lax.fori_loop(1 - slot, lon_size, wait_bias, 0)
        for p in range(PAIRS):
            owner, r = p // pairs_here, p % pairs_here
            zq, zt = p // ZONE, p % ZONE
            spread[zt * 8 : zt * 8 + 8, zq * SLOT : (zq + 1) * SLOT] = bias_recv[
                slot, owner, :, r * SLOT : (r + 1) * SLOT
            ]
        for b in range(WIN_LON):
            table = spread[...]
            if b:
                table = pltpu.roll(table, b, 1)
            high = table.astype(BF16)
            rest = table - high.astype(F32)
            middle = rest.astype(BF16)
            low = (rest - middle.astype(F32)).astype(BF16)
            pick = selector[...]
            wide = dot_nn(high, pick) + (dot_nn(middle, pick) + dot_nn(low, pick))
            for zt in range(ZONE):
                row = (zt * WIN_LON + b) * 8
                bias_flat[0, row : row + 8, :] = wide[zt * 8 : zt * 8 + 8, 0:128]
                bias_flat[1, row : row + 8, 0 : TOKENS - 128] = wide[
                    zt * 8 : zt * 8 + 8, 128:TOKENS
                ]
        for h in range(HEADS):
            left = bias_flat[0, pl.ds(h, TOKENS, stride=8), :]
            right = bias_flat[1, pl.ds(h, TOKENS, stride=8), :]
            whole = jnp.concatenate([left, right[:, 0 : TOKENS - 128]], axis=1)
            bias_full[h] = jnp.where(allowed, whole, MASKED)

        for h in range(HEADS):
            at_q = pl.ds(h * HEAD_DIM, HEAD_DIM)
            at_k = pl.ds(WIDTH + h * HEAD_DIM, HEAD_DIM)
            at_v = pl.ds(2 * WIDTH + h * HEAD_DIM, HEAD_DIM)
            bias = bias_full[h]
            summed = None
            for w in range(WINDOWS):
                q_t = proj_t[w, at_q, :]
                g_t = gmix_t[w, at_q, :]
                scores = dot_nn(k_nat[w, h], q_t) * SCALE + bias
                raised = jnp.exp(scores - jnp.max(scores, axis=0, keepdims=True))
                weights = raised * (1.0 / jnp.sum(raised, axis=0, keepdims=True))
                weights_low = weights.astype(BF16)
                mixed_t[w, at_q, :] = dot_nn(proj_t[w, at_v, :], weights_low).astype(BF16)
                grad_w = dot_nn(v_nat[w, h], g_t)
                grad_s = weights * (grad_w - jnp.sum(weights * grad_w, axis=0, keepdims=True))
                grad_low = grad_s.astype(BF16)
                gproj_t[w, at_q, :] = (dot_nn(proj_t[w, at_k, :], grad_low) * SCALE).astype(BF16)
                gproj_t[w, at_k, :] = (dot_nt(q_t, grad_low) * SCALE).astype(BF16)
                gproj_t[w, at_v, :] = dot_nt(g_t, weights_low).astype(BF16)
                summed = grad_s if summed is None else summed + grad_s
            gflat[0, pl.ds(h, TOKENS, stride=8), :] = summed[:, 0:128]
            gflat[1, pl.ds(h, TOKENS, stride=8), 0 : TOKENS - 128] = summed[:, 128:TOKENS]

        give_back(
            0, slot, [xtok[w] + dot_tn(mixed_t[w], wo_in[...]) for w in range(WINDOWS)]
        )
        grads = []
        for w in range(WINDOWS):
            scaled = dot_tn(gproj_t[w], w_t[...]) * gain
            normed = xhat[w]
            centered = (
                scaled
                - jnp.mean(scaled, axis=1, keepdims=True)
                - normed * jnp.mean(scaled * normed, axis=1, keepdims=True)
            )
            grads.append(ctok[w] + spread_inv[w] * centered)
        give_back(1, slot, grads)

        total = jnp.zeros((ZONE * 8, BAND), F32)
        for b in range(WIN_LON):
            picked_rows = []
            for zt in range(ZONE):
                row = (zt * WIN_LON + b) * 8
                picked_rows.append(
                    jnp.concatenate(
                        [
                            gflat[0, row : row + 8, :],
                            gflat[1, row : row + 8, 0 : TOKENS - 128],
                        ],
                        axis=1,
                    )
                )
            part = jnp.concatenate(picked_rows, axis=0)
            high = part.astype(BF16)
            low = (part - high.astype(F32)).astype(BF16)
            placed = dot_nt(high, selector[...]) + dot_nt(low, selector[...])
            if b:
                placed = pltpu.roll(placed, BAND - b, 1)
            total = total + placed
        spread[...] = total
        for p in range(PAIRS):
            owner, r = p // pairs_here, p % pairs_here
            zq, zt = p // ZONE, p % ZONE
            table_msg[slot, owner, :, r * SLOT : (r + 1) * SLOT] = spread[
                zt * 8 : zt * 8 + 8, zq * SLOT : (zq + 1) * SLOT
            ]

        def send_table(s, inner):
            table_copy(slot, s).start()
            return inner

        lax.fori_loop(1 - slot, lon_size, send_table, 0)

        @pl.when(slot == 0)
        def _():
            table_recv[lon] = table_msg[0, lon]

        return carry

    rows_here = 1 + one_if_first - one_if_last
    lax.fori_loop(0, rows_here, window_row, 0)

    def take_back(kind, dst):
        def arrived_big(half):
            remote(
                res_big.at[kind, 0, half],
                back_big.at[kind, half],
                back_send.at[kind, 0, 0],
                back_recv.at[kind, half],
                (dn, lon),
            ).wait_recv()

        @pl.when(is_last)
        def _():
            arrived_big(0)

        @pl.when(jnp.logical_not(is_first))
        def _():
            arrived_big(1)

        for half in range(2):
            remote(
                res_small.at[kind, 0, half],
                back_small.at[kind, half],
                back_send.at[kind, 0, 1],
                back_recv.at[kind, 2 + half],
                (dn, rt),
            ).wait_recv()
        for half, first in ((0, RIM_R), (1, 0)):
            base, side = half * 88, 64 + half * 88
            tmp[base : base + BIG, :] = back_big[kind, half].astype(F32)
            tmp[side : side + SMALL, :] = back_small[kind, half].astype(F32)
            for r in range(RIM_R):
                row = (first + r) * COLS
                raw[row + 6 : row + 18, :] = tmp[base + r * 12 : base + r * 12 + 12, :]
                raw[row + 18 : row + 24, :] = tmp[base + 36 + r * 6 : base + 42 + r * 6, :]
                raw[row : row + 6, :] = tmp[side + r * 6 : side + 6 + r * 6, :]
        for r in range(WIN_LAT):
            dst[r] = raw[r * COLS : (r + 1) * COLS, :].astype(BF16)

    take_back(0, out_ref)
    take_back(1, grads_ref)

    def wait_table(s, carry):
        table_arrival(s).wait_recv()
        return carry

    lax.fori_loop(1 - one_if_last, lon_size, wait_table, 0)
    added = table_recv[0]
    for j in range(1, lon_size):
        added = added + table_recv[j]
    for r in range(pairs_here):
        piece = added[:, r * SLOT : r * SLOT + OFFSETS]
        for h in range(HEADS):
            table_ref[h, r] = piece[h : h + 1, :]

    for kind in range(2):

        @pl.when(is_last)
        def _():
            big_last(kind).wait_send()

        @pl.when(jnp.logical_not(is_first))
        def _():
            big_up(kind).wait_send()

        small_low(kind).wait_send()
        small_top(kind).wait_send()

    def drain_bias(s, carry):
        bias_copy(s).wait_send()
        return carry

    lax.fori_loop(1 - one_if_last, lon_size, drain_bias, 0)

    def drain_row(slot, carry):
        for kind in range(2):
            back_copy_big(kind, slot).wait_send()
            for half in range(2):
                back_copy_small(kind, slot, half).wait_send()

        def drain_table(s, inner):
            table_copy(slot, s).wait_send()
            return inner

        lax.fori_loop(1 - slot, lon_size, drain_table, 0)
        return carry

    lax.fori_loop(0, rows_here, drain_row, 0)


def place_out(*refs):
    sources, targets, sem = refs[:3], refs[3:6], refs[6]
    copies = [
        pltpu.make_async_copy(src, dst, sem.at[n])
        for n, (src, dst) in enumerate(zip(sources, targets))
    ]
    for copy in copies:
        copy.start()
    for copy in copies:
        copy.wait()


def solution(mesh):
    lat_size, lon_size = mesh.shape["lat"], mesh.shape["lon"]
    pairs_here = PAIRS // lon_size
    lanes = -(-pairs_here * SLOT // 128) * 128

    def per_device(fields, norm_gain, project_in, project_out, bias_table, pad_rows, cotangent):
        hbm_spec = pl.BlockSpec(memory_space=pltpu.HBM)
        vmem_spec = pl.BlockSpec(memory_space=pltpu.VMEM)
        out_fields, field_grads, table_grads = pl.pallas_call(
            functools.partial(kernel, lat_size, lon_size, pairs_here),
            out_shape=(
                jax.ShapeDtypeStruct(fields.shape, BF16),
                jax.ShapeDtypeStruct(fields.shape, BF16),
                jax.ShapeDtypeStruct((HEADS, pairs_here, 1, OFFSETS), F32),
            ),
            in_specs=[hbm_spec] * 7,
            out_specs=(vmem_spec, vmem_spec, vmem_spec),
            scratch_shapes=[
                pltpu.VMEM(fields.shape, BF16),
                pltpu.VMEM(fields.shape, BF16),
                pltpu.VMEM(project_in.shape, BF16),
                pltpu.VMEM(project_out.shape, BF16),
                pltpu.VMEM((HEADS, pairs_here, 1, OFFSETS), F32),
                pltpu.VMEM((1, WIDTH), F32),
                pltpu.SMEM(pad_rows.shape, jnp.int32),
                pltpu.VMEM((WIN_LAT * COLS, FEATS), F32),
                pltpu.VMEM((WINDOWS * CELLS, FEATS), F32),
                pltpu.VMEM((176, FEATS), F32),
                pltpu.VMEM((2, 2, BIG, FEATS), BF16),
                pltpu.VMEM((2, 2, SMALL, FEATS), BF16),
                pltpu.VMEM((2, 2, 2, BIG, FEATS), BF16),
                pltpu.VMEM((2, 2, 2, SMALL, FEATS), BF16),
                pltpu.VMEM((2, 2, 2, BIG, FEATS), BF16),
                pltpu.VMEM((2, 2, 2, SMALL, FEATS), BF16),
                pltpu.VMEM((2, 2, BIG, FEATS), BF16),
                pltpu.VMEM((2, 2, SMALL, FEATS), BF16),
                pltpu.VMEM((8, lanes), F32),
                pltpu.VMEM((2, lon_size, 8, lanes), F32),
                pltpu.VMEM((ZONE * 8, BAND), F32),
                pltpu.VMEM((2, TOKENS * 8, 128), F32),
                pltpu.VMEM((HEADS, TOKENS, TOKENS), F32),
                pltpu.VMEM((3 * WIDTH, WIDTH), BF16),
                pltpu.VMEM((WINDOWS, TOKENS, WIDTH), F32),
                pltpu.VMEM((WINDOWS, TOKENS, WIDTH), F32),
                pltpu.VMEM((WINDOWS, TOKENS, WIDTH), F32),
                pltpu.VMEM((WINDOWS, TOKENS, 1), F32),
                pltpu.VMEM((WINDOWS, 3 * WIDTH, TOKENS), BF16),
                pltpu.VMEM((WINDOWS, HEADS, TOKENS, HEAD_DIM), BF16),
                pltpu.VMEM((WINDOWS, HEADS, TOKENS, HEAD_DIM), BF16),
                pltpu.VMEM((WINDOWS, WIDTH, TOKENS), BF16),
                pltpu.VMEM((WINDOWS, WIDTH, TOKENS), BF16),
                pltpu.VMEM((WINDOWS, 3 * WIDTH, TOKENS), BF16),
                pltpu.VMEM((2, TOKENS * 8, 128), F32),
                pltpu.VMEM((WINDOWS * CELLS, FEATS), F32),
                pltpu.VMEM((2, lon_size, 8, lanes), F32),
                pltpu.VMEM((lon_size, 8, lanes), F32),
                pltpu.VMEM((BAND, TOKENS), BF16),
                pltpu.SemaphoreType.DMA((7,)),
                pltpu.SemaphoreType.DMA((2, 4)),
                pltpu.SemaphoreType.DMA((2, 2, 3)),
                pltpu.SemaphoreType.DMA((2, 2, 3)),
                pltpu.SemaphoreType.DMA((2, 4)),
                pltpu.SemaphoreType.DMA((lon_size,)),
                pltpu.SemaphoreType.DMA((2, lon_size)),
                pltpu.SemaphoreType.DMA((2, lon_size)),
                pltpu.SemaphoreType.DMA((lon_size,)),
                pltpu.SemaphoreType.REGULAR,
            ],
            compiler_params=pltpu.CompilerParams(
                collective_id=0, has_side_effects=True, vmem_limit_bytes=48 << 20
            ),
        )(
            *(
                pltpu.with_memory_space_constraint(x, pltpu.HBM)
                for x in (
                    fields,
                    norm_gain.reshape(1, WIDTH),
                    project_in,
                    project_out,
                    bias_table.reshape(HEADS, pairs_here, 1, OFFSETS),
                    pad_rows,
                    cotangent,
                )
            )
        )
        parts = (out_fields, field_grads, table_grads)
        any_spec = pl.BlockSpec(memory_space=pl.ANY)
        out_fields, field_grads, table_grads = pl.pallas_call(
            place_out,
            out_shape=tuple(jax.ShapeDtypeStruct(x.shape, x.dtype) for x in parts),
            in_specs=[any_spec] * 3,
            out_specs=(hbm_spec,) * 3,
            scratch_shapes=[pltpu.SemaphoreType.DMA((3,))],
            compiler_params=pltpu.CompilerParams(vmem_limit_bytes=1 << 20),
        )(*parts)
        return out_fields, field_grads, table_grads.reshape(bias_table.shape)

    in_specs = (
        P("lat", "lon", None),
        P(),
        P(),
        P(),
        P("lat", None, "lon", None),
        P(),
        P("lat", "lon", None),
    )
    out_specs = (P("lat", "lon", None), P("lat", "lon", None), P("lat", None, "lon", None))
    return jax.shard_map(
        per_device, mesh=mesh, in_specs=in_specs, out_specs=out_specs, check_vma=False
    )
```

```python
import functools

import jax
import jax.numpy as jnp
from jax import lax
from jax.experimental import pallas as pl
from jax.experimental.pallas import tpu as pltpu
from jax.sharding import PartitionSpec as P

WIDTH = 192
HEADS = 6
HEAD_DIM = 32
LEVELS = 2
WIN_LAT = 6
WIN_LON = 12
ZONE = LEVELS * WIN_LAT
CELLS = WIN_LAT * WIN_LON
TOKENS = LEVELS * CELLS
OFFSETS = 23
SLOT = 24
PAIRS = ZONE * ZONE
RIM_R = WIN_LAT // 2
RIM_C = WIN_LON // 2
WINDOWS = 2
COLS = WINDOWS * WIN_LON
FEATS = LEVELS * WIDTH
BAND = 384
BIG = 56
SMALL = 24
SCALE = HEAD_DIM**-0.5
EPS = 1e-05
MASKED = -1e30
MESH = pl.DeviceIdType.MESH
F32 = jnp.float32
BF16 = jnp.bfloat16


def dot_nn(a, b):
    return lax.dot_general(a, b, (((1,), (0,)), ((), ())), preferred_element_type=F32)


def dot_nt(a, b):
    return lax.dot_general(a, b, (((1,), (1,)), ((), ())), preferred_element_type=F32)


def dot_tn(a, b):
    return lax.dot_general(a, b, (((0,), (0,)), ((), ())), preferred_element_type=F32)


def kernel(
    lat_size,
    lon_size,
    pairs_here,
    fields_hbm,
    gain_hbm,
    win_hbm,
    wout_hbm,
    bias_hbm,
    pad_hbm,
    cot_hbm,
    out_ref,
    grads_ref,
    table_ref,
    f_in,
    c_in,
    w_in,
    wo_in,
    bias_in,
    gain_ref,
    pad_ref,
    raw,
    xw,
    tmp,
    send_big,
    send_small,
    in_big,
    in_small,
    res_big,
    res_small,
    back_big,
    back_small,
    bias_msg,
    bias_recv,
    spread,
    bias_flat,
    bias_full,
    w_t,
    xtok,
    ctok,
    xhat,
    spread_inv,
    proj_t,
    k_nat,
    v_nat,
    gmix_t,
    mixed_t,
    gproj_t,
    gflat,
    cells,
    table_msg,
    table_recv,
    spreader,
    gatherer,
    score_buf,
    gw_buf,
    p_low,
    d_low,
    load_sem,
    halo_send,
    halo_recv,
    back_send,
    back_recv,
    bias_send,
    bias_rsem,
    table_send,
    table_rsem,
    ready_sem,
):
    lat = lax.axis_index("lat")
    lon = lax.axis_index("lon")
    up = lax.rem(lat + lat_size - 1, lat_size)
    dn = lax.rem(lat + 1, lat_size)
    lf = lax.rem(lon + lon_size - 1, lon_size)
    rt = lax.rem(lon + 1, lon_size)
    group = lat_size // 2
    place = lax.rem(lat, group)
    is_first = place == 0
    is_last = place == group - 1
    before_last = place == group - 2
    one_if_last = jnp.where(is_last, 1, 0)
    one_if_first = jnp.where(is_first, 1, 0)
    below = jnp.where(is_last, dn, lat)
    above = jnp.where(is_first, lat, up)

    barrier = pltpu.get_barrier_semaphore()

    def signal(dev):
        pl.semaphore_signal(barrier, inc=1, device_id=dev, device_id_type=MESH)

    def greet_seam(s, carry):
        signal((up, lax.rem(lon + s, lon_size)))
        return carry

    def greet(s, carry):
        signal((lat, lax.rem(lon + s, lon_size)))
        return carry

    @pl.when(is_first)
    def _():
        lax.fori_loop(0, lon_size, greet_seam, 0)

    @pl.when(jnp.logical_not(is_first))
    def _():
        signal((up, lon))
        signal((up, lf))

    @pl.when(jnp.logical_not(is_last))
    def _():
        signal((dn, lon))
        lax.fori_loop(1, lon_size, greet, 0)

    @pl.when(jnp.logical_not(is_last | before_last))
    def _():
        signal((dn, rt))

    loads = [
        pltpu.make_async_copy(src, dst, load_sem.at[n])
        for n, (src, dst) in enumerate(
            (
                (bias_hbm, bias_in),
                (fields_hbm, f_in),
                (cot_hbm, c_in),
                (win_hbm, w_in),
                (wout_hbm, wo_in),
                (gain_hbm, gain_ref),
                (pad_hbm, pad_ref),
            )
        )
    ]
    for load in loads:
        load.start()

    def remote(src, dst, send, recv, dev):
        return pltpu.make_async_remote_copy(
            src_ref=src,
            dst_ref=dst,
            send_sem=send,
            recv_sem=recv,
            device_id=dev,
            device_id_type=MESH,
        )

    def big_last(kind):
        return remote(
            send_big.at[kind, 0],
            in_big.at[kind, 1, 0],
            halo_send.at[kind, 0],
            halo_recv.at[kind, 1, 0],
            (dn, lon),
        )

    def big_up(kind):
        return remote(
            send_big.at[kind, 1],
            in_big.at[kind, 0, 1],
            halo_send.at[kind, 1],
            halo_recv.at[kind, 0, 0],
            (up, lon),
        )

    def small_low(kind):
        return remote(
            send_small.at[kind, 0],
            in_small.at[kind, one_if_last, 0],
            halo_send.at[kind, 2],
            halo_recv.at[kind, one_if_last, 1],
            (below, lf),
        )

    def small_top(kind):
        return remote(
            send_small.at[kind, 1],
            in_small.at[kind, one_if_first, 1],
            halo_send.at[kind, 3],
            halo_recv.at[kind, one_if_first, 2],
            (above, lf),
        )

    def wait_halo(kind, slot):
        remote(
            send_big.at[kind, 0],
            in_big.at[kind, slot, 1 - slot],
            halo_send.at[kind, 0],
            halo_recv.at[kind, slot, 0],
            (dn, lon),
        ).wait_recv()
        for half in range(2):
            remote(
                send_small.at[kind, half],
                in_small.at[kind, slot, half],
                halo_send.at[kind, 2],
                halo_recv.at[kind, slot, 1 + half],
                (dn, lon),
            ).wait_recv()

    def pack_in(src, kind):
        for r in range(WIN_LAT):
            raw[r * COLS : (r + 1) * COLS, :] = src[r].astype(F32)
        for half, first in ((0, RIM_R), (1, 0)):
            base, side = half * 88, 64 + half * 88
            for r in range(RIM_R):
                row = (first + r) * COLS
                tmp[base + r * 12 : base + r * 12 + 12, :] = raw[row + 6 : row + 18, :]
                tmp[base + 36 + r * 6 : base + 42 + r * 6, :] = raw[row + 18 : row + 24, :]
                tmp[side + r * 6 : side + 6 + r * 6, :] = raw[row : row + 6, :]
            piece = tmp[base : base + BIG, :].astype(BF16)
            send_big[kind, half] = piece
            in_big[kind, half, half] = piece
            send_small[kind, half] = tmp[side : side + SMALL, :].astype(BF16)

    def unpack_in(kind, slot):
        for half in range(2):
            base, side = half * 88, 64 + half * 88
            tmp[base : base + BIG, :] = in_big[kind, slot, half].astype(F32)
            tmp[side : side + SMALL, :] = in_small[kind, slot, half].astype(F32)
            xw[36 * half : 36 * half + 36, :] = tmp[base : base + 36, :]
            for r in range(RIM_R):
                row = CELLS + (RIM_R * half + r) * 12
                xw[row : row + 6, :] = tmp[base + 36 + r * 6 : base + 42 + r * 6, :]
                xw[row + 6 : row + 12, :] = tmp[side + r * 6 : side + 6 + r * 6, :]

    tmp[...] = jnp.zeros_like(tmp)
    bias_msg[...] = jnp.zeros_like(bias_msg)
    loads[0].wait()
    for r in range(pairs_here):
        for h in range(HEADS):
            bias_msg[h : h + 1, r * SLOT : r * SLOT + OFFSETS] = bias_in[h, r]
    bias_recv[0, lon] = bias_msg[...]
    loads[1].wait()
    pack_in(f_in, 0)

    pl.semaphore_wait(barrier, jnp.where(is_first | is_last, lon_size + 1, lon_size + 3))

    @pl.when(before_last)
    def _():
        pl.semaphore_signal(ready_sem, inc=1, device_id=(dn, rt), device_id_type=MESH)

    def bias_copy(s):
        return remote(
            bias_msg,
            bias_recv.at[one_if_last, lon],
            bias_send.at[s],
            bias_rsem.at[one_if_last, lon],
            (below, lax.rem(lon + s, lon_size)),
        )

    def bias_arrival(slot, s):
        source = lax.rem(lon + s, lon_size)
        return remote(
            bias_msg,
            bias_recv.at[slot, source],
            bias_send.at[s],
            bias_rsem.at[slot, source],
            (dn, lon),
        )

    def send_bias(s, carry):
        bias_copy(s).start()
        return carry

    def send_halo(kind):
        @pl.when(is_last)
        def _():
            big_last(kind).start()

        small_low(kind).start()

        @pl.when(jnp.logical_not(is_first))
        def _():
            big_up(kind).start()

        @pl.when(jnp.logical_not(is_last))
        def _():
            small_top(kind).start()

    lax.fori_loop(1 - one_if_last, lon_size, send_bias, 0)
    send_halo(0)
    loads[2].wait()
    pack_in(c_in, 1)
    send_halo(1)

    @pl.when(is_last)
    def _():
        pl.semaphore_wait(ready_sem, 1)
        for kind in range(2):
            small_top(kind).start()

    gflat[...] = jnp.zeros_like(gflat)
    table_msg[...] = jnp.zeros_like(table_msg)
    spread[...] = jnp.zeros_like(spread)

    def make_selectors(b, carry):
        lane = lax.broadcasted_iota(jnp.int32, (BAND, TOKENS), 0)
        query = lax.broadcasted_iota(jnp.int32, (BAND, TOKENS), 1)
        picked = (query // WIN_LON) * SLOT + query % WIN_LON + WIN_LON - 1 - b
        spreader[b] = (lane == picked).astype(F32).astype(BF16)
        lane = lax.broadcasted_iota(jnp.int32, (TOKENS, BAND), 1)
        query = lax.broadcasted_iota(jnp.int32, (TOKENS, BAND), 0)
        picked = (query // WIN_LON) * SLOT + query % WIN_LON + WIN_LON - 1 - b
        gatherer[b] = (lane == picked).astype(F32).astype(BF16)
        return carry

    lax.fori_loop(0, WIN_LON, make_selectors, 0)
    loads[3].wait()
    loads[4].wait()
    loads[5].wait()
    loads[6].wait()
    w_t[...] = w_in[...].astype(F32).T.astype(BF16)
    total_rows = lat_size * WIN_LAT
    key_band = (lax.broadcasted_iota(jnp.int32, (TOKENS, TOKENS), 0) // WIN_LON) % WIN_LAT
    query_band = (lax.broadcasted_iota(jnp.int32, (TOKENS, TOKENS), 1) // WIN_LON) % WIN_LAT

    def back_copy_big(kind, slot):
        return remote(
            res_big.at[kind, slot, 1 - slot],
            back_big.at[kind, 1 - slot],
            back_send.at[kind, slot, 0],
            back_recv.at[kind, 1 - slot],
            (jnp.where(slot == 0, dn, up), lon),
        )

    def back_copy_small(kind, slot, half):
        owner = lax.rem(lat + half - slot + lat_size, lat_size)
        return remote(
            res_small.at[kind, slot, half],
            back_small.at[kind, half],
            back_send.at[kind, slot, 1 + half],
            back_recv.at[kind, 2 + half],
            (owner, rt),
        )

    def give_back(kind, slot, tokens):
        for w in range(WINDOWS):
            cells[w * CELLS : (w + 1) * CELLS, 0:WIDTH] = tokens[w][0:CELLS]
            cells[w * CELLS : (w + 1) * CELLS, WIDTH:] = tokens[w][CELLS:]
        for half in range(2):
            base, side = half * 88, 64 + half * 88
            tmp[base : base + 36, :] = cells[36 * half : 36 * half + 36, :]
            for r in range(RIM_R):
                row = CELLS + (RIM_R * half + r) * 12
                tmp[base + 36 + r * 6 : base + 42 + r * 6, :] = cells[row : row + 6, :]
                tmp[side + r * 6 : side + 6 + r * 6, :] = cells[row + 6 : row + 12, :]
            res_big[kind, slot, half] = tmp[base : base + BIG, :].astype(BF16)
            res_small[kind, slot, half] = tmp[side : side + SMALL, :].astype(BF16)
        for half in range(2):
            back_copy_small(kind, slot, half).start()
        back_copy_big(kind, slot).start()
        back_big[kind, slot] = res_big[kind, slot, slot]

    def table_copy(slot, s):
        peer = lax.rem(lon + s, lon_size)
        return remote(
            table_msg.at[slot, peer],
            table_recv.at[lon],
            table_send.at[slot, s],
            table_rsem.at[lon],
            (jnp.where(slot == 0, lat, up), peer),
        )

    def table_arrival(s):
        source = lax.rem(lon + s, lon_size)
        return remote(
            table_msg.at[0, source],
            table_recv.at[source],
            table_send.at[0, s],
            table_rsem.at[source],
            (lat, source),
        )

    def window_row(slot, carry):
        gain = gain_ref[...]
        wait_halo(0, slot)
        unpack_in(0, slot)
        for w in range(WINDOWS):
            block = xw[w * CELLS : (w + 1) * CELLS, :]
            x = jnp.concatenate([block[:, :WIDTH], block[:, WIDTH:]], axis=0)
            xtok[w] = x
            center = x - jnp.mean(x, axis=1, keepdims=True)
            inverse = lax.rsqrt(jnp.mean(center * center, axis=1, keepdims=True) + EPS)
            normed = center * inverse
            xhat[w] = normed
            spread_inv[w] = inverse
            x_n = (normed * gain).astype(BF16)
            proj_t[w] = dot_nt(w_t[...], x_n).astype(BF16)
            kv = dot_nn(x_n, w_in[:, WIDTH:]).astype(BF16)
            for h in range(HEADS):
                k_nat[w, h] = kv[:, h * HEAD_DIM : (h + 1) * HEAD_DIM]
                v_nat[w, h] = kv[:, WIDTH + h * HEAD_DIM : WIDTH + (h + 1) * HEAD_DIM]
        wait_halo(1, slot)
        unpack_in(1, slot)
        for w in range(WINDOWS):
            block = xw[w * CELLS : (w + 1) * CELLS, :]
            c = jnp.concatenate([block[:, :WIDTH], block[:, WIDTH:]], axis=0)
            ctok[w] = c
            gmix_t[w] = dot_nt(wo_in[...], c.astype(BF16)).astype(BF16)

        first_row = jnp.where(slot == 0, lat, up) * WIN_LAT + RIM_R
        key_row = lax.rem(first_row + key_band, total_rows)
        query_row = lax.rem(first_row + query_band, total_rows)
        real = jnp.zeros((TOKENS, TOKENS), jnp.int32)
        for a in range(WIN_LAT):
            real = jnp.where(key_band == a, pad_ref[lax.rem(first_row + a, total_rows)], real)
        allowed = (jnp.abs(query_row - key_row) < WIN_LAT) & (real == 1)

        def wait_bias(s, inner):
            bias_arrival(slot, s).wait_recv()
            return inner

        lax.fori_loop(1 - slot, lon_size, wait_bias, 0)
        for p in range(PAIRS):
            owner, r = p // pairs_here, p % pairs_here
            zq, zt = p // ZONE, p % ZONE
            spread[zt * 8 : zt * 8 + 8, zq * SLOT : (zq + 1) * SLOT] = bias_recv[
                slot, owner, :, r * SLOT : (r + 1) * SLOT
            ]
        table = spread[...]
        high = table.astype(BF16)
        rest = table - high.astype(F32)
        middle = rest.astype(BF16)
        low = (rest - middle.astype(F32)).astype(BF16)
        rows = ZONE * 8
        stacked = jnp.concatenate([high, middle, low], axis=0)
        for b in range(WIN_LON):
            three = dot_nn(stacked, spreader[b])
            wide = three[0:rows] + (three[rows : 2 * rows] + three[2 * rows :])
            for zt in range(ZONE):
                row = (zt * WIN_LON + b) * 8
                bias_flat[0, row : row + 8, :] = wide[zt * 8 : zt * 8 + 8, 0:128]
                bias_flat[1, row : row + 8, 0 : TOKENS - 128] = wide[
                    zt * 8 : zt * 8 + 8, 128:TOKENS
                ]
        for h in range(HEADS):
            left = bias_flat[0, pl.ds(h, TOKENS, stride=8), :]
            right = bias_flat[1, pl.ds(h, TOKENS, stride=8), :]
            whole = jnp.concatenate([left, right[:, 0 : TOKENS - 128]], axis=1)
            bias_full[h] = jnp.where(allowed, whole, MASKED)

        def rows_of(part, h):
            return pl.ds(part * WIDTH + h * HEAD_DIM, HEAD_DIM)

        for h in range(HEADS):
            for w in range(WINDOWS):
                score_buf[w, h] = (
                    dot_nn(k_nat[w, h], proj_t[w, rows_of(0, h), :]) * SCALE + bias_full[h]
                )
                gw_buf[w, h] = dot_nn(v_nat[w, h], gmix_t[w, rows_of(0, h), :])
        for h in range(HEADS):
            summed = None
            for w in range(WINDOWS):
                scores = score_buf[w, h]
                raised = jnp.exp(scores - jnp.max(scores, axis=0, keepdims=True))
                weights = raised * (1.0 / jnp.sum(raised, axis=0, keepdims=True))
                p_low[w, h] = weights.astype(BF16)
                grad_w = gw_buf[w, h]
                grad_s = weights * (grad_w - jnp.sum(weights * grad_w, axis=0, keepdims=True))
                d_low[w, h] = grad_s.astype(BF16)
                summed = grad_s if summed is None else summed + grad_s
            gflat[0, pl.ds(h, TOKENS, stride=8), :] = summed[:, 0:128]
            gflat[1, pl.ds(h, TOKENS, stride=8), 0 : TOKENS - 128] = summed[:, 128:TOKENS]
        for h in range(HEADS):
            for w in range(WINDOWS):
                q_t = proj_t[w, rows_of(0, h), :]
                g_t = gmix_t[w, rows_of(0, h), :]
                weights_low = p_low[w, h]
                grad_low = d_low[w, h]
                mixed_t[w, rows_of(0, h), :] = dot_nn(
                    proj_t[w, rows_of(2, h), :], weights_low
                ).astype(BF16)
                gproj_t[w, rows_of(0, h), :] = (
                    dot_nn(proj_t[w, rows_of(1, h), :], grad_low) * SCALE
                ).astype(BF16)
                gproj_t[w, rows_of(1, h), :] = (dot_nt(q_t, grad_low) * SCALE).astype(BF16)
                gproj_t[w, rows_of(2, h), :] = dot_nt(g_t, weights_low).astype(BF16)

        give_back(
            0, slot, [xtok[w] + dot_tn(mixed_t[w], wo_in[...]) for w in range(WINDOWS)]
        )
        grads = []
        for w in range(WINDOWS):
            scaled = dot_tn(gproj_t[w], w_t[...]) * gain
            normed = xhat[w]
            centered = (
                scaled
                - jnp.mean(scaled, axis=1, keepdims=True)
                - normed * jnp.mean(scaled * normed, axis=1, keepdims=True)
            )
            grads.append(ctok[w] + spread_inv[w] * centered)
        give_back(1, slot, grads)

        total = jnp.zeros((ZONE * 8, BAND), F32)
        for b in range(WIN_LON):
            picked_rows = []
            for zt in range(ZONE):
                row = (zt * WIN_LON + b) * 8
                picked_rows.append(
                    jnp.concatenate(
                        [
                            gflat[0, row : row + 8, :],
                            gflat[1, row : row + 8, 0 : TOKENS - 128],
                        ],
                        axis=1,
                    )
                )
            part = jnp.concatenate(picked_rows, axis=0).astype(BF16)
            total = total + dot_nn(part, gatherer[b])
        spread[...] = total
        for p in range(PAIRS):
            owner, r = p // pairs_here, p % pairs_here
            zq, zt = p // ZONE, p % ZONE
            table_msg[slot, owner, :, r * SLOT : (r + 1) * SLOT] = spread[
                zt * 8 : zt * 8 + 8, zq * SLOT : (zq + 1) * SLOT
            ]

        def send_table(s, inner):
            table_copy(slot, s).start()
            return inner

        lax.fori_loop(1 - slot, lon_size, send_table, 0)

        @pl.when(slot == 0)
        def _():
            table_recv[lon] = table_msg[0, lon]

        return carry

    rows_here = 1 + one_if_first - one_if_last
    lax.fori_loop(0, rows_here, window_row, 0)

    def take_back(kind, dst):
        def arrived_big(half):
            remote(
                res_big.at[kind, 0, half],
                back_big.at[kind, half],
                back_send.at[kind, 0, 0],
                back_recv.at[kind, half],
                (dn, lon),
            ).wait_recv()

        @pl.when(is_last)
        def _():
            arrived_big(0)

        @pl.when(jnp.logical_not(is_first))
        def _():
            arrived_big(1)

        for half in range(2):
            remote(
                res_small.at[kind, 0, half],
                back_small.at[kind, half],
                back_send.at[kind, 0, 1],
                back_recv.at[kind, 2 + half],
                (dn, rt),
            ).wait_recv()
        for half, first in ((0, RIM_R), (1, 0)):
            base, side = half * 88, 64 + half * 88
            tmp[base : base + BIG, :] = back_big[kind, half].astype(F32)
            tmp[side : side + SMALL, :] = back_small[kind, half].astype(F32)
            for r in range(RIM_R):
                row = (first + r) * COLS
                raw[row + 6 : row + 18, :] = tmp[base + r * 12 : base + r * 12 + 12, :]
                raw[row + 18 : row + 24, :] = tmp[base + 36 + r * 6 : base + 42 + r * 6, :]
                raw[row : row + 6, :] = tmp[side + r * 6 : side + 6 + r * 6, :]
        for r in range(WIN_LAT):
            dst[r] = raw[r * COLS : (r + 1) * COLS, :].astype(BF16)

    take_back(0, out_ref)
    take_back(1, grads_ref)

    def wait_table(s, carry):
        table_arrival(s).wait_recv()
        return carry

    lax.fori_loop(1 - one_if_last, lon_size, wait_table, 0)
    added = table_recv[0]
    for j in range(1, lon_size):
        added = added + table_recv[j]
    for r in range(pairs_here):
        piece = added[:, r * SLOT : r * SLOT + OFFSETS]
        for h in range(HEADS):
            table_ref[h, r] = piece[h : h + 1, :]

    for kind in range(2):

        @pl.when(is_last)
        def _():
            big_last(kind).wait_send()

        @pl.when(jnp.logical_not(is_first))
        def _():
            big_up(kind).wait_send()

        small_low(kind).wait_send()
        small_top(kind).wait_send()

    def drain_bias(s, carry):
        bias_copy(s).wait_send()
        return carry

    lax.fori_loop(1 - one_if_last, lon_size, drain_bias, 0)

    def drain_row(slot, carry):
        for kind in range(2):
            back_copy_big(kind, slot).wait_send()
            for half in range(2):
                back_copy_small(kind, slot, half).wait_send()

        def drain_table(s, inner):
            table_copy(slot, s).wait_send()
            return inner

        lax.fori_loop(1 - slot, lon_size, drain_table, 0)
        return carry

    lax.fori_loop(0, rows_here, drain_row, 0)


def place_out(*refs):
    sources, targets, sem = refs[:3], refs[3:6], refs[6]
    copies = [
        pltpu.make_async_copy(src, dst, sem.at[n])
        for n, (src, dst) in enumerate(zip(sources, targets))
    ]
    for copy in copies:
        copy.start()
    for copy in copies:
        copy.wait()


def solution(mesh):
    lat_size, lon_size = mesh.shape["lat"], mesh.shape["lon"]
    pairs_here = PAIRS // lon_size
    lanes = -(-pairs_here * SLOT // 128) * 128

    def per_device(fields, norm_gain, project_in, project_out, bias_table, pad_rows, cotangent):
        hbm_spec = pl.BlockSpec(memory_space=pltpu.HBM)
        vmem_spec = pl.BlockSpec(memory_space=pltpu.VMEM)
        out_fields, field_grads, table_grads = pl.pallas_call(
            functools.partial(kernel, lat_size, lon_size, pairs_here),
            out_shape=(
                jax.ShapeDtypeStruct(fields.shape, BF16),
                jax.ShapeDtypeStruct(fields.shape, BF16),
                jax.ShapeDtypeStruct((HEADS, pairs_here, 1, OFFSETS), F32),
            ),
            in_specs=[hbm_spec] * 7,
            out_specs=(vmem_spec, vmem_spec, vmem_spec),
            scratch_shapes=[
                pltpu.VMEM(fields.shape, BF16),
                pltpu.VMEM(fields.shape, BF16),
                pltpu.VMEM(project_in.shape, BF16),
                pltpu.VMEM(project_out.shape, BF16),
                pltpu.VMEM((HEADS, pairs_here, 1, OFFSETS), F32),
                pltpu.VMEM((1, WIDTH), F32),
                pltpu.SMEM(pad_rows.shape, jnp.int32),
                pltpu.VMEM((WIN_LAT * COLS, FEATS), F32),
                pltpu.VMEM((WINDOWS * CELLS, FEATS), F32),
                pltpu.VMEM((176, FEATS), F32),
                pltpu.VMEM((2, 2, BIG, FEATS), BF16),
                pltpu.VMEM((2, 2, SMALL, FEATS), BF16),
                pltpu.VMEM((2, 2, 2, BIG, FEATS), BF16),
                pltpu.VMEM((2, 2, 2, SMALL, FEATS), BF16),
                pltpu.VMEM((2, 2, 2, BIG, FEATS), BF16),
                pltpu.VMEM((2, 2, 2, SMALL, FEATS), BF16),
                pltpu.VMEM((2, 2, BIG, FEATS), BF16),
                pltpu.VMEM((2, 2, SMALL, FEATS), BF16),
                pltpu.VMEM((8, lanes), F32),
                pltpu.VMEM((2, lon_size, 8, lanes), F32),
                pltpu.VMEM((ZONE * 8, BAND), F32),
                pltpu.VMEM((2, TOKENS * 8, 128), F32),
                pltpu.VMEM((HEADS, TOKENS, TOKENS), F32),
                pltpu.VMEM((3 * WIDTH, WIDTH), BF16),
                pltpu.VMEM((WINDOWS, TOKENS, WIDTH), F32),
                pltpu.VMEM((WINDOWS, TOKENS, WIDTH), F32),
                pltpu.VMEM((WINDOWS, TOKENS, WIDTH), F32),
                pltpu.VMEM((WINDOWS, TOKENS, 1), F32),
                pltpu.VMEM((WINDOWS, 3 * WIDTH, TOKENS), BF16),
                pltpu.VMEM((WINDOWS, HEADS, TOKENS, HEAD_DIM), BF16),
                pltpu.VMEM((WINDOWS, HEADS, TOKENS, HEAD_DIM), BF16),
                pltpu.VMEM((WINDOWS, WIDTH, TOKENS), BF16),
                pltpu.VMEM((WINDOWS, WIDTH, TOKENS), BF16),
                pltpu.VMEM((WINDOWS, 3 * WIDTH, TOKENS), BF16),
                pltpu.VMEM((2, TOKENS * 8, 128), F32),
                pltpu.VMEM((WINDOWS * CELLS, FEATS), F32),
                pltpu.VMEM((2, lon_size, 8, lanes), F32),
                pltpu.VMEM((lon_size, 8, lanes), F32),
                pltpu.VMEM((WIN_LON, BAND, TOKENS), BF16),
                pltpu.VMEM((WIN_LON, TOKENS, BAND), BF16),
                pltpu.VMEM((WINDOWS, HEADS, TOKENS, TOKENS), F32),
                pltpu.VMEM((WINDOWS, HEADS, TOKENS, TOKENS), F32),
                pltpu.VMEM((WINDOWS, HEADS, TOKENS, TOKENS), BF16),
                pltpu.VMEM((WINDOWS, HEADS, TOKENS, TOKENS), BF16),
                pltpu.SemaphoreType.DMA((7,)),
                pltpu.SemaphoreType.DMA((2, 4)),
                pltpu.SemaphoreType.DMA((2, 2, 3)),
                pltpu.SemaphoreType.DMA((2, 2, 3)),
                pltpu.SemaphoreType.DMA((2, 4)),
                pltpu.SemaphoreType.DMA((lon_size,)),
                pltpu.SemaphoreType.DMA((2, lon_size)),
                pltpu.SemaphoreType.DMA((2, lon_size)),
                pltpu.SemaphoreType.DMA((lon_size,)),
                pltpu.SemaphoreType.REGULAR,
            ],
            compiler_params=pltpu.CompilerParams(
                collective_id=0, has_side_effects=True, vmem_limit_bytes=48 << 20
            ),
        )(
            *(
                pltpu.with_memory_space_constraint(x, pltpu.HBM)
                for x in (
                    fields,
                    norm_gain.reshape(1, WIDTH),
                    project_in,
                    project_out,
                    bias_table.reshape(HEADS, pairs_here, 1, OFFSETS),
                    pad_rows,
                    cotangent,
                )
            )
        )
        parts = (out_fields, field_grads, table_grads)
        any_spec = pl.BlockSpec(memory_space=pl.ANY)
        out_fields, field_grads, table_grads = pl.pallas_call(
            place_out,
            out_shape=tuple(jax.ShapeDtypeStruct(x.shape, x.dtype) for x in parts),
            in_specs=[any_spec] * 3,
            out_specs=(hbm_spec,) * 3,
            scratch_shapes=[pltpu.SemaphoreType.DMA((3,))],
            compiler_params=pltpu.CompilerParams(vmem_limit_bytes=1 << 20),
        )(*parts)
        return out_fields, field_grads, table_grads.reshape(bias_table.shape)

    in_specs = (
        P("lat", "lon", None),
        P(),
        P(),
        P(),
        P("lat", None, "lon", None),
        P(),
        P("lat", "lon", None),
    )
    out_specs = (P("lat", "lon", None), P("lat", "lon", None), P("lat", None, "lon", None))
    return jax.shard_map(
        per_device, mesh=mesh, in_specs=in_specs, out_specs=out_specs, check_vma=False
    )
```

```python
import functools

import jax
import jax.numpy as jnp
from jax import lax
from jax.experimental import pallas as pl
from jax.experimental.pallas import tpu as pltpu
from jax.sharding import PartitionSpec as P

WIDTH = 192
HEADS = 6
HEAD_DIM = 32
LEVELS = 2
WIN_LAT = 6
WIN_LON = 12
ZONE = LEVELS * WIN_LAT
CELLS = WIN_LAT * WIN_LON
TOKENS = LEVELS * CELLS
OFFSETS = 23
SLOT = 24
PAIRS = ZONE * ZONE
RIM_R = WIN_LAT // 2
RIM_C = WIN_LON // 2
WINDOWS = 2
COLS = WINDOWS * WIN_LON
FEATS = LEVELS * WIDTH
BAND = 384
BIG = 56
SMALL = 24
RUN = 4
SCALE = HEAD_DIM**-0.5
EPS = 1e-05
MASKED = -1e30
MESH = pl.DeviceIdType.MESH
F32 = jnp.float32
BF16 = jnp.bfloat16


def dot_nn(a, b):
    return lax.dot_general(a, b, (((1,), (0,)), ((), ())), preferred_element_type=F32)


def dot_nt(a, b):
    return lax.dot_general(a, b, (((1,), (1,)), ((), ())), preferred_element_type=F32)


def dot_tn(a, b):
    return lax.dot_general(a, b, (((0,), (0,)), ((), ())), preferred_element_type=F32)


def kernel(
    lat_size,
    lon_size,
    pairs_here,
    fields_hbm,
    gain_hbm,
    win_hbm,
    wout_hbm,
    bias_hbm,
    pad_hbm,
    cot_hbm,
    out_ref,
    grads_ref,
    table_ref,
    f_in,
    c_in,
    w_in,
    wo_in,
    bias_in,
    gain_ref,
    pad_ref,
    raw,
    xw,
    tmp,
    send_big,
    send_small,
    in_big,
    in_small,
    res_big,
    res_small,
    back_big,
    back_small,
    bias_msg,
    bias_recv,
    spread,
    bias_flat,
    bias_full,
    w_t,
    xtok,
    ctok,
    xhat,
    spread_inv,
    proj_t,
    k_nat,
    v_nat,
    gmix_t,
    mixed_t,
    gproj_t,
    gflat,
    cells,
    table_msg,
    table_mid,
    table_out,
    table_recv,
    spreader,
    gatherer,
    score_buf,
    gw_buf,
    p_low,
    d_low,
    load_sem,
    halo_send,
    halo_recv,
    back_send,
    back_recv,
    bias_send,
    bias_rsem,
    pass_send,
    pass_recv,
    table_xsend,
    table_xrecv,
    table_send,
    table_rsem,
    ready_sem,
):
    lat = lax.axis_index("lat")
    lon = lax.axis_index("lon")
    up = lax.rem(lat + lat_size - 1, lat_size)
    dn = lax.rem(lat + 1, lat_size)
    lf = lax.rem(lon + lon_size - 1, lon_size)
    rt = lax.rem(lon + 1, lon_size)
    group = lat_size // 2
    place = lax.rem(lat, group)
    is_first = place == 0
    is_last = place == group - 1
    before_last = place == group - 2
    one_if_last = jnp.where(is_last, 1, 0)
    one_if_first = jnp.where(is_first, 1, 0)
    steps = lon_size // RUN
    column = lon // RUN
    inside = lax.rem(lon, RUN)
    at_start = inside == 0
    at_end = inside == RUN - 1
    below = jnp.where(is_last, dn, lat)
    above = jnp.where(is_first, lat, up)

    barrier = pltpu.get_barrier_semaphore()

    def signal(dev):
        pl.semaphore_signal(barrier, inc=1, device_id=dev, device_id_type=MESH)

    def greet_seam(s, carry):
        signal((up, lax.rem(lon + s, lon_size)))
        return carry

    def run_peer(s):
        return column * RUN + lax.rem(inside + s, RUN)

    def column_peer(s):
        return lax.rem(column + s, steps)

    @pl.when(is_first)
    def _():
        lax.fori_loop(0, lon_size, greet_seam, 0)

    @pl.when(jnp.logical_not(is_first))
    def _():
        signal((up, lon))
        signal((up, lf))

    @pl.when(jnp.logical_not(is_last))
    def _():
        signal((dn, lon))
        for s in range(1, RUN):
            signal((lat, run_peer(s)))
        for s in range(1, steps):
            signal((lat, column_peer(s) * RUN + inside))

    @pl.when(jnp.logical_not(is_last) & at_start)
    def _():
        signal((lat, lf))

    @pl.when(jnp.logical_not(is_last) & at_end)
    def _():
        signal((lat, rt))

    @pl.when(jnp.logical_not(is_last | before_last))
    def _():
        signal((dn, rt))

    loads = [
        pltpu.make_async_copy(src, dst, load_sem.at[n])
        for n, (src, dst) in enumerate(
            (
                (bias_hbm, bias_in),
                (fields_hbm, f_in),
                (cot_hbm, c_in),
                (win_hbm, w_in),
                (wout_hbm, wo_in),
                (gain_hbm, gain_ref),
                (pad_hbm, pad_ref),
            )
        )
    ]
    for load in loads:
        load.start()

    def remote(src, dst, send, recv, dev):
        return pltpu.make_async_remote_copy(
            src_ref=src,
            dst_ref=dst,
            send_sem=send,
            recv_sem=recv,
            device_id=dev,
            device_id_type=MESH,
        )

    def big_last(kind):
        return remote(
            send_big.at[kind, 0],
            in_big.at[kind, 1, 0],
            halo_send.at[kind, 0],
            halo_recv.at[kind, 1, 0],
            (dn, lon),
        )

    def big_up(kind):
        return remote(
            send_big.at[kind, 1],
            in_big.at[kind, 0, 1],
            halo_send.at[kind, 1],
            halo_recv.at[kind, 0, 0],
            (up, lon),
        )

    def small_low(kind):
        return remote(
            send_small.at[kind, 0],
            in_small.at[kind, one_if_last, 0],
            halo_send.at[kind, 2],
            halo_recv.at[kind, one_if_last, 1],
            (below, lf),
        )

    def small_top(kind):
        return remote(
            send_small.at[kind, 1],
            in_small.at[kind, one_if_first, 1],
            halo_send.at[kind, 3],
            halo_recv.at[kind, one_if_first, 2],
            (above, lf),
        )

    def wait_halo(kind, slot):
        remote(
            send_big.at[kind, 0],
            in_big.at[kind, slot, 1 - slot],
            halo_send.at[kind, 0],
            halo_recv.at[kind, slot, 0],
            (dn, lon),
        ).wait_recv()
        for half in range(2):
            remote(
                send_small.at[kind, half],
                in_small.at[kind, slot, half],
                halo_send.at[kind, 2],
                halo_recv.at[kind, slot, 1 + half],
                (dn, lon),
            ).wait_recv()

    def pack_in(src, kind):
        for r in range(WIN_LAT):
            raw[r * COLS : (r + 1) * COLS, :] = src[r].astype(F32)
        for half, first in ((0, RIM_R), (1, 0)):
            base, side = half * 88, 64 + half * 88
            for r in range(RIM_R):
                row = (first + r) * COLS
                tmp[base + r * 12 : base + r * 12 + 12, :] = raw[row + 6 : row + 18, :]
                tmp[base + 36 + r * 6 : base + 42 + r * 6, :] = raw[row + 18 : row + 24, :]
                tmp[side + r * 6 : side + 6 + r * 6, :] = raw[row : row + 6, :]
            piece = tmp[base : base + BIG, :].astype(BF16)
            send_big[kind, half] = piece
            in_big[kind, half, half] = piece
            send_small[kind, half] = tmp[side : side + SMALL, :].astype(BF16)

    def unpack_in(kind, slot):
        for half in range(2):
            base, side = half * 88, 64 + half * 88
            tmp[base : base + BIG, :] = in_big[kind, slot, half].astype(F32)
            tmp[side : side + SMALL, :] = in_small[kind, slot, half].astype(F32)
            xw[36 * half : 36 * half + 36, :] = tmp[base : base + 36, :]
            for r in range(RIM_R):
                row = CELLS + (RIM_R * half + r) * 12
                xw[row : row + 6, :] = tmp[base + 36 + r * 6 : base + 42 + r * 6, :]
                xw[row + 6 : row + 12, :] = tmp[side + r * 6 : side + 6 + r * 6, :]

    tmp[...] = jnp.zeros_like(tmp)
    bias_msg[...] = jnp.zeros_like(bias_msg)
    loads[0].wait()
    for r in range(pairs_here):
        for h in range(HEADS):
            bias_msg[h : h + 1, r * SLOT : r * SLOT + OFFSETS] = bias_in[h, r]
    bias_recv[0, lon] = bias_msg[...]
    loads[1].wait()
    pack_in(f_in, 0)

    around = RUN + steps - 2 + jnp.where(at_start | at_end, 1, 0)
    greetings = jnp.where(is_last, lon_size + 1, around + jnp.where(is_first, 2, 4))
    pl.semaphore_wait(barrier, greetings)

    @pl.when(before_last)
    def _():
        pl.semaphore_signal(ready_sem, inc=1, device_id=(dn, rt), device_id_type=MESH)

    def bias_copy(s):
        return remote(
            bias_msg,
            bias_recv.at[one_if_last, lon],
            bias_send.at[s],
            bias_rsem.at[one_if_last, lon],
            (below, run_peer(s)),
        )

    def bias_arrival(slot, s):
        source = run_peer(s)
        return remote(
            bias_msg,
            bias_recv.at[slot, source],
            bias_send.at[s],
            bias_rsem.at[slot, source],
            (dn, lon),
        )

    def bias_pass(slot, s):
        mine = bias_recv.at[slot, pl.ds(column * RUN, RUN)]
        return remote(
            mine,
            mine,
            pass_send.at[slot, s],
            pass_recv.at[slot, column],
            (lat, column_peer(s) * RUN + inside),
        )

    def bias_passed(slot, s):
        source = column_peer(s)
        theirs = bias_recv.at[slot, pl.ds(source * RUN, RUN)]
        return remote(
            theirs, theirs, pass_send.at[slot, s], pass_recv.at[slot, source], (dn, lon)
        )

    def send_bias(s, carry):
        bias_copy(s).start()
        return carry

    def send_halo(kind):
        @pl.when(is_last)
        def _():
            big_last(kind).start()

        small_low(kind).start()

        @pl.when(jnp.logical_not(is_first))
        def _():
            big_up(kind).start()

        @pl.when(jnp.logical_not(is_last))
        def _():
            small_top(kind).start()

    lax.fori_loop(1 - one_if_last, RUN, send_bias, 0)
    send_halo(0)
    loads[2].wait()
    pack_in(c_in, 1)
    send_halo(1)

    @pl.when(is_last)
    def _():
        pl.semaphore_wait(ready_sem, 1)
        for kind in range(2):
            small_top(kind).start()

    gflat[...] = jnp.zeros_like(gflat)
    table_msg[...] = jnp.zeros_like(table_msg)
    spread[...] = jnp.zeros_like(spread)

    def make_selectors(b, carry):
        lane = lax.broadcasted_iota(jnp.int32, (BAND, TOKENS), 0)
        query = lax.broadcasted_iota(jnp.int32, (BAND, TOKENS), 1)
        picked = (query // WIN_LON) * SLOT + query % WIN_LON + WIN_LON - 1 - b
        spreader[b] = (lane == picked).astype(F32).astype(BF16)
        lane = lax.broadcasted_iota(jnp.int32, (TOKENS, BAND), 1)
        query = lax.broadcasted_iota(jnp.int32, (TOKENS, BAND), 0)
        picked = (query // WIN_LON) * SLOT + query % WIN_LON + WIN_LON - 1 - b
        gatherer[b] = (lane == picked).astype(F32).astype(BF16)
        return carry

    lax.fori_loop(0, WIN_LON, make_selectors, 0)
    loads[3].wait()
    loads[4].wait()
    loads[5].wait()
    loads[6].wait()
    w_t[...] = w_in[...].astype(F32).T.astype(BF16)
    total_rows = lat_size * WIN_LAT
    key_band = (lax.broadcasted_iota(jnp.int32, (TOKENS, TOKENS), 0) // WIN_LON) % WIN_LAT
    query_band = (lax.broadcasted_iota(jnp.int32, (TOKENS, TOKENS), 1) // WIN_LON) % WIN_LAT

    def back_copy_big(kind, slot):
        return remote(
            res_big.at[kind, slot, 1 - slot],
            back_big.at[kind, 1 - slot],
            back_send.at[kind, slot, 0],
            back_recv.at[kind, 1 - slot],
            (jnp.where(slot == 0, dn, up), lon),
        )

    def back_copy_small(kind, slot, half):
        owner = lax.rem(lat + half - slot + lat_size, lat_size)
        return remote(
            res_small.at[kind, slot, half],
            back_small.at[kind, half],
            back_send.at[kind, slot, 1 + half],
            back_recv.at[kind, 2 + half],
            (owner, rt),
        )

    def give_back(kind, slot, tokens):
        for w in range(WINDOWS):
            cells[w * CELLS : (w + 1) * CELLS, 0:WIDTH] = tokens[w][0:CELLS]
            cells[w * CELLS : (w + 1) * CELLS, WIDTH:] = tokens[w][CELLS:]
        for half in range(2):
            base, side = half * 88, 64 + half * 88
            tmp[base : base + 36, :] = cells[36 * half : 36 * half + 36, :]
            for r in range(RIM_R):
                row = CELLS + (RIM_R * half + r) * 12
                tmp[base + 36 + r * 6 : base + 42 + r * 6, :] = cells[row : row + 6, :]
                tmp[side + r * 6 : side + 6 + r * 6, :] = cells[row + 6 : row + 12, :]
            res_big[kind, slot, half] = tmp[base : base + BIG, :].astype(BF16)
            res_small[kind, slot, half] = tmp[side : side + SMALL, :].astype(BF16)
        for half in range(2):
            back_copy_small(kind, slot, half).start()
        back_copy_big(kind, slot).start()
        back_big[kind, slot] = res_big[kind, slot, slot]

    def table_pass(slot, s):
        target = column_peer(s)
        return remote(
            table_msg.at[slot, pl.ds(target * RUN, RUN)],
            table_mid.at[slot, column],
            table_xsend.at[slot, s],
            table_xrecv.at[slot, column],
            (lat, target * RUN + inside),
        )

    def table_passed(slot, s):
        source = column_peer(s)
        return remote(
            table_msg.at[slot, pl.ds(source * RUN, RUN)],
            table_mid.at[slot, source],
            table_xsend.at[slot, s],
            table_xrecv.at[slot, source],
            (lat, lon),
        )

    def table_copy(slot, s):
        peer = lax.rem(inside + s, RUN)
        return remote(
            table_out.at[slot, peer],
            table_recv.at[inside],
            table_send.at[slot, s],
            table_rsem.at[inside],
            (jnp.where(slot == 0, lat, up), run_peer(s)),
        )

    def table_arrival(s):
        source = lax.rem(inside + s, RUN)
        return remote(
            table_out.at[0, source],
            table_recv.at[source],
            table_send.at[0, s],
            table_rsem.at[source],
            (lat, run_peer(s)),
        )

    def window_row(slot, carry):
        def wait_bias(s, inner):
            bias_arrival(slot, s).wait_recv()
            return inner

        lax.fori_loop(1 - slot, RUN, wait_bias, 0)
        for s in range(1, steps):
            bias_pass(slot, s).start()
        gain = gain_ref[...]
        wait_halo(0, slot)
        unpack_in(0, slot)
        for w in range(WINDOWS):
            block = xw[w * CELLS : (w + 1) * CELLS, :]
            x = jnp.concatenate([block[:, :WIDTH], block[:, WIDTH:]], axis=0)
            xtok[w] = x
            center = x - jnp.mean(x, axis=1, keepdims=True)
            inverse = lax.rsqrt(jnp.mean(center * center, axis=1, keepdims=True) + EPS)
            normed = center * inverse
            xhat[w] = normed
            spread_inv[w] = inverse
            x_n = (normed * gain).astype(BF16)
            proj_t[w] = dot_nt(w_t[...], x_n).astype(BF16)
            kv = dot_nn(x_n, w_in[:, WIDTH:]).astype(BF16)
            for h in range(HEADS):
                k_nat[w, h] = kv[:, h * HEAD_DIM : (h + 1) * HEAD_DIM]
                v_nat[w, h] = kv[:, WIDTH + h * HEAD_DIM : WIDTH + (h + 1) * HEAD_DIM]
        wait_halo(1, slot)
        unpack_in(1, slot)
        for w in range(WINDOWS):
            block = xw[w * CELLS : (w + 1) * CELLS, :]
            c = jnp.concatenate([block[:, :WIDTH], block[:, WIDTH:]], axis=0)
            ctok[w] = c
            gmix_t[w] = dot_nt(wo_in[...], c.astype(BF16)).astype(BF16)

        first_row = jnp.where(slot == 0, lat, up) * WIN_LAT + RIM_R
        key_row = lax.rem(first_row + key_band, total_rows)
        query_row = lax.rem(first_row + query_band, total_rows)
        real = jnp.zeros((TOKENS, TOKENS), jnp.int32)
        for a in range(WIN_LAT):
            real = jnp.where(key_band == a, pad_ref[lax.rem(first_row + a, total_rows)], real)
        allowed = (jnp.abs(query_row - key_row) < WIN_LAT) & (real == 1)

        for s in range(1, steps):
            bias_passed(slot, s).wait_recv()
        for p in range(PAIRS):
            owner, r = p // pairs_here, p % pairs_here
            zq, zt = p // ZONE, p % ZONE
            spread[zt * 8 : zt * 8 + 8, zq * SLOT : (zq + 1) * SLOT] = bias_recv[
                slot, owner, :, r * SLOT : (r + 1) * SLOT
            ]
        table = spread[...]
        high = table.astype(BF16)
        rest = table - high.astype(F32)
        middle = rest.astype(BF16)
        low = (rest - middle.astype(F32)).astype(BF16)
        rows = ZONE * 8
        stacked = jnp.concatenate([high, middle, low], axis=0)
        for b in range(WIN_LON):
            three = dot_nn(stacked, spreader[b])
            wide = three[0:rows] + (three[rows : 2 * rows] + three[2 * rows :])
            for zt in range(ZONE):
                row = (zt * WIN_LON + b) * 8
                bias_flat[0, row : row + 8, :] = wide[zt * 8 : zt * 8 + 8, 0:128]
                bias_flat[1, row : row + 8, 0 : TOKENS - 128] = wide[
                    zt * 8 : zt * 8 + 8, 128:TOKENS
                ]
        for h in range(HEADS):
            left = bias_flat[0, pl.ds(h, TOKENS, stride=8), :]
            right = bias_flat[1, pl.ds(h, TOKENS, stride=8), :]
            whole = jnp.concatenate([left, right[:, 0 : TOKENS - 128]], axis=1)
            bias_full[h] = jnp.where(allowed, whole, MASKED)

        def rows_of(part, h):
            return pl.ds(part * WIDTH + h * HEAD_DIM, HEAD_DIM)

        for h in range(HEADS):
            for w in range(WINDOWS):
                score_buf[w, h] = (
                    dot_nn(k_nat[w, h], proj_t[w, rows_of(0, h), :]) * SCALE + bias_full[h]
                )
                gw_buf[w, h] = dot_nn(v_nat[w, h], gmix_t[w, rows_of(0, h), :])
        for h in range(HEADS):
            summed = None
            for w in range(WINDOWS):
                scores = score_buf[w, h]
                raised = jnp.exp(scores - jnp.max(scores, axis=0, keepdims=True))
                weights = raised * (1.0 / jnp.sum(raised, axis=0, keepdims=True))
                p_low[w, h] = weights.astype(BF16)
                grad_w = gw_buf[w, h]
                grad_s = weights * (grad_w - jnp.sum(weights * grad_w, axis=0, keepdims=True))
                d_low[w, h] = grad_s.astype(BF16)
                summed = grad_s if summed is None else summed + grad_s
            gflat[0, pl.ds(h, TOKENS, stride=8), :] = summed[:, 0:128]
            gflat[1, pl.ds(h, TOKENS, stride=8), 0 : TOKENS - 128] = summed[:, 128:TOKENS]
        for h in range(HEADS):
            for w in range(WINDOWS):
                q_t = proj_t[w, rows_of(0, h), :]
                g_t = gmix_t[w, rows_of(0, h), :]
                weights_low = p_low[w, h]
                grad_low = d_low[w, h]
                mixed_t[w, rows_of(0, h), :] = dot_nn(
                    proj_t[w, rows_of(2, h), :], weights_low
                ).astype(BF16)
                gproj_t[w, rows_of(0, h), :] = (
                    dot_nn(proj_t[w, rows_of(1, h), :], grad_low) * SCALE
                ).astype(BF16)
                gproj_t[w, rows_of(1, h), :] = (dot_nt(q_t, grad_low) * SCALE).astype(BF16)
                gproj_t[w, rows_of(2, h), :] = dot_nt(g_t, weights_low).astype(BF16)

        give_back(
            0, slot, [xtok[w] + dot_tn(mixed_t[w], wo_in[...]) for w in range(WINDOWS)]
        )
        grads = []
        for w in range(WINDOWS):
            scaled = dot_tn(gproj_t[w], w_t[...]) * gain
            normed = xhat[w]
            centered = (
                scaled
                - jnp.mean(scaled, axis=1, keepdims=True)
                - normed * jnp.mean(scaled * normed, axis=1, keepdims=True)
            )
            grads.append(ctok[w] + spread_inv[w] * centered)
        give_back(1, slot, grads)

        total = jnp.zeros((ZONE * 8, BAND), F32)
        for b in range(WIN_LON):
            picked_rows = []
            for zt in range(ZONE):
                row = (zt * WIN_LON + b) * 8
                picked_rows.append(
                    jnp.concatenate(
                        [
                            gflat[0, row : row + 8, :],
                            gflat[1, row : row + 8, 0 : TOKENS - 128],
                        ],
                        axis=1,
                    )
                )
            part = jnp.concatenate(picked_rows, axis=0).astype(BF16)
            total = total + dot_nn(part, gatherer[b])
        spread[...] = total
        for p in range(PAIRS):
            owner, r = p // pairs_here, p % pairs_here
            zq, zt = p // ZONE, p % ZONE
            table_msg[slot, owner, :, r * SLOT : (r + 1) * SLOT] = spread[
                zt * 8 : zt * 8 + 8, zq * SLOT : (zq + 1) * SLOT
            ]

        for s in range(1, steps):
            table_pass(slot, s).start()
        return carry

    rows_here = 1 + one_if_first - one_if_last
    lax.fori_loop(0, rows_here, window_row, 0)

    def take_back(kind, dst):
        def arrived_big(half):
            remote(
                res_big.at[kind, 0, half],
                back_big.at[kind, half],
                back_send.at[kind, 0, 0],
                back_recv.at[kind, half],
                (dn, lon),
            ).wait_recv()

        @pl.when(is_last)
        def _():
            arrived_big(0)

        @pl.when(jnp.logical_not(is_first))
        def _():
            arrived_big(1)

        for half in range(2):
            remote(
                res_small.at[kind, 0, half],
                back_small.at[kind, half],
                back_send.at[kind, 0, 1],
                back_recv.at[kind, 2 + half],
                (dn, rt),
            ).wait_recv()
        for half, first in ((0, RIM_R), (1, 0)):
            base, side = half * 88, 64 + half * 88
            tmp[base : base + BIG, :] = back_big[kind, half].astype(F32)
            tmp[side : side + SMALL, :] = back_small[kind, half].astype(F32)
            for r in range(RIM_R):
                row = (first + r) * COLS
                raw[row + 6 : row + 18, :] = tmp[base + r * 12 : base + r * 12 + 12, :]
                raw[row + 18 : row + 24, :] = tmp[base + 36 + r * 6 : base + 42 + r * 6, :]
                raw[row : row + 6, :] = tmp[side + r * 6 : side + 6 + r * 6, :]
        for r in range(WIN_LAT):
            dst[r] = raw[r * COLS : (r + 1) * COLS, :].astype(BF16)

    def table_row(slot, carry):
        summed = table_msg[slot, pl.ds(column * RUN, RUN)]
        for s in range(1, steps):
            table_passed(slot, s).wait_recv()
        for s in range(1, steps):
            summed = summed + table_mid[slot, column_peer(s)]
        table_out[slot] = summed

        def send_table(s, inner):
            table_copy(slot, s).start()
            return inner

        lax.fori_loop(1 - slot, RUN, send_table, 0)

        @pl.when(slot == 0)
        def _():
            table_recv[inside] = table_out[0, inside]

        return carry

    lax.fori_loop(0, rows_here, table_row, 0)
    take_back(0, out_ref)
    take_back(1, grads_ref)

    def wait_table(s, carry):
        table_arrival(s).wait_recv()
        return carry

    lax.fori_loop(1 - one_if_last, RUN, wait_table, 0)
    added = table_recv[0]
    for j in range(1, RUN):
        added = added + table_recv[j]
    for r in range(pairs_here):
        piece = added[:, r * SLOT : r * SLOT + OFFSETS]
        for h in range(HEADS):
            table_ref[h, r] = piece[h : h + 1, :]

    for kind in range(2):

        @pl.when(is_last)
        def _():
            big_last(kind).wait_send()

        @pl.when(jnp.logical_not(is_first))
        def _():
            big_up(kind).wait_send()

        small_low(kind).wait_send()
        small_top(kind).wait_send()

    def drain_bias(s, carry):
        bias_copy(s).wait_send()
        return carry

    lax.fori_loop(1 - one_if_last, RUN, drain_bias, 0)

    def drain_row(slot, carry):
        for kind in range(2):
            back_copy_big(kind, slot).wait_send()
            for half in range(2):
                back_copy_small(kind, slot, half).wait_send()

        def drain_table(s, inner):
            table_copy(slot, s).wait_send()
            return inner

        lax.fori_loop(1 - slot, RUN, drain_table, 0)
        for s in range(1, steps):
            bias_pass(slot, s).wait_send()
            table_pass(slot, s).wait_send()
        return carry

    lax.fori_loop(0, rows_here, drain_row, 0)


def place_out(*refs):
    sources, targets, sem = refs[:3], refs[3:6], refs[6]
    copies = [
        pltpu.make_async_copy(src, dst, sem.at[n])
        for n, (src, dst) in enumerate(zip(sources, targets))
    ]
    for copy in copies:
        copy.start()
    for copy in copies:
        copy.wait()


def solution(mesh):
    lat_size, lon_size = mesh.shape["lat"], mesh.shape["lon"]
    pairs_here = PAIRS // lon_size
    lanes = -(-pairs_here * SLOT // 128) * 128

    def per_device(fields, norm_gain, project_in, project_out, bias_table, pad_rows, cotangent):
        hbm_spec = pl.BlockSpec(memory_space=pltpu.HBM)
        vmem_spec = pl.BlockSpec(memory_space=pltpu.VMEM)
        out_fields, field_grads, table_grads = pl.pallas_call(
            functools.partial(kernel, lat_size, lon_size, pairs_here),
            out_shape=(
                jax.ShapeDtypeStruct(fields.shape, BF16),
                jax.ShapeDtypeStruct(fields.shape, BF16),
                jax.ShapeDtypeStruct((HEADS, pairs_here, 1, OFFSETS), F32),
            ),
            in_specs=[hbm_spec] * 7,
            out_specs=(vmem_spec, vmem_spec, vmem_spec),
            scratch_shapes=[
                pltpu.VMEM(fields.shape, BF16),
                pltpu.VMEM(fields.shape, BF16),
                pltpu.VMEM(project_in.shape, BF16),
                pltpu.VMEM(project_out.shape, BF16),
                pltpu.VMEM((HEADS, pairs_here, 1, OFFSETS), F32),
                pltpu.VMEM((1, WIDTH), F32),
                pltpu.SMEM(pad_rows.shape, jnp.int32),
                pltpu.VMEM((WIN_LAT * COLS, FEATS), F32),
                pltpu.VMEM((WINDOWS * CELLS, FEATS), F32),
                pltpu.VMEM((176, FEATS), F32),
                pltpu.VMEM((2, 2, BIG, FEATS), BF16),
                pltpu.VMEM((2, 2, SMALL, FEATS), BF16),
                pltpu.VMEM((2, 2, 2, BIG, FEATS), BF16),
                pltpu.VMEM((2, 2, 2, SMALL, FEATS), BF16),
                pltpu.VMEM((2, 2, 2, BIG, FEATS), BF16),
                pltpu.VMEM((2, 2, 2, SMALL, FEATS), BF16),
                pltpu.VMEM((2, 2, BIG, FEATS), BF16),
                pltpu.VMEM((2, 2, SMALL, FEATS), BF16),
                pltpu.VMEM((8, lanes), F32),
                pltpu.VMEM((2, lon_size, 8, lanes), F32),
                pltpu.VMEM((ZONE * 8, BAND), F32),
                pltpu.VMEM((2, TOKENS * 8, 128), F32),
                pltpu.VMEM((HEADS, TOKENS, TOKENS), F32),
                pltpu.VMEM((3 * WIDTH, WIDTH), BF16),
                pltpu.VMEM((WINDOWS, TOKENS, WIDTH), F32),
                pltpu.VMEM((WINDOWS, TOKENS, WIDTH), F32),
                pltpu.VMEM((WINDOWS, TOKENS, WIDTH), F32),
                pltpu.VMEM((WINDOWS, TOKENS, 1), F32),
                pltpu.VMEM((WINDOWS, 3 * WIDTH, TOKENS), BF16),
                pltpu.VMEM((WINDOWS, HEADS, TOKENS, HEAD_DIM), BF16),
                pltpu.VMEM((WINDOWS, HEADS, TOKENS, HEAD_DIM), BF16),
                pltpu.VMEM((WINDOWS, WIDTH, TOKENS), BF16),
                pltpu.VMEM((WINDOWS, WIDTH, TOKENS), BF16),
                pltpu.VMEM((WINDOWS, 3 * WIDTH, TOKENS), BF16),
                pltpu.VMEM((2, TOKENS * 8, 128), F32),
                pltpu.VMEM((WINDOWS * CELLS, FEATS), F32),
                pltpu.VMEM((2, lon_size, 8, lanes), F32),
                pltpu.VMEM((2, lon_size // RUN, RUN, 8, lanes), F32),
                pltpu.VMEM((2, RUN, 8, lanes), F32),
                pltpu.VMEM((RUN, 8, lanes), F32),
                pltpu.VMEM((WIN_LON, BAND, TOKENS), BF16),
                pltpu.VMEM((WIN_LON, TOKENS, BAND), BF16),
                pltpu.VMEM((WINDOWS, HEADS, TOKENS, TOKENS), F32),
                pltpu.VMEM((WINDOWS, HEADS, TOKENS, TOKENS), F32),
                pltpu.VMEM((WINDOWS, HEADS, TOKENS, TOKENS), BF16),
                pltpu.VMEM((WINDOWS, HEADS, TOKENS, TOKENS), BF16),
                pltpu.SemaphoreType.DMA((7,)),
                pltpu.SemaphoreType.DMA((2, 4)),
                pltpu.SemaphoreType.DMA((2, 2, 3)),
                pltpu.SemaphoreType.DMA((2, 2, 3)),
                pltpu.SemaphoreType.DMA((2, 4)),
                pltpu.SemaphoreType.DMA((RUN,)),
                pltpu.SemaphoreType.DMA((2, lon_size)),
                pltpu.SemaphoreType.DMA((2, lon_size // RUN)),
                pltpu.SemaphoreType.DMA((2, lon_size // RUN)),
                pltpu.SemaphoreType.DMA((2, lon_size // RUN)),
                pltpu.SemaphoreType.DMA((2, lon_size // RUN)),
                pltpu.SemaphoreType.DMA((2, RUN)),
                pltpu.SemaphoreType.DMA((RUN,)),
                pltpu.SemaphoreType.REGULAR,
            ],
            compiler_params=pltpu.CompilerParams(
                collective_id=0, has_side_effects=True, vmem_limit_bytes=48 << 20
            ),
        )(
            *(
                pltpu.with_memory_space_constraint(x, pltpu.HBM)
                for x in (
                    fields,
                    norm_gain.reshape(1, WIDTH),
                    project_in,
                    project_out,
                    bias_table.reshape(HEADS, pairs_here, 1, OFFSETS),
                    pad_rows,
                    cotangent,
                )
            )
        )
        parts = (out_fields, field_grads, table_grads)
        any_spec = pl.BlockSpec(memory_space=pl.ANY)
        out_fields, field_grads, table_grads = pl.pallas_call(
            place_out,
            out_shape=tuple(jax.ShapeDtypeStruct(x.shape, x.dtype) for x in parts),
            in_specs=[any_spec] * 3,
            out_specs=(hbm_spec,) * 3,
            scratch_shapes=[pltpu.SemaphoreType.DMA((3,))],
            compiler_params=pltpu.CompilerParams(vmem_limit_bytes=1 << 20),
        )(*parts)
        return out_fields, field_grads, table_grads.reshape(bias_table.shape)

    in_specs = (
        P("lat", "lon", None),
        P(),
        P(),
        P(),
        P("lat", None, "lon", None),
        P(),
        P("lat", "lon", None),
    )
    out_specs = (P("lat", "lon", None), P("lat", "lon", None), P("lat", None, "lon", None))
    return jax.shard_map(
        per_device, mesh=mesh, in_specs=in_specs, out_specs=out_specs, check_vma=False
    )
```

```python
import functools

import jax
import jax.numpy as jnp
from jax import lax
from jax.experimental import pallas as pl
from jax.experimental.pallas import tpu as pltpu
from jax.sharding import PartitionSpec as P

WIDTH = 192
HEADS = 6
HEAD_DIM = 32
LEVELS = 2
WIN_LAT = 6
WIN_LON = 12
ZONE = LEVELS * WIN_LAT
CELLS = WIN_LAT * WIN_LON
TOKENS = LEVELS * CELLS
OFFSETS = 23
SLOT = 24
PAIRS = ZONE * ZONE
RIM_R = WIN_LAT // 2
RIM_C = WIN_LON // 2
WINDOWS = 2
COLS = WINDOWS * WIN_LON
FEATS = LEVELS * WIDTH
BAND = 384
BIG = 56
SMALL = 24
RUN = 4
SCALE = HEAD_DIM**-0.5
EPS = 1e-05
MASKED = -1e30
MESH = pl.DeviceIdType.MESH
F32 = jnp.float32
BF16 = jnp.bfloat16


def dot_nn(a, b):
    return lax.dot_general(a, b, (((1,), (0,)), ((), ())), preferred_element_type=F32)


def dot_nt(a, b):
    return lax.dot_general(a, b, (((1,), (1,)), ((), ())), preferred_element_type=F32)


def dot_tn(a, b):
    return lax.dot_general(a, b, (((0,), (0,)), ((), ())), preferred_element_type=F32)


def kernel(
    lat_size,
    lon_size,
    pairs_here,
    fields_hbm,
    gain_hbm,
    win_hbm,
    wout_hbm,
    bias_hbm,
    pad_hbm,
    cot_hbm,
    out_ref,
    grads_ref,
    table_ref,
    f_in,
    c_in,
    w_in,
    wo_in,
    bias_in,
    gain_ref,
    pad_ref,
    raw,
    xw,
    tmp,
    send_big,
    send_small,
    in_big,
    in_small,
    res_big,
    res_small,
    back_big,
    back_small,
    bias_msg,
    bias_recv,
    spread,
    bias_flat,
    bias_full,
    w_t,
    xtok,
    ctok,
    xhat,
    spread_inv,
    proj_t,
    k_nat,
    v_nat,
    gmix_t,
    mixed_t,
    gproj_t,
    gflat,
    cells,
    table_msg,
    table_mid,
    table_out,
    table_recv,
    spreader,
    gatherer,
    score_buf,
    gw_buf,
    p_low,
    d_low,
    load_sem,
    halo_send,
    halo_recv,
    back_send,
    back_recv,
    bias_send,
    bias_rsem,
    pass_send,
    pass_recv,
    table_xsend,
    table_xrecv,
    table_send,
    table_rsem,
    ready_sem,
):
    lat = lax.axis_index("lat")
    lon = lax.axis_index("lon")
    up = lax.rem(lat + lat_size - 1, lat_size)
    dn = lax.rem(lat + 1, lat_size)
    lf = lax.rem(lon + lon_size - 1, lon_size)
    rt = lax.rem(lon + 1, lon_size)
    group = lat_size // 2
    place = lax.rem(lat, group)
    is_first = place == 0
    is_last = place == group - 1
    before_last = place == group - 2
    one_if_last = jnp.where(is_last, 1, 0)
    is_helper = place == 1
    one_if_first = jnp.where(is_first, 1, 0)
    one_if_helper = jnp.where(is_helper, 1, 0)
    helper = lax.rem(lat + 2, lat_size)
    helped = lax.rem(lat + lat_size - 2, lat_size)
    steps = lon_size // RUN
    column = lon // RUN
    inside = lax.rem(lon, RUN)
    at_start = inside == 0
    at_end = inside == RUN - 1
    below = jnp.where(is_last, helper, lat)
    above = jnp.where(is_first, dn, up)

    barrier = pltpu.get_barrier_semaphore()

    def signal(dev):
        pl.semaphore_signal(barrier, inc=1, device_id=dev, device_id_type=MESH)

    def greet_seam(s, carry):
        signal((helped, lax.rem(lon + s, lon_size)))
        return carry

    def run_peer(s):
        return column * RUN + lax.rem(inside + s, RUN)

    def column_peer(s):
        return lax.rem(column + s, steps)

    @pl.when(is_helper)
    def _():
        signal((up, rt))
        lax.fori_loop(0, lon_size, greet_seam, 0)

    @pl.when(is_first)
    def _():
        signal((dn, lf))

    @pl.when(jnp.logical_not(is_first))
    def _():
        signal((up, lon))
        signal((up, lf))

    @pl.when(jnp.logical_not(is_last))
    def _():
        signal((dn, lon))
        for s in range(1, RUN):
            signal((lat, run_peer(s)))
        for s in range(1, steps):
            signal((lat, column_peer(s) * RUN + inside))

    @pl.when(jnp.logical_not(is_last) & at_start)
    def _():
        signal((lat, lf))

    @pl.when(jnp.logical_not(is_last) & at_end)
    def _():
        signal((lat, rt))

    @pl.when(jnp.logical_not(is_last | before_last))
    def _():
        signal((dn, rt))

    loads = [
        pltpu.make_async_copy(src, dst, load_sem.at[n])
        for n, (src, dst) in enumerate(
            (
                (bias_hbm, bias_in),
                (fields_hbm, f_in),
                (cot_hbm, c_in),
                (win_hbm, w_in),
                (wout_hbm, wo_in),
                (gain_hbm, gain_ref),
                (pad_hbm, pad_ref),
            )
        )
    ]
    for load in loads:
        load.start()

    def remote(src, dst, send, recv, dev):
        return pltpu.make_async_remote_copy(
            src_ref=src,
            dst_ref=dst,
            send_sem=send,
            recv_sem=recv,
            device_id=dev,
            device_id_type=MESH,
        )

    def big_last(kind):
        return remote(
            send_big.at[kind, 0],
            in_big.at[kind, 1, 0],
            halo_send.at[kind, 0],
            halo_recv.at[kind, 1, 0],
            (helper, lon),
        )

    def big_top(kind):
        return remote(
            send_big.at[kind, 1],
            in_big.at[kind, one_if_first, 1],
            halo_send.at[kind, 1],
            halo_recv.at[kind, one_if_first, 1],
            (above, lon),
        )

    def small_low(kind):
        return remote(
            send_small.at[kind, 0],
            in_small.at[kind, one_if_last, 0],
            halo_send.at[kind, 2],
            halo_recv.at[kind, one_if_last, 2],
            (below, lf),
        )

    def small_top(kind):
        return remote(
            send_small.at[kind, 1],
            in_small.at[kind, one_if_first, 1],
            halo_send.at[kind, 3],
            halo_recv.at[kind, one_if_first, 3],
            (above, lf),
        )

    def wait_halo(kind, slot):
        def arrived_big(half, carry):
            remote(
                send_big.at[kind, 0],
                in_big.at[kind, slot, half],
                halo_send.at[kind, 0],
                halo_recv.at[kind, slot, half],
                (dn, lon),
            ).wait_recv()
            return carry

        lax.fori_loop(1 - slot, 2, arrived_big, 0)
        for half in range(2):
            remote(
                send_small.at[kind, half],
                in_small.at[kind, slot, half],
                halo_send.at[kind, 2],
                halo_recv.at[kind, slot, 2 + half],
                (dn, lon),
            ).wait_recv()

    def pack_in(src, kind):
        for r in range(WIN_LAT):
            raw[r * COLS : (r + 1) * COLS, :] = src[r].astype(F32)
        for half, first in ((0, RIM_R), (1, 0)):
            base, side = half * 88, 64 + half * 88
            for r in range(RIM_R):
                row = (first + r) * COLS
                tmp[base + r * 12 : base + r * 12 + 12, :] = raw[row + 6 : row + 18, :]
                tmp[base + 36 + r * 6 : base + 42 + r * 6, :] = raw[row + 18 : row + 24, :]
                tmp[side + r * 6 : side + 6 + r * 6, :] = raw[row : row + 6, :]
            piece = tmp[base : base + BIG, :].astype(BF16)
            send_big[kind, half] = piece
            if half == 0:
                in_big[kind, 0, 0] = piece
            send_small[kind, half] = tmp[side : side + SMALL, :].astype(BF16)

    def unpack_in(kind, slot):
        for half in range(2):
            base, side = half * 88, 64 + half * 88
            tmp[base : base + BIG, :] = in_big[kind, slot, half].astype(F32)
            tmp[side : side + SMALL, :] = in_small[kind, slot, half].astype(F32)
            xw[36 * half : 36 * half + 36, :] = tmp[base : base + 36, :]
            for r in range(RIM_R):
                row = CELLS + (RIM_R * half + r) * 12
                xw[row : row + 6, :] = tmp[base + 36 + r * 6 : base + 42 + r * 6, :]
                xw[row + 6 : row + 12, :] = tmp[side + r * 6 : side + 6 + r * 6, :]

    tmp[...] = jnp.zeros_like(tmp)
    bias_msg[...] = jnp.zeros_like(bias_msg)
    loads[0].wait()
    for r in range(pairs_here):
        for h in range(HEADS):
            bias_msg[h : h + 1, r * SLOT : r * SLOT + OFFSETS] = bias_in[h, r]
    bias_recv[0, lon] = bias_msg[...]
    loads[1].wait()
    pack_in(f_in, 0)

    around = RUN + steps - 2 + jnp.where(at_start | at_end, 1, 0)
    greetings = jnp.where(
        is_last, lon_size + 1, around + jnp.where(is_first, 3, 4 + one_if_helper)
    )
    pl.semaphore_wait(barrier, greetings)

    @pl.when(before_last)
    def _():
        pl.semaphore_signal(ready_sem, inc=1, device_id=(dn, rt), device_id_type=MESH)

    def bias_copy(s):
        return remote(
            bias_msg,
            bias_recv.at[one_if_last, lon],
            bias_send.at[s],
            bias_rsem.at[one_if_last, lon],
            (below, run_peer(s)),
        )

    def bias_arrival(slot, s):
        source = run_peer(s)
        return remote(
            bias_msg,
            bias_recv.at[slot, source],
            bias_send.at[s],
            bias_rsem.at[slot, source],
            (dn, lon),
        )

    def bias_pass(slot, s):
        mine = bias_recv.at[slot, pl.ds(column * RUN, RUN)]
        return remote(
            mine,
            mine,
            pass_send.at[slot, s],
            pass_recv.at[slot, column],
            (lat, column_peer(s) * RUN + inside),
        )

    def bias_passed(slot, s):
        source = column_peer(s)
        theirs = bias_recv.at[slot, pl.ds(source * RUN, RUN)]
        return remote(
            theirs, theirs, pass_send.at[slot, s], pass_recv.at[slot, source], (dn, lon)
        )

    def send_bias(s, carry):
        bias_copy(s).start()
        return carry

    def send_halo(kind):
        @pl.when(is_last)
        def _():
            big_last(kind).start()

        small_low(kind).start()

        big_top(kind).start()

        @pl.when(jnp.logical_not(is_last))
        def _():
            small_top(kind).start()

    lax.fori_loop(1 - one_if_last, RUN, send_bias, 0)
    send_halo(0)
    loads[2].wait()
    pack_in(c_in, 1)
    send_halo(1)

    @pl.when(is_last)
    def _():
        pl.semaphore_wait(ready_sem, 1)
        for kind in range(2):
            small_top(kind).start()

    gflat[...] = jnp.zeros_like(gflat)
    table_msg[...] = jnp.zeros_like(table_msg)
    spread[...] = jnp.zeros_like(spread)

    def make_selectors(b, carry):
        lane = lax.broadcasted_iota(jnp.int32, (BAND, TOKENS), 0)
        query = lax.broadcasted_iota(jnp.int32, (BAND, TOKENS), 1)
        picked = (query // WIN_LON) * SLOT + query % WIN_LON + WIN_LON - 1 - b
        spreader[b] = (lane == picked).astype(F32).astype(BF16)
        lane = lax.broadcasted_iota(jnp.int32, (TOKENS, BAND), 1)
        query = lax.broadcasted_iota(jnp.int32, (TOKENS, BAND), 0)
        picked = (query // WIN_LON) * SLOT + query % WIN_LON + WIN_LON - 1 - b
        gatherer[b] = (lane == picked).astype(F32).astype(BF16)
        return carry

    lax.fori_loop(0, WIN_LON, make_selectors, 0)
    loads[3].wait()
    loads[4].wait()
    loads[5].wait()
    loads[6].wait()
    w_t[...] = w_in[...].astype(F32).T.astype(BF16)
    total_rows = lat_size * WIN_LAT
    key_band = (lax.broadcasted_iota(jnp.int32, (TOKENS, TOKENS), 0) // WIN_LON) % WIN_LAT
    query_band = (lax.broadcasted_iota(jnp.int32, (TOKENS, TOKENS), 1) // WIN_LON) % WIN_LAT

    def owner_of(slot, half):
        return lax.rem(lat + half - 2 * slot + lat_size, lat_size)

    def back_copy_big(kind, slot, half):
        return remote(
            res_big.at[kind, slot, half],
            back_big.at[kind, half],
            back_send.at[kind, slot, half],
            back_recv.at[kind, half],
            (owner_of(slot, half), lon),
        )

    def back_copy_small(kind, slot, half):
        return remote(
            res_small.at[kind, slot, half],
            back_small.at[kind, half],
            back_send.at[kind, slot, 2 + half],
            back_recv.at[kind, 2 + half],
            (owner_of(slot, half), rt),
        )

    def give_back(kind, slot, tokens):
        for w in range(WINDOWS):
            cells[w * CELLS : (w + 1) * CELLS, 0:WIDTH] = tokens[w][0:CELLS]
            cells[w * CELLS : (w + 1) * CELLS, WIDTH:] = tokens[w][CELLS:]
        for half in range(2):
            base, side = half * 88, 64 + half * 88
            tmp[base : base + 36, :] = cells[36 * half : 36 * half + 36, :]
            for r in range(RIM_R):
                row = CELLS + (RIM_R * half + r) * 12
                tmp[base + 36 + r * 6 : base + 42 + r * 6, :] = cells[row : row + 6, :]
                tmp[side + r * 6 : side + 6 + r * 6, :] = cells[row + 6 : row + 12, :]
            res_big[kind, slot, half] = tmp[base : base + BIG, :].astype(BF16)
            res_small[kind, slot, half] = tmp[side : side + SMALL, :].astype(BF16)
        for half in range(2):
            back_copy_small(kind, slot, half).start()
        back_copy_big(kind, slot, 1).start()

        @pl.when(slot == 1)
        def _():
            back_copy_big(kind, slot, 0).start()

        @pl.when(slot == 0)
        def _():
            back_big[kind, 0] = res_big[kind, 0, 0]

    def table_pass(slot, s):
        target = column_peer(s)
        return remote(
            table_msg.at[slot, pl.ds(target * RUN, RUN)],
            table_mid.at[slot, column],
            table_xsend.at[slot, s],
            table_xrecv.at[slot, column],
            (lat, target * RUN + inside),
        )

    def table_passed(slot, s):
        source = column_peer(s)
        return remote(
            table_msg.at[slot, pl.ds(source * RUN, RUN)],
            table_mid.at[slot, source],
            table_xsend.at[slot, s],
            table_xrecv.at[slot, source],
            (lat, lon),
        )

    def table_copy(slot, s):
        peer = lax.rem(inside + s, RUN)
        return remote(
            table_out.at[slot, peer],
            table_recv.at[inside],
            table_send.at[slot, s],
            table_rsem.at[inside],
            (jnp.where(slot == 0, lat, helped), run_peer(s)),
        )

    def table_arrival(s):
        source = lax.rem(inside + s, RUN)
        return remote(
            table_out.at[0, source],
            table_recv.at[source],
            table_send.at[0, s],
            table_rsem.at[source],
            (lat, run_peer(s)),
        )

    def table_row(slot, carry):
        summed = table_msg[slot, pl.ds(column * RUN, RUN)]
        for s in range(1, steps):
            table_passed(slot, s).wait_recv()
        for s in range(1, steps):
            summed = summed + table_mid[slot, column_peer(s)]
        table_out[slot] = summed

        def send_table(s, inner):
            table_copy(slot, s).start()
            return inner

        lax.fori_loop(1 - slot, RUN, send_table, 0)

        @pl.when(slot == 0)
        def _():
            table_recv[inside] = table_out[0, inside]

        return carry

    def window_row(slot, carry):
        @pl.when(slot == 1)
        def _():
            table_row(0, 0)

        def wait_bias(s, inner):
            bias_arrival(slot, s).wait_recv()
            return inner

        lax.fori_loop(1 - slot, RUN, wait_bias, 0)
        for s in range(1, steps):
            bias_pass(slot, s).start()
        gain = gain_ref[...]
        wait_halo(0, slot)
        unpack_in(0, slot)
        for w in range(WINDOWS):
            block = xw[w * CELLS : (w + 1) * CELLS, :]
            x = jnp.concatenate([block[:, :WIDTH], block[:, WIDTH:]], axis=0)
            xtok[w] = x
            center = x - jnp.mean(x, axis=1, keepdims=True)
            inverse = lax.rsqrt(jnp.mean(center * center, axis=1, keepdims=True) + EPS)
            normed = center * inverse
            xhat[w] = normed
            spread_inv[w] = inverse
            x_n = (normed * gain).astype(BF16)
            proj_t[w] = dot_nt(w_t[...], x_n).astype(BF16)
            kv = dot_nn(x_n, w_in[:, WIDTH:]).astype(BF16)
            for h in range(HEADS):
                k_nat[w, h] = kv[:, h * HEAD_DIM : (h + 1) * HEAD_DIM]
                v_nat[w, h] = kv[:, WIDTH + h * HEAD_DIM : WIDTH + (h + 1) * HEAD_DIM]
        wait_halo(1, slot)
        unpack_in(1, slot)
        for w in range(WINDOWS):
            block = xw[w * CELLS : (w + 1) * CELLS, :]
            c = jnp.concatenate([block[:, :WIDTH], block[:, WIDTH:]], axis=0)
            ctok[w] = c
            gmix_t[w] = dot_nt(wo_in[...], c.astype(BF16)).astype(BF16)

        first_row = jnp.where(slot == 0, lat, helped) * WIN_LAT + RIM_R
        key_row = lax.rem(first_row + key_band, total_rows)
        query_row = lax.rem(first_row + query_band, total_rows)
        real = jnp.zeros((TOKENS, TOKENS), jnp.int32)
        for a in range(WIN_LAT):
            real = jnp.where(key_band == a, pad_ref[lax.rem(first_row + a, total_rows)], real)
        allowed = (jnp.abs(query_row - key_row) < WIN_LAT) & (real == 1)

        for s in range(1, steps):
            bias_passed(slot, s).wait_recv()
        for p in range(PAIRS):
            owner, r = p // pairs_here, p % pairs_here
            zq, zt = p // ZONE, p % ZONE
            spread[zt * 8 : zt * 8 + 8, zq * SLOT : (zq + 1) * SLOT] = bias_recv[
                slot, owner, :, r * SLOT : (r + 1) * SLOT
            ]
        table = spread[...]
        high = table.astype(BF16)
        rest = table - high.astype(F32)
        middle = rest.astype(BF16)
        low = (rest - middle.astype(F32)).astype(BF16)
        rows = ZONE * 8
        stacked = jnp.concatenate([high, middle, low], axis=0)
        for b in range(WIN_LON):
            three = dot_nn(stacked, spreader[b])
            wide = three[0:rows] + (three[rows : 2 * rows] + three[2 * rows :])
            for zt in range(ZONE):
                row = (zt * WIN_LON + b) * 8
                bias_flat[0, row : row + 8, :] = wide[zt * 8 : zt * 8 + 8, 0:128]
                bias_flat[1, row : row + 8, 0 : TOKENS - 128] = wide[
                    zt * 8 : zt * 8 + 8, 128:TOKENS
                ]
        for h in range(HEADS):
            left = bias_flat[0, pl.ds(h, TOKENS, stride=8), :]
            right = bias_flat[1, pl.ds(h, TOKENS, stride=8), :]
            whole = jnp.concatenate([left, right[:, 0 : TOKENS - 128]], axis=1)
            bias_full[h] = jnp.where(allowed, whole, MASKED)

        def rows_of(part, h):
            return pl.ds(part * WIDTH + h * HEAD_DIM, HEAD_DIM)

        for h in range(HEADS):
            for w in range(WINDOWS):
                score_buf[w, h] = (
                    dot_nn(k_nat[w, h], proj_t[w, rows_of(0, h), :]) * SCALE + bias_full[h]
                )
                gw_buf[w, h] = dot_nn(v_nat[w, h], gmix_t[w, rows_of(0, h), :])
        for h in range(HEADS):
            summed = None
            for w in range(WINDOWS):
                scores = score_buf[w, h]
                raised = jnp.exp(scores - jnp.max(scores, axis=0, keepdims=True))
                weights = raised * (1.0 / jnp.sum(raised, axis=0, keepdims=True))
                p_low[w, h] = weights.astype(BF16)
                grad_w = gw_buf[w, h]
                grad_s = weights * (grad_w - jnp.sum(weights * grad_w, axis=0, keepdims=True))
                d_low[w, h] = grad_s.astype(BF16)
                summed = grad_s if summed is None else summed + grad_s
            gflat[0, pl.ds(h, TOKENS, stride=8), :] = summed[:, 0:128]
            gflat[1, pl.ds(h, TOKENS, stride=8), 0 : TOKENS - 128] = summed[:, 128:TOKENS]
        for h in range(HEADS):
            for w in range(WINDOWS):
                q_t = proj_t[w, rows_of(0, h), :]
                g_t = gmix_t[w, rows_of(0, h), :]
                weights_low = p_low[w, h]
                grad_low = d_low[w, h]
                mixed_t[w, rows_of(0, h), :] = dot_nn(
                    proj_t[w, rows_of(2, h), :], weights_low
                ).astype(BF16)
                gproj_t[w, rows_of(0, h), :] = (
                    dot_nn(proj_t[w, rows_of(1, h), :], grad_low) * SCALE
                ).astype(BF16)
                gproj_t[w, rows_of(1, h), :] = (dot_nt(q_t, grad_low) * SCALE).astype(BF16)
                gproj_t[w, rows_of(2, h), :] = dot_nt(g_t, weights_low).astype(BF16)

        give_back(
            0, slot, [xtok[w] + dot_tn(mixed_t[w], wo_in[...]) for w in range(WINDOWS)]
        )
        grads = []
        for w in range(WINDOWS):
            scaled = dot_tn(gproj_t[w], w_t[...]) * gain
            normed = xhat[w]
            centered = (
                scaled
                - jnp.mean(scaled, axis=1, keepdims=True)
                - normed * jnp.mean(scaled * normed, axis=1, keepdims=True)
            )
            grads.append(ctok[w] + spread_inv[w] * centered)
        give_back(1, slot, grads)

        total = jnp.zeros((ZONE * 8, BAND), F32)
        for b in range(WIN_LON):
            picked_rows = []
            for zt in range(ZONE):
                row = (zt * WIN_LON + b) * 8
                picked_rows.append(
                    jnp.concatenate(
                        [
                            gflat[0, row : row + 8, :],
                            gflat[1, row : row + 8, 0 : TOKENS - 128],
                        ],
                        axis=1,
                    )
                )
            part = jnp.concatenate(picked_rows, axis=0).astype(BF16)
            total = total + dot_nn(part, gatherer[b])
        spread[...] = total
        for p in range(PAIRS):
            owner, r = p // pairs_here, p % pairs_here
            zq, zt = p // ZONE, p % ZONE
            table_msg[slot, owner, :, r * SLOT : (r + 1) * SLOT] = spread[
                zt * 8 : zt * 8 + 8, zq * SLOT : (zq + 1) * SLOT
            ]

        for s in range(1, steps):
            table_pass(slot, s).start()
        return carry

    rows_here = 1 + one_if_helper - one_if_last
    lax.fori_loop(0, rows_here, window_row, 0)

    def take_back(kind, dst):
        def arrived_big(half):
            remote(
                res_big.at[kind, 0, half],
                back_big.at[kind, half],
                back_send.at[kind, 0, 0],
                back_recv.at[kind, half],
                (dn, lon),
            ).wait_recv()

        @pl.when(is_last)
        def _():
            arrived_big(0)

        arrived_big(1)
        for half in range(2):
            remote(
                res_small.at[kind, 0, half],
                back_small.at[kind, half],
                back_send.at[kind, 0, 1],
                back_recv.at[kind, 2 + half],
                (dn, rt),
            ).wait_recv()
        for half, first in ((0, RIM_R), (1, 0)):
            base, side = half * 88, 64 + half * 88
            tmp[base : base + BIG, :] = back_big[kind, half].astype(F32)
            tmp[side : side + SMALL, :] = back_small[kind, half].astype(F32)
            for r in range(RIM_R):
                row = (first + r) * COLS
                raw[row + 6 : row + 18, :] = tmp[base + r * 12 : base + r * 12 + 12, :]
                raw[row + 18 : row + 24, :] = tmp[base + 36 + r * 6 : base + 42 + r * 6, :]
                raw[row : row + 6, :] = tmp[side + r * 6 : side + 6 + r * 6, :]
        for r in range(WIN_LAT):
            dst[r] = raw[r * COLS : (r + 1) * COLS, :].astype(BF16)

    take_back(0, out_ref)
    lax.fori_loop(jnp.maximum(rows_here - 1, 0), rows_here, table_row, 0)
    take_back(1, grads_ref)

    def wait_table(s, carry):
        table_arrival(s).wait_recv()
        return carry

    lax.fori_loop(1 - one_if_last, RUN, wait_table, 0)
    added = table_recv[0]
    for j in range(1, RUN):
        added = added + table_recv[j]
    for r in range(pairs_here):
        piece = added[:, r * SLOT : r * SLOT + OFFSETS]
        for h in range(HEADS):
            table_ref[h, r] = piece[h : h + 1, :]

    for kind in range(2):

        @pl.when(is_last)
        def _():
            big_last(kind).wait_send()

        big_top(kind).wait_send()
        small_low(kind).wait_send()
        small_top(kind).wait_send()

    def drain_bias(s, carry):
        bias_copy(s).wait_send()
        return carry

    lax.fori_loop(1 - one_if_last, RUN, drain_bias, 0)

    def drain_row(slot, carry):
        for kind in range(2):
            back_copy_big(kind, slot, 1).wait_send()

            @pl.when(slot == 1)
            def _():
                back_copy_big(kind, slot, 0).wait_send()

            for half in range(2):
                back_copy_small(kind, slot, half).wait_send()

        def drain_table(s, inner):
            table_copy(slot, s).wait_send()
            return inner

        lax.fori_loop(1 - slot, RUN, drain_table, 0)
        for s in range(1, steps):
            bias_pass(slot, s).wait_send()
            table_pass(slot, s).wait_send()
        return carry

    lax.fori_loop(0, rows_here, drain_row, 0)


def place_out(*refs):
    sources, targets, sem = refs[:3], refs[3:6], refs[6]
    copies = [
        pltpu.make_async_copy(src, dst, sem.at[n])
        for n, (src, dst) in enumerate(zip(sources, targets))
    ]
    for copy in copies:
        copy.start()
    for copy in copies:
        copy.wait()


def solution(mesh):
    lat_size, lon_size = mesh.shape["lat"], mesh.shape["lon"]
    pairs_here = PAIRS // lon_size
    lanes = -(-pairs_here * SLOT // 128) * 128

    def per_device(fields, norm_gain, project_in, project_out, bias_table, pad_rows, cotangent):
        hbm_spec = pl.BlockSpec(memory_space=pltpu.HBM)
        vmem_spec = pl.BlockSpec(memory_space=pltpu.VMEM)
        out_fields, field_grads, table_grads = pl.pallas_call(
            functools.partial(kernel, lat_size, lon_size, pairs_here),
            out_shape=(
                jax.ShapeDtypeStruct(fields.shape, BF16),
                jax.ShapeDtypeStruct(fields.shape, BF16),
                jax.ShapeDtypeStruct((HEADS, pairs_here, 1, OFFSETS), F32),
            ),
            in_specs=[hbm_spec] * 7,
            out_specs=(vmem_spec, vmem_spec, vmem_spec),
            scratch_shapes=[
                pltpu.VMEM(fields.shape, BF16),
                pltpu.VMEM(fields.shape, BF16),
                pltpu.VMEM(project_in.shape, BF16),
                pltpu.VMEM(project_out.shape, BF16),
                pltpu.VMEM((HEADS, pairs_here, 1, OFFSETS), F32),
                pltpu.VMEM((1, WIDTH), F32),
                pltpu.SMEM(pad_rows.shape, jnp.int32),
                pltpu.VMEM((WIN_LAT * COLS, FEATS), F32),
                pltpu.VMEM((WINDOWS * CELLS, FEATS), F32),
                pltpu.VMEM((176, FEATS), F32),
                pltpu.VMEM((2, 2, BIG, FEATS), BF16),
                pltpu.VMEM((2, 2, SMALL, FEATS), BF16),
                pltpu.VMEM((2, 2, 2, BIG, FEATS), BF16),
                pltpu.VMEM((2, 2, 2, SMALL, FEATS), BF16),
                pltpu.VMEM((2, 2, 2, BIG, FEATS), BF16),
                pltpu.VMEM((2, 2, 2, SMALL, FEATS), BF16),
                pltpu.VMEM((2, 2, BIG, FEATS), BF16),
                pltpu.VMEM((2, 2, SMALL, FEATS), BF16),
                pltpu.VMEM((8, lanes), F32),
                pltpu.VMEM((2, lon_size, 8, lanes), F32),
                pltpu.VMEM((ZONE * 8, BAND), F32),
                pltpu.VMEM((2, TOKENS * 8, 128), F32),
                pltpu.VMEM((HEADS, TOKENS, TOKENS), F32),
                pltpu.VMEM((3 * WIDTH, WIDTH), BF16),
                pltpu.VMEM((WINDOWS, TOKENS, WIDTH), F32),
                pltpu.VMEM((WINDOWS, TOKENS, WIDTH), F32),
                pltpu.VMEM((WINDOWS, TOKENS, WIDTH), F32),
                pltpu.VMEM((WINDOWS, TOKENS, 1), F32),
                pltpu.VMEM((WINDOWS, 3 * WIDTH, TOKENS), BF16),
                pltpu.VMEM((WINDOWS, HEADS, TOKENS, HEAD_DIM), BF16),
                pltpu.VMEM((WINDOWS, HEADS, TOKENS, HEAD_DIM), BF16),
                pltpu.VMEM((WINDOWS, WIDTH, TOKENS), BF16),
                pltpu.VMEM((WINDOWS, WIDTH, TOKENS), BF16),
                pltpu.VMEM((WINDOWS, 3 * WIDTH, TOKENS), BF16),
                pltpu.VMEM((2, TOKENS * 8, 128), F32),
                pltpu.VMEM((WINDOWS * CELLS, FEATS), F32),
                pltpu.VMEM((2, lon_size, 8, lanes), F32),
                pltpu.VMEM((2, lon_size // RUN, RUN, 8, lanes), F32),
                pltpu.VMEM((2, RUN, 8, lanes), F32),
                pltpu.VMEM((RUN, 8, lanes), F32),
                pltpu.VMEM((WIN_LON, BAND, TOKENS), BF16),
                pltpu.VMEM((WIN_LON, TOKENS, BAND), BF16),
                pltpu.VMEM((WINDOWS, HEADS, TOKENS, TOKENS), F32),
                pltpu.VMEM((WINDOWS, HEADS, TOKENS, TOKENS), F32),
                pltpu.VMEM((WINDOWS, HEADS, TOKENS, TOKENS), BF16),
                pltpu.VMEM((WINDOWS, HEADS, TOKENS, TOKENS), BF16),
                pltpu.SemaphoreType.DMA((7,)),
                pltpu.SemaphoreType.DMA((2, 4)),
                pltpu.SemaphoreType.DMA((2, 2, 4)),
                pltpu.SemaphoreType.DMA((2, 2, 4)),
                pltpu.SemaphoreType.DMA((2, 4)),
                pltpu.SemaphoreType.DMA((RUN,)),
                pltpu.SemaphoreType.DMA((2, lon_size)),
                pltpu.SemaphoreType.DMA((2, lon_size // RUN)),
                pltpu.SemaphoreType.DMA((2, lon_size // RUN)),
                pltpu.SemaphoreType.DMA((2, lon_size // RUN)),
                pltpu.SemaphoreType.DMA((2, lon_size // RUN)),
                pltpu.SemaphoreType.DMA((2, RUN)),
                pltpu.SemaphoreType.DMA((RUN,)),
                pltpu.SemaphoreType.REGULAR,
            ],
            compiler_params=pltpu.CompilerParams(
                collective_id=0, has_side_effects=True, vmem_limit_bytes=48 << 20
            ),
        )(
            *(
                pltpu.with_memory_space_constraint(x, pltpu.HBM)
                for x in (
                    fields,
                    norm_gain.reshape(1, WIDTH),
                    project_in,
                    project_out,
                    bias_table.reshape(HEADS, pairs_here, 1, OFFSETS),
                    pad_rows,
                    cotangent,
                )
            )
        )
        parts = (out_fields, field_grads, table_grads)
        any_spec = pl.BlockSpec(memory_space=pl.ANY)
        out_fields, field_grads, table_grads = pl.pallas_call(
            place_out,
            out_shape=tuple(jax.ShapeDtypeStruct(x.shape, x.dtype) for x in parts),
            in_specs=[any_spec] * 3,
            out_specs=(hbm_spec,) * 3,
            scratch_shapes=[pltpu.SemaphoreType.DMA((3,))],
            compiler_params=pltpu.CompilerParams(vmem_limit_bytes=1 << 20),
        )(*parts)
        return out_fields, field_grads, table_grads.reshape(bias_table.shape)

    in_specs = (
        P("lat", "lon", None),
        P(),
        P(),
        P(),
        P("lat", None, "lon", None),
        P(),
        P("lat", "lon", None),
    )
    out_specs = (P("lat", "lon", None), P("lat", "lon", None), P("lat", None, "lon", None))
    return jax.shard_map(
        per_device, mesh=mesh, in_specs=in_specs, out_specs=out_specs, check_vma=False
    )
```

```python
import functools

import jax
import jax.numpy as jnp
from jax import lax
from jax.experimental import pallas as pl
from jax.experimental.pallas import tpu as pltpu
from jax.sharding import PartitionSpec as P

WIDTH = 192
HEADS = 6
HEAD_DIM = 32
LEVELS = 2
WIN_LAT = 6
WIN_LON = 12
ZONE = LEVELS * WIN_LAT
CELLS = WIN_LAT * WIN_LON
TOKENS = LEVELS * CELLS
OFFSETS = 23
SLOT = 24
PAIRS = ZONE * ZONE
RIM_R = WIN_LAT // 2
RIM_C = WIN_LON // 2
WINDOWS = 2
COLS = WINDOWS * WIN_LON
FEATS = LEVELS * WIDTH
BAND = 384
BIG = 56
SMALL = 24
RUN = 4
SCALE = HEAD_DIM**-0.5
EPS = 1e-05
MASKED = -1e30
MESH = pl.DeviceIdType.MESH
F32 = jnp.float32
BF16 = jnp.bfloat16


def dot_nn(a, b):
    return lax.dot_general(a, b, (((1,), (0,)), ((), ())), preferred_element_type=F32)


def dot_nt(a, b):
    return lax.dot_general(a, b, (((1,), (1,)), ((), ())), preferred_element_type=F32)


def dot_tn(a, b):
    return lax.dot_general(a, b, (((0,), (0,)), ((), ())), preferred_element_type=F32)


def kernel(
    lat_size,
    lon_size,
    pairs_here,
    fields_hbm,
    gain_hbm,
    win_hbm,
    wout_hbm,
    bias_hbm,
    pad_hbm,
    cot_hbm,
    out_ref,
    grads_ref,
    table_ref,
    f_in,
    c_in,
    w_in,
    wo_in,
    bias_in,
    gain_ref,
    pad_ref,
    raw,
    xw,
    tmp,
    send_big,
    send_small,
    in_big,
    in_small,
    res_big,
    res_small,
    back_big,
    back_small,
    bias_msg,
    bias_recv,
    spread,
    bias_flat,
    bias_full,
    w_t,
    xtok,
    ctok,
    xhat,
    spread_inv,
    proj_t,
    k_nat,
    v_nat,
    gmix_t,
    mixed_t,
    gproj_t,
    gflat,
    cells,
    table_msg,
    table_mid,
    table_out,
    table_recv,
    spreader,
    gatherer,
    score_buf,
    gw_buf,
    p_low,
    d_low,
    load_sem,
    halo_send,
    halo_recv,
    back_send,
    back_recv,
    bias_send,
    bias_rsem,
    pass_send,
    pass_recv,
    table_xsend,
    table_xrecv,
    table_send,
    table_rsem,
    far_send,
    ready_sem,
    alive_sem,
):
    lat = lax.axis_index("lat")
    lon = lax.axis_index("lon")
    up = lax.rem(lat + lat_size - 1, lat_size)
    dn = lax.rem(lat + 1, lat_size)
    lf = lax.rem(lon + lon_size - 1, lon_size)
    rt = lax.rem(lon + 1, lon_size)
    group = lat_size // 2
    place = lax.rem(lat, group)
    is_first = place == 0
    is_last = place == group - 1
    before_last = place == group - 2
    one_if_last = jnp.where(is_last, 1, 0)
    one_if_first = jnp.where(is_first, 1, 0)
    steps = lon_size // RUN
    column = lon // RUN
    inside = lax.rem(lon, RUN)
    at_start = inside == 0
    at_end = inside == RUN - 1
    below = jnp.where(is_last, dn, lat)
    above = jnp.where(is_first, lat, up)

    barrier = pltpu.get_barrier_semaphore()

    def signal(dev):
        pl.semaphore_signal(barrier, inc=1, device_id=dev, device_id_type=MESH)

    def greet_seam(s, carry):
        signal((up, lax.rem(lon + s, lon_size)))
        return carry

    def run_peer(s):
        return column * RUN + lax.rem(inside + s, RUN)

    def column_peer(s):
        return lax.rem(column + s, steps)

    @pl.when(is_first)
    def _():
        lax.fori_loop(0, lon_size, greet_seam, 0)

    @pl.when(jnp.logical_not(is_first))
    def _():
        signal((up, lon))
        signal((up, lf))

    @pl.when(jnp.logical_not(is_last))
    def _():
        signal((dn, lon))
        for s in range(1, RUN):
            signal((lat, run_peer(s)))
        for s in range(1, steps):
            signal((lat, column_peer(s) * RUN + inside))

    @pl.when(jnp.logical_not(is_last) & at_start)
    def _():
        signal((lat, lf))

    @pl.when(jnp.logical_not(is_last) & at_end)
    def _():
        signal((lat, rt))

    @pl.when(jnp.logical_not(is_last | before_last))
    def _():
        signal((dn, rt))

    loads = [
        pltpu.make_async_copy(src, dst, load_sem.at[n])
        for n, (src, dst) in enumerate(
            (
                (bias_hbm, bias_in),
                (fields_hbm, f_in),
                (cot_hbm, c_in),
                (win_hbm, w_in),
                (wout_hbm, wo_in),
                (gain_hbm, gain_ref),
                (pad_hbm, pad_ref),
            )
        )
    ]
    for load in loads:
        load.start()

    def remote(src, dst, send, recv, dev):
        return pltpu.make_async_remote_copy(
            src_ref=src,
            dst_ref=dst,
            send_sem=send,
            recv_sem=recv,
            device_id=dev,
            device_id_type=MESH,
        )

    def big_last(kind):
        return remote(
            send_big.at[kind, 0],
            in_big.at[kind, 1, 0],
            halo_send.at[kind, 0],
            halo_recv.at[kind, 1, 0],
            (dn, lon),
        )

    def big_up(kind):
        return remote(
            send_big.at[kind, 1],
            in_big.at[kind, 0, 1],
            halo_send.at[kind, 1],
            halo_recv.at[kind, 0, 0],
            (up, lon),
        )

    def small_low(kind):
        return remote(
            send_small.at[kind, 0],
            in_small.at[kind, one_if_last, 0],
            halo_send.at[kind, 2],
            halo_recv.at[kind, one_if_last, 1],
            (below, lf),
        )

    def small_top(kind):
        return remote(
            send_small.at[kind, 1],
            in_small.at[kind, one_if_first, 1],
            halo_send.at[kind, 3],
            halo_recv.at[kind, one_if_first, 2],
            (above, lf),
        )

    def wait_halo(kind, slot):
        remote(
            send_big.at[kind, 0],
            in_big.at[kind, slot, 1 - slot],
            halo_send.at[kind, 0],
            halo_recv.at[kind, slot, 0],
            (dn, lon),
        ).wait_recv()
        for half in range(2):
            remote(
                send_small.at[kind, half],
                in_small.at[kind, slot, half],
                halo_send.at[kind, 2],
                halo_recv.at[kind, slot, 1 + half],
                (dn, lon),
            ).wait_recv()

    def pack_in(src, kind):
        for r in range(WIN_LAT):
            raw[r * COLS : (r + 1) * COLS, :] = src[r].astype(F32)
        for half, first in ((0, RIM_R), (1, 0)):
            base, side = half * 88, 64 + half * 88
            for r in range(RIM_R):
                row = (first + r) * COLS
                tmp[base + r * 12 : base + r * 12 + 12, :] = raw[row + 6 : row + 18, :]
                tmp[base + 36 + r * 6 : base + 42 + r * 6, :] = raw[row + 18 : row + 24, :]
                tmp[side + r * 6 : side + 6 + r * 6, :] = raw[row : row + 6, :]
            piece = tmp[base : base + BIG, :].astype(BF16)
            send_big[kind, half] = piece
            in_big[kind, half, half] = piece
            send_small[kind, half] = tmp[side : side + SMALL, :].astype(BF16)

    def unpack_in(kind, slot):
        for half in range(2):
            base, side = half * 88, 64 + half * 88
            tmp[base : base + BIG, :] = in_big[kind, slot, half].astype(F32)
            tmp[side : side + SMALL, :] = in_small[kind, slot, half].astype(F32)
            xw[36 * half : 36 * half + 36, :] = tmp[base : base + 36, :]
            for r in range(RIM_R):
                row = CELLS + (RIM_R * half + r) * 12
                xw[row : row + 6, :] = tmp[base + 36 + r * 6 : base + 42 + r * 6, :]
                xw[row + 6 : row + 12, :] = tmp[side + r * 6 : side + 6 + r * 6, :]

    tmp[...] = jnp.zeros_like(tmp)
    bias_msg[...] = jnp.zeros_like(bias_msg)
    loads[0].wait()
    for r in range(pairs_here):
        for h in range(HEADS):
            bias_msg[h : h + 1, r * SLOT : r * SLOT + OFFSETS] = bias_in[h, r]
    bias_recv[0, lon] = bias_msg[...]
    around = RUN + steps - 2 + jnp.where(at_start | at_end, 1, 0)
    greetings = jnp.where(is_last, lon_size + 1, around + jnp.where(is_first, 2, 4))
    pl.semaphore_wait(barrier, greetings)

    @pl.when(before_last)
    def _():
        pl.semaphore_signal(ready_sem, inc=1, device_id=(dn, rt), device_id_type=MESH)

    def bias_copy(s):
        return remote(
            bias_msg,
            bias_recv.at[one_if_last, lon],
            bias_send.at[s],
            bias_rsem.at[one_if_last, lon],
            (below, run_peer(s)),
        )

    def bias_arrival(slot, s):
        source = run_peer(s)
        return remote(
            bias_msg,
            bias_recv.at[slot, source],
            bias_send.at[s],
            bias_rsem.at[slot, source],
            (dn, lon),
        )

    def bias_pass(slot, s):
        mine = bias_recv.at[slot, pl.ds(column * RUN, RUN)]
        return remote(
            mine,
            mine,
            pass_send.at[slot, s],
            pass_recv.at[slot, column],
            (lat, column_peer(s) * RUN + inside),
        )

    def bias_passed(slot, s):
        source = column_peer(s)
        theirs = bias_recv.at[slot, pl.ds(source * RUN, RUN)]
        return remote(
            theirs, theirs, pass_send.at[slot, s], pass_recv.at[slot, source], (dn, lon)
        )

    def send_bias(s, carry):
        bias_copy(s).start()
        return carry

    def send_halo(kind):
        @pl.when(is_last)
        def _():
            big_last(kind).start()

        small_low(kind).start()

        @pl.when(jnp.logical_not(is_first))
        def _():
            big_up(kind).start()

        @pl.when(jnp.logical_not(is_last))
        def _():
            small_top(kind).start()

    lax.fori_loop(1 - one_if_last, RUN, send_bias, 0)
    loads[1].wait()
    pack_in(f_in, 0)
    send_halo(0)
    loads[2].wait()
    pack_in(c_in, 1)
    send_halo(1)

    def say_alive(j, carry):
        pl.semaphore_signal(alive_sem, inc=1, device_id=(dn, j), device_id_type=MESH)
        return carry

    @pl.when(is_last)
    def _():
        lax.fori_loop(0, lon_size, say_alive, 0)
        pl.semaphore_wait(ready_sem, 1)
        for kind in range(2):
            small_top(kind).start()

    gflat[...] = jnp.zeros_like(gflat)
    table_msg[...] = jnp.zeros_like(table_msg)
    spread[...] = jnp.zeros_like(spread)

    def make_selectors(b, carry):
        lane = lax.broadcasted_iota(jnp.int32, (BAND, TOKENS), 0)
        query = lax.broadcasted_iota(jnp.int32, (BAND, TOKENS), 1)
        picked = (query // WIN_LON) * SLOT + query % WIN_LON + WIN_LON - 1 - b
        spreader[b] = (lane == picked).astype(F32).astype(BF16)
        lane = lax.broadcasted_iota(jnp.int32, (TOKENS, BAND), 1)
        query = lax.broadcasted_iota(jnp.int32, (TOKENS, BAND), 0)
        picked = (query // WIN_LON) * SLOT + query % WIN_LON + WIN_LON - 1 - b
        gatherer[b] = (lane == picked).astype(F32).astype(BF16)
        return carry

    lax.fori_loop(0, WIN_LON, make_selectors, 0)
    loads[3].wait()
    loads[4].wait()
    loads[5].wait()
    loads[6].wait()
    w_t[...] = w_in[...].astype(F32).T.astype(BF16)
    total_rows = lat_size * WIN_LAT
    key_band = (lax.broadcasted_iota(jnp.int32, (TOKENS, TOKENS), 0) // WIN_LON) % WIN_LAT
    query_band = (lax.broadcasted_iota(jnp.int32, (TOKENS, TOKENS), 1) // WIN_LON) % WIN_LAT

    def back_copy_big(kind, slot):
        return remote(
            res_big.at[kind, slot, 1 - slot],
            back_big.at[kind, 1 - slot],
            back_send.at[kind, slot, 0],
            back_recv.at[kind, 1 - slot],
            (jnp.where(slot == 0, dn, up), lon),
        )

    def back_copy_small(kind, slot, half):
        owner = lax.rem(lat + half - slot + lat_size, lat_size)
        return remote(
            res_small.at[kind, slot, half],
            back_small.at[kind, half],
            back_send.at[kind, slot, 1 + half],
            back_recv.at[kind, 2 + half],
            (owner, rt),
        )

    def give_back(kind, slot, tokens):
        for w in range(WINDOWS):
            cells[w * CELLS : (w + 1) * CELLS, 0:WIDTH] = tokens[w][0:CELLS]
            cells[w * CELLS : (w + 1) * CELLS, WIDTH:] = tokens[w][CELLS:]
        for half in range(2):
            base, side = half * 88, 64 + half * 88
            tmp[base : base + 36, :] = cells[36 * half : 36 * half + 36, :]
            for r in range(RIM_R):
                row = CELLS + (RIM_R * half + r) * 12
                tmp[base + 36 + r * 6 : base + 42 + r * 6, :] = cells[row : row + 6, :]
                tmp[side + r * 6 : side + 6 + r * 6, :] = cells[row + 6 : row + 12, :]
            res_big[kind, slot, half] = tmp[base : base + BIG, :].astype(BF16)
            res_small[kind, slot, half] = tmp[side : side + SMALL, :].astype(BF16)
        for half in range(2):
            back_copy_small(kind, slot, half).start()
        back_copy_big(kind, slot).start()
        back_big[kind, slot] = res_big[kind, slot, slot]

    def table_pass(slot, s):
        target = column_peer(s)
        return remote(
            table_msg.at[slot, pl.ds(target * RUN, RUN)],
            table_mid.at[slot, column],
            table_xsend.at[slot, s],
            table_xrecv.at[slot, column],
            (lat, target * RUN + inside),
        )

    def table_passed(slot, s):
        source = column_peer(s)
        return remote(
            table_msg.at[slot, pl.ds(source * RUN, RUN)],
            table_mid.at[slot, source],
            table_xsend.at[slot, s],
            table_xrecv.at[slot, source],
            (lat, lon),
        )

    def table_copy(slot, s):
        peer = lax.rem(inside + s, RUN)
        return remote(
            table_out.at[slot, peer],
            table_recv.at[inside],
            table_send.at[slot, s],
            table_rsem.at[inside],
            (lat, run_peer(s)),
        )

    def table_arrival(s):
        source = lax.rem(inside + s, RUN)
        return remote(
            table_out.at[0, source],
            table_recv.at[source],
            table_send.at[0, s],
            table_rsem.at[source],
            (lat, run_peer(s)),
        )

    def table_far(j):
        return remote(
            table_msg.at[1, j],
            table_recv.at[lon],
            far_send.at[j],
            table_rsem.at[lon],
            (up, j),
        )

    def near_table():
        summed = table_msg[0, pl.ds(column * RUN, RUN)]
        for s in range(1, steps):
            table_passed(0, s).wait_recv()
        for s in range(1, steps):
            summed = summed + table_mid[0, column_peer(s)]
        table_out[0] = summed

        def send_table(s, inner):
            table_copy(0, s).start()
            return inner

        lax.fori_loop(1, RUN, send_table, 0)
        table_recv[inside] = table_out[0, inside]

    def window_row(slot, carry):
        def wait_bias(s, inner):
            bias_arrival(slot, s).wait_recv()
            return inner

        lax.fori_loop(1 - slot, RUN, wait_bias, 0)
        for s in range(1, steps):
            bias_pass(slot, s).start()
        gain = gain_ref[...]
        wait_halo(0, slot)
        unpack_in(0, slot)
        for w in range(WINDOWS):
            block = xw[w * CELLS : (w + 1) * CELLS, :]
            x = jnp.concatenate([block[:, :WIDTH], block[:, WIDTH:]], axis=0)
            xtok[w] = x
            center = x - jnp.mean(x, axis=1, keepdims=True)
            inverse = lax.rsqrt(jnp.mean(center * center, axis=1, keepdims=True) + EPS)
            normed = center * inverse
            xhat[w] = normed
            spread_inv[w] = inverse
            x_n = (normed * gain).astype(BF16)
            proj_t[w] = dot_nt(w_t[...], x_n).astype(BF16)
            kv = dot_nn(x_n, w_in[:, WIDTH:]).astype(BF16)
            for h in range(HEADS):
                k_nat[w, h] = kv[:, h * HEAD_DIM : (h + 1) * HEAD_DIM]
                v_nat[w, h] = kv[:, WIDTH + h * HEAD_DIM : WIDTH + (h + 1) * HEAD_DIM]
        wait_halo(1, slot)
        unpack_in(1, slot)
        for w in range(WINDOWS):
            block = xw[w * CELLS : (w + 1) * CELLS, :]
            c = jnp.concatenate([block[:, :WIDTH], block[:, WIDTH:]], axis=0)
            ctok[w] = c
            gmix_t[w] = dot_nt(wo_in[...], c.astype(BF16)).astype(BF16)

        def rows_of(part, h):
            return pl.ds(part * WIDTH + h * HEAD_DIM, HEAD_DIM)

        for h in range(HEADS):
            for w in range(WINDOWS):
                score_buf[w, h] = dot_nn(k_nat[w, h], proj_t[w, rows_of(0, h), :]) * SCALE
                gw_buf[w, h] = dot_nn(v_nat[w, h], gmix_t[w, rows_of(0, h), :])
        first_row = jnp.where(slot == 0, lat, up) * WIN_LAT + RIM_R
        key_row = lax.rem(first_row + key_band, total_rows)
        query_row = lax.rem(first_row + query_band, total_rows)
        real = jnp.zeros((TOKENS, TOKENS), jnp.int32)
        for a in range(WIN_LAT):
            real = jnp.where(key_band == a, pad_ref[lax.rem(first_row + a, total_rows)], real)
        allowed = (jnp.abs(query_row - key_row) < WIN_LAT) & (real == 1)

        @pl.when(slot == 1)
        def _():
            near_table()

        for s in range(1, steps):
            bias_passed(slot, s).wait_recv()
        for p in range(PAIRS):
            owner, r = p // pairs_here, p % pairs_here
            zq, zt = p // ZONE, p % ZONE
            spread[zt * 8 : zt * 8 + 8, zq * SLOT : (zq + 1) * SLOT] = bias_recv[
                slot, owner, :, r * SLOT : (r + 1) * SLOT
            ]
        table = spread[...]
        high = table.astype(BF16)
        rest = table - high.astype(F32)
        middle = rest.astype(BF16)
        low = (rest - middle.astype(F32)).astype(BF16)
        rows = ZONE * 8
        stacked = jnp.concatenate([high, middle, low], axis=0)
        for b in range(WIN_LON):
            three = dot_nn(stacked, spreader[b])
            wide = three[0:rows] + (three[rows : 2 * rows] + three[2 * rows :])
            for zt in range(ZONE):
                row = (zt * WIN_LON + b) * 8
                bias_flat[0, row : row + 8, :] = wide[zt * 8 : zt * 8 + 8, 0:128]
                bias_flat[1, row : row + 8, 0 : TOKENS - 128] = wide[
                    zt * 8 : zt * 8 + 8, 128:TOKENS
                ]
        for h in range(HEADS):
            left = bias_flat[0, pl.ds(h, TOKENS, stride=8), :]
            right = bias_flat[1, pl.ds(h, TOKENS, stride=8), :]
            whole = jnp.concatenate([left, right[:, 0 : TOKENS - 128]], axis=1)
            bias_full[h] = jnp.where(allowed, whole, MASKED)

        for h in range(HEADS):
            summed = None
            for w in range(WINDOWS):
                scores = score_buf[w, h] + bias_full[h]
                raised = jnp.exp(scores - jnp.max(scores, axis=0, keepdims=True))
                weights = raised * (1.0 / jnp.sum(raised, axis=0, keepdims=True))
                p_low[w, h] = weights.astype(BF16)
                grad_w = gw_buf[w, h]
                grad_s = weights * (grad_w - jnp.sum(weights * grad_w, axis=0, keepdims=True))
                d_low[w, h] = grad_s.astype(BF16)
                summed = grad_s if summed is None else summed + grad_s
            gflat[0, pl.ds(h, TOKENS, stride=8), :] = summed[:, 0:128]
            gflat[1, pl.ds(h, TOKENS, stride=8), 0 : TOKENS - 128] = summed[:, 128:TOKENS]
        for h in range(HEADS):
            for w in range(WINDOWS):
                q_t = proj_t[w, rows_of(0, h), :]
                g_t = gmix_t[w, rows_of(0, h), :]
                weights_low = p_low[w, h]
                grad_low = d_low[w, h]
                mixed_t[w, rows_of(0, h), :] = dot_nn(
                    proj_t[w, rows_of(2, h), :], weights_low
                ).astype(BF16)
                gproj_t[w, rows_of(0, h), :] = (
                    dot_nn(proj_t[w, rows_of(1, h), :], grad_low) * SCALE
                ).astype(BF16)
                gproj_t[w, rows_of(1, h), :] = (dot_nt(q_t, grad_low) * SCALE).astype(BF16)
                gproj_t[w, rows_of(2, h), :] = dot_nt(g_t, weights_low).astype(BF16)

        give_back(
            0, slot, [xtok[w] + dot_tn(mixed_t[w], wo_in[...]) for w in range(WINDOWS)]
        )
        grads = []
        for w in range(WINDOWS):
            scaled = dot_tn(gproj_t[w], w_t[...]) * gain
            normed = xhat[w]
            centered = (
                scaled
                - jnp.mean(scaled, axis=1, keepdims=True)
                - normed * jnp.mean(scaled * normed, axis=1, keepdims=True)
            )
            grads.append(ctok[w] + spread_inv[w] * centered)
        give_back(1, slot, grads)

        total = jnp.zeros((ZONE * 8, BAND), F32)
        for b in range(WIN_LON):
            picked_rows = []
            for zt in range(ZONE):
                row = (zt * WIN_LON + b) * 8
                picked_rows.append(
                    jnp.concatenate(
                        [
                            gflat[0, row : row + 8, :],
                            gflat[1, row : row + 8, 0 : TOKENS - 128],
                        ],
                        axis=1,
                    )
                )
            part = jnp.concatenate(picked_rows, axis=0).astype(BF16)
            total = total + dot_nn(part, gatherer[b])
        spread[...] = total
        for p in range(PAIRS):
            owner, r = p // pairs_here, p % pairs_here
            zq, zt = p // ZONE, p % ZONE
            table_msg[slot, owner, :, r * SLOT : (r + 1) * SLOT] = spread[
                zt * 8 : zt * 8 + 8, zq * SLOT : (zq + 1) * SLOT
            ]

        @pl.when(slot == 0)
        def _():
            for s in range(1, steps):
                table_pass(0, s).start()

        @pl.when(slot == 1)
        def _():
            pl.semaphore_wait(alive_sem, lon_size)

            def send_far(j, inner):
                table_far(j).start()
                return inner

            lax.fori_loop(0, lon_size, send_far, 0)

        return carry

    rows_here = 1 + one_if_first - one_if_last
    lax.fori_loop(0, rows_here, window_row, 0)

    def take_back(kind, dst):
        def arrived_big(half):
            remote(
                res_big.at[kind, 0, half],
                back_big.at[kind, half],
                back_send.at[kind, 0, 0],
                back_recv.at[kind, half],
                (dn, lon),
            ).wait_recv()

        @pl.when(is_last)
        def _():
            arrived_big(0)

        @pl.when(jnp.logical_not(is_first))
        def _():
            arrived_big(1)

        for half in range(2):
            remote(
                res_small.at[kind, 0, half],
                back_small.at[kind, half],
                back_send.at[kind, 0, 1],
                back_recv.at[kind, 2 + half],
                (dn, rt),
            ).wait_recv()
        for half, first in ((0, RIM_R), (1, 0)):
            base, side = half * 88, 64 + half * 88
            tmp[base : base + BIG, :] = back_big[kind, half].astype(F32)
            tmp[side : side + SMALL, :] = back_small[kind, half].astype(F32)
            for r in range(RIM_R):
                row = (first + r) * COLS
                raw[row + 6 : row + 18, :] = tmp[base + r * 12 : base + r * 12 + 12, :]
                raw[row + 18 : row + 24, :] = tmp[base + 36 + r * 6 : base + 42 + r * 6, :]
                raw[row : row + 6, :] = tmp[side + r * 6 : side + 6 + r * 6, :]
        for r in range(WIN_LAT):
            dst[r] = raw[r * COLS : (r + 1) * COLS, :].astype(BF16)

    @pl.when(jnp.logical_not(is_first | is_last))
    def _():
        near_table()

    take_back(0, out_ref)
    take_back(1, grads_ref)

    def wait_table(s, carry):
        table_arrival(s).wait_recv()
        return carry

    def wait_far(j, carry):
        remote(
            table_msg.at[1, j],
            table_recv.at[j],
            far_send.at[j],
            table_rsem.at[j],
            (up, j),
        ).wait_recv()
        return carry

    @pl.when(is_last)
    def _():
        lax.fori_loop(0, lon_size, wait_far, 0)

    @pl.when(jnp.logical_not(is_last))
    def _():
        lax.fori_loop(1, RUN, wait_table, 0)
        table_recv[RUN:lon_size] = jnp.zeros_like(table_recv[RUN:lon_size])

    added = table_recv[0]
    for j in range(1, lon_size):
        added = added + table_recv[j]
    for r in range(pairs_here):
        piece = added[:, r * SLOT : r * SLOT + OFFSETS]
        for h in range(HEADS):
            table_ref[h, r] = piece[h : h + 1, :]

    for kind in range(2):

        @pl.when(is_last)
        def _():
            big_last(kind).wait_send()

        @pl.when(jnp.logical_not(is_first))
        def _():
            big_up(kind).wait_send()

        small_low(kind).wait_send()
        small_top(kind).wait_send()

    def drain_bias(s, carry):
        bias_copy(s).wait_send()
        return carry

    lax.fori_loop(1 - one_if_last, RUN, drain_bias, 0)

    def drain_row(slot, carry):
        for kind in range(2):
            back_copy_big(kind, slot).wait_send()
            for half in range(2):
                back_copy_small(kind, slot, half).wait_send()

        for s in range(1, steps):
            bias_pass(slot, s).wait_send()

        @pl.when(slot == 0)
        def _():
            for s in range(1, steps):
                table_pass(0, s).wait_send()
            for s in range(1, RUN):
                table_copy(0, s).wait_send()

        @pl.when(slot == 1)
        def _():
            def drain_far(j, inner):
                table_far(j).wait_send()
                return inner

            lax.fori_loop(0, lon_size, drain_far, 0)

        return carry

    lax.fori_loop(0, rows_here, drain_row, 0)


def place_out(*refs):
    sources, targets, sem = refs[:3], refs[3:6], refs[6]
    copies = [
        pltpu.make_async_copy(src, dst, sem.at[n])
        for n, (src, dst) in enumerate(zip(sources, targets))
    ]
    for copy in copies:
        copy.start()
    for copy in copies:
        copy.wait()


def solution(mesh):
    lat_size, lon_size = mesh.shape["lat"], mesh.shape["lon"]
    pairs_here = PAIRS // lon_size
    lanes = -(-pairs_here * SLOT // 128) * 128

    def per_device(fields, norm_gain, project_in, project_out, bias_table, pad_rows, cotangent):
        hbm_spec = pl.BlockSpec(memory_space=pltpu.HBM)
        vmem_spec = pl.BlockSpec(memory_space=pltpu.VMEM)
        out_fields, field_grads, table_grads = pl.pallas_call(
            functools.partial(kernel, lat_size, lon_size, pairs_here),
            out_shape=(
                jax.ShapeDtypeStruct(fields.shape, BF16),
                jax.ShapeDtypeStruct(fields.shape, BF16),
                jax.ShapeDtypeStruct((HEADS, pairs_here, 1, OFFSETS), F32),
            ),
            in_specs=[hbm_spec] * 7,
            out_specs=(vmem_spec, vmem_spec, vmem_spec),
            scratch_shapes=[
                pltpu.VMEM(fields.shape, BF16),
                pltpu.VMEM(fields.shape, BF16),
                pltpu.VMEM(project_in.shape, BF16),
                pltpu.VMEM(project_out.shape, BF16),
                pltpu.VMEM((HEADS, pairs_here, 1, OFFSETS), F32),
                pltpu.VMEM((1, WIDTH), F32),
                pltpu.SMEM(pad_rows.shape, jnp.int32),
                pltpu.VMEM((WIN_LAT * COLS, FEATS), F32),
                pltpu.VMEM((WINDOWS * CELLS, FEATS), F32),
                pltpu.VMEM((176, FEATS), F32),
                pltpu.VMEM((2, 2, BIG, FEATS), BF16),
                pltpu.VMEM((2, 2, SMALL, FEATS), BF16),
                pltpu.VMEM((2, 2, 2, BIG, FEATS), BF16),
                pltpu.VMEM((2, 2, 2, SMALL, FEATS), BF16),
                pltpu.VMEM((2, 2, 2, BIG, FEATS), BF16),
                pltpu.VMEM((2, 2, 2, SMALL, FEATS), BF16),
                pltpu.VMEM((2, 2, BIG, FEATS), BF16),
                pltpu.VMEM((2, 2, SMALL, FEATS), BF16),
                pltpu.VMEM((8, lanes), F32),
                pltpu.VMEM((2, lon_size, 8, lanes), F32),
                pltpu.VMEM((ZONE * 8, BAND), F32),
                pltpu.VMEM((2, TOKENS * 8, 128), F32),
                pltpu.VMEM((HEADS, TOKENS, TOKENS), F32),
                pltpu.VMEM((3 * WIDTH, WIDTH), BF16),
                pltpu.VMEM((WINDOWS, TOKENS, WIDTH), F32),
                pltpu.VMEM((WINDOWS, TOKENS, WIDTH), F32),
                pltpu.VMEM((WINDOWS, TOKENS, WIDTH), F32),
                pltpu.VMEM((WINDOWS, TOKENS, 1), F32),
                pltpu.VMEM((WINDOWS, 3 * WIDTH, TOKENS), BF16),
                pltpu.VMEM((WINDOWS, HEADS, TOKENS, HEAD_DIM), BF16),
                pltpu.VMEM((WINDOWS, HEADS, TOKENS, HEAD_DIM), BF16),
                pltpu.VMEM((WINDOWS, WIDTH, TOKENS), BF16),
                pltpu.VMEM((WINDOWS, WIDTH, TOKENS), BF16),
                pltpu.VMEM((WINDOWS, 3 * WIDTH, TOKENS), BF16),
                pltpu.VMEM((2, TOKENS * 8, 128), F32),
                pltpu.VMEM((WINDOWS * CELLS, FEATS), F32),
                pltpu.VMEM((2, lon_size, 8, lanes), F32),
                pltpu.VMEM((2, lon_size // RUN, RUN, 8, lanes), F32),
                pltpu.VMEM((2, RUN, 8, lanes), F32),
                pltpu.VMEM((lon_size, 8, lanes), F32),
                pltpu.VMEM((WIN_LON, BAND, TOKENS), BF16),
                pltpu.VMEM((WIN_LON, TOKENS, BAND), BF16),
                pltpu.VMEM((WINDOWS, HEADS, TOKENS, TOKENS), F32),
                pltpu.VMEM((WINDOWS, HEADS, TOKENS, TOKENS), F32),
                pltpu.VMEM((WINDOWS, HEADS, TOKENS, TOKENS), BF16),
                pltpu.VMEM((WINDOWS, HEADS, TOKENS, TOKENS), BF16),
                pltpu.SemaphoreType.DMA((7,)),
                pltpu.SemaphoreType.DMA((2, 4)),
                pltpu.SemaphoreType.DMA((2, 2, 3)),
                pltpu.SemaphoreType.DMA((2, 2, 3)),
                pltpu.SemaphoreType.DMA((2, 4)),
                pltpu.SemaphoreType.DMA((RUN,)),
                pltpu.SemaphoreType.DMA((2, lon_size)),
                pltpu.SemaphoreType.DMA((2, lon_size // RUN)),
                pltpu.SemaphoreType.DMA((2, lon_size // RUN)),
                pltpu.SemaphoreType.DMA((2, lon_size // RUN)),
                pltpu.SemaphoreType.DMA((2, lon_size // RUN)),
                pltpu.SemaphoreType.DMA((2, RUN)),
                pltpu.SemaphoreType.DMA((lon_size,)),
                pltpu.SemaphoreType.DMA((lon_size,)),
                pltpu.SemaphoreType.REGULAR,
                pltpu.SemaphoreType.REGULAR,
            ],
            compiler_params=pltpu.CompilerParams(
                collective_id=0, has_side_effects=True, vmem_limit_bytes=48 << 20
            ),
        )(
            *(
                pltpu.with_memory_space_constraint(x, pltpu.HBM)
                for x in (
                    fields,
                    norm_gain.reshape(1, WIDTH),
                    project_in,
                    project_out,
                    bias_table.reshape(HEADS, pairs_here, 1, OFFSETS),
                    pad_rows,
                    cotangent,
                )
            )
        )
        parts = (out_fields, field_grads, table_grads)
        any_spec = pl.BlockSpec(memory_space=pl.ANY)
        out_fields, field_grads, table_grads = pl.pallas_call(
            place_out,
            out_shape=tuple(jax.ShapeDtypeStruct(x.shape, x.dtype) for x in parts),
            in_specs=[any_spec] * 3,
            out_specs=(hbm_spec,) * 3,
            scratch_shapes=[pltpu.SemaphoreType.DMA((3,))],
            compiler_params=pltpu.CompilerParams(vmem_limit_bytes=1 << 20),
        )(*parts)
        return out_fields, field_grads, table_grads.reshape(bias_table.shape)

    in_specs = (
        P("lat", "lon", None),
        P(),
        P(),
        P(),
        P("lat", None, "lon", None),
        P(),
        P("lat", "lon", None),
    )
    out_specs = (P("lat", "lon", None), P("lat", "lon", None), P("lat", None, "lon", None))
    return jax.shard_map(
        per_device, mesh=mesh, in_specs=in_specs, out_specs=out_specs, check_vma=False
    )
```

```python
import functools

import jax
import jax.numpy as jnp
from jax import lax
from jax.experimental import pallas as pl
from jax.experimental.pallas import tpu as pltpu
from jax.sharding import PartitionSpec as P

WIDTH = 192
HEADS = 6
HEAD_DIM = 32
LEVELS = 2
WIN_LAT = 6
WIN_LON = 12
ZONE = LEVELS * WIN_LAT
CELLS = WIN_LAT * WIN_LON
TOKENS = LEVELS * CELLS
OFFSETS = 23
SLOT = 24
PAIRS = ZONE * ZONE
RIM_R = WIN_LAT // 2
RIM_C = WIN_LON // 2
WINDOWS = 2
COLS = WINDOWS * WIN_LON
FEATS = LEVELS * WIDTH
BAND = 384
BIG = 56
SMALL = 24
RUN = 4
SCALE = HEAD_DIM**-0.5
EPS = 1e-05
MASKED = -1e30
MESH = pl.DeviceIdType.MESH
F32 = jnp.float32
BF16 = jnp.bfloat16


def dot_nn(a, b):
    return lax.dot_general(a, b, (((1,), (0,)), ((), ())), preferred_element_type=F32)


def dot_nt(a, b):
    return lax.dot_general(a, b, (((1,), (1,)), ((), ())), preferred_element_type=F32)


def dot_tn(a, b):
    return lax.dot_general(a, b, (((0,), (0,)), ((), ())), preferred_element_type=F32)


def kernel(
    lat_size,
    lon_size,
    pairs_here,
    fields_hbm,
    gain_hbm,
    win_hbm,
    wout_hbm,
    bias_hbm,
    pad_hbm,
    cot_hbm,
    out_ref,
    grads_ref,
    table_ref,
    f_in,
    c_in,
    w_in,
    wo_in,
    bias_in,
    gain_ref,
    pad_ref,
    raw,
    xw,
    tmp,
    send_big,
    send_small,
    in_big,
    in_small,
    res_big,
    res_small,
    back_big,
    back_small,
    bias_msg,
    bias_recv,
    spread,
    bias_flat,
    bias_full,
    w_t,
    xtok,
    ctok,
    xhat,
    spread_inv,
    proj_t,
    k_nat,
    v_nat,
    gmix_t,
    mixed_t,
    gproj_t,
    gflat,
    cells,
    table_msg,
    table_mid,
    table_out,
    far_msg,
    far_recv,
    table_recv,
    spreader,
    gatherer,
    score_buf,
    gw_buf,
    p_low,
    d_low,
    load_sem,
    halo_send,
    halo_recv,
    back_send,
    back_recv,
    bias_send,
    bias_rsem,
    pass_send,
    pass_recv,
    table_xsend,
    table_xrecv,
    table_send,
    table_rsem,
    far_send,
    ready_sem,
    alive_sem,
):
    lat = lax.axis_index("lat")
    lon = lax.axis_index("lon")
    up = lax.rem(lat + lat_size - 1, lat_size)
    dn = lax.rem(lat + 1, lat_size)
    lf = lax.rem(lon + lon_size - 1, lon_size)
    rt = lax.rem(lon + 1, lon_size)
    group = lat_size // 2
    place = lax.rem(lat, group)
    is_first = place == 0
    is_last = place == group - 1
    before_last = place == group - 2
    one_if_last = jnp.where(is_last, 1, 0)
    one_if_first = jnp.where(is_first, 1, 0)
    steps = lon_size // RUN
    column = lon // RUN
    inside = lax.rem(lon, RUN)
    at_start = inside == 0
    at_end = inside == RUN - 1
    below = jnp.where(is_last, dn, lat)
    above = jnp.where(is_first, lat, up)

    barrier = pltpu.get_barrier_semaphore()

    def signal(dev):
        pl.semaphore_signal(barrier, inc=1, device_id=dev, device_id_type=MESH)

    def greet_seam(s, carry):
        signal((up, lax.rem(lon + s, lon_size)))
        return carry

    def run_peer(s):
        return column * RUN + lax.rem(inside + s, RUN)

    def column_peer(s):
        return lax.rem(column + s, steps)

    @pl.when(is_first)
    def _():
        lax.fori_loop(0, lon_size, greet_seam, 0)

    @pl.when(jnp.logical_not(is_first))
    def _():
        signal((up, lon))
        signal((up, lf))

    @pl.when(jnp.logical_not(is_last))
    def _():
        signal((dn, lon))
        for s in range(1, RUN):
            signal((lat, run_peer(s)))
        for s in range(1, steps):
            signal((lat, column_peer(s) * RUN + inside))

    @pl.when(jnp.logical_not(is_last) & at_start)
    def _():
        signal((lat, lf))

    @pl.when(jnp.logical_not(is_last) & at_end)
    def _():
        signal((lat, rt))

    @pl.when(jnp.logical_not(is_last | before_last))
    def _():
        signal((dn, rt))

    loads = [
        pltpu.make_async_copy(src, dst, load_sem.at[n])
        for n, (src, dst) in enumerate(
            (
                (bias_hbm, bias_in),
                (fields_hbm, f_in),
                (cot_hbm, c_in),
                (win_hbm, w_in),
                (wout_hbm, wo_in),
                (gain_hbm, gain_ref),
                (pad_hbm, pad_ref),
            )
        )
    ]
    for load in loads:
        load.start()

    def remote(src, dst, send, recv, dev):
        return pltpu.make_async_remote_copy(
            src_ref=src,
            dst_ref=dst,
            send_sem=send,
            recv_sem=recv,
            device_id=dev,
            device_id_type=MESH,
        )

    def big_last(kind):
        return remote(
            send_big.at[kind, 0],
            in_big.at[kind, 1, 0],
            halo_send.at[kind, 0],
            halo_recv.at[kind, 1, 0],
            (dn, lon),
        )

    def big_up(kind):
        return remote(
            send_big.at[kind, 1],
            in_big.at[kind, 0, 1],
            halo_send.at[kind, 1],
            halo_recv.at[kind, 0, 0],
            (up, lon),
        )

    def small_low(kind):
        return remote(
            send_small.at[kind, 0],
            in_small.at[kind, one_if_last, 0],
            halo_send.at[kind, 2],
            halo_recv.at[kind, one_if_last, 1],
            (below, lf),
        )

    def small_top(kind):
        return remote(
            send_small.at[kind, 1],
            in_small.at[kind, one_if_first, 1],
            halo_send.at[kind, 3],
            halo_recv.at[kind, one_if_first, 2],
            (above, lf),
        )

    def wait_halo(kind, slot):
        remote(
            send_big.at[kind, 0],
            in_big.at[kind, slot, 1 - slot],
            halo_send.at[kind, 0],
            halo_recv.at[kind, slot, 0],
            (dn, lon),
        ).wait_recv()
        for half in range(2):
            remote(
                send_small.at[kind, half],
                in_small.at[kind, slot, half],
                halo_send.at[kind, 2],
                halo_recv.at[kind, slot, 1 + half],
                (dn, lon),
            ).wait_recv()

    def pack_in(src, kind):
        for r in range(WIN_LAT):
            raw[r * COLS : (r + 1) * COLS, :] = src[r].astype(F32)
        for half, first in ((0, RIM_R), (1, 0)):
            base, side = half * 88, 64 + half * 88
            for r in range(RIM_R):
                row = (first + r) * COLS
                tmp[base + r * 12 : base + r * 12 + 12, :] = raw[row + 6 : row + 18, :]
                tmp[base + 36 + r * 6 : base + 42 + r * 6, :] = raw[row + 18 : row + 24, :]
                tmp[side + r * 6 : side + 6 + r * 6, :] = raw[row : row + 6, :]
            piece = tmp[base : base + BIG, :].astype(BF16)
            send_big[kind, half] = piece
            in_big[kind, half, half] = piece
            send_small[kind, half] = tmp[side : side + SMALL, :].astype(BF16)

    def unpack_in(kind, slot):
        for half in range(2):
            base, side = half * 88, 64 + half * 88
            tmp[base : base + BIG, :] = in_big[kind, slot, half].astype(F32)
            tmp[side : side + SMALL, :] = in_small[kind, slot, half].astype(F32)
            xw[36 * half : 36 * half + 36, :] = tmp[base : base + 36, :]
            for r in range(RIM_R):
                row = CELLS + (RIM_R * half + r) * 12
                xw[row : row + 6, :] = tmp[base + 36 + r * 6 : base + 42 + r * 6, :]
                xw[row + 6 : row + 12, :] = tmp[side + r * 6 : side + 6 + r * 6, :]

    tmp[...] = jnp.zeros_like(tmp)
    bias_msg[...] = jnp.zeros_like(bias_msg)
    loads[0].wait()
    for r in range(pairs_here):
        for h in range(HEADS):
            bias_msg[h : h + 1, r * SLOT : r * SLOT + OFFSETS] = bias_in[h, r]
    bias_recv[0, lon] = bias_msg[...]
    around = RUN + steps - 2 + jnp.where(at_start | at_end, 1, 0)
    greetings = jnp.where(is_last, lon_size + 1, around + jnp.where(is_first, 2, 4))
    pl.semaphore_wait(barrier, greetings)

    @pl.when(before_last)
    def _():
        pl.semaphore_signal(ready_sem, inc=1, device_id=(dn, rt), device_id_type=MESH)

    def bias_copy(s):
        return remote(
            bias_msg,
            bias_recv.at[one_if_last, lon],
            bias_send.at[s],
            bias_rsem.at[one_if_last, lon],
            (below, run_peer(s)),
        )

    def bias_arrival(slot, s):
        source = run_peer(s)
        return remote(
            bias_msg,
            bias_recv.at[slot, source],
            bias_send.at[s],
            bias_rsem.at[slot, source],
            (dn, lon),
        )

    def bias_pass(slot, s):
        mine = bias_recv.at[slot, pl.ds(column * RUN, RUN)]
        return remote(
            mine,
            mine,
            pass_send.at[slot, s],
            pass_recv.at[slot, column],
            (lat, column_peer(s) * RUN + inside),
        )

    def bias_passed(slot, s):
        source = column_peer(s)
        theirs = bias_recv.at[slot, pl.ds(source * RUN, RUN)]
        return remote(
            theirs, theirs, pass_send.at[slot, s], pass_recv.at[slot, source], (dn, lon)
        )

    def send_bias(s, carry):
        bias_copy(s).start()
        return carry

    def send_halo(kind):
        @pl.when(is_last)
        def _():
            big_last(kind).start()

        small_low(kind).start()

        @pl.when(jnp.logical_not(is_first))
        def _():
            big_up(kind).start()

        @pl.when(jnp.logical_not(is_last))
        def _():
            small_top(kind).start()

    lax.fori_loop(1 - one_if_last, RUN, send_bias, 0)
    loads[1].wait()
    pack_in(f_in, 0)
    send_halo(0)
    loads[2].wait()
    pack_in(c_in, 1)
    send_halo(1)

    def say_alive(j, carry):
        pl.semaphore_signal(alive_sem, inc=1, device_id=(dn, j), device_id_type=MESH)
        return carry

    @pl.when(is_last)
    def _():
        lax.fori_loop(0, lon_size, say_alive, 0)
        pl.semaphore_wait(ready_sem, 1)
        for kind in range(2):
            small_top(kind).start()

    gflat[...] = jnp.zeros_like(gflat)
    table_msg[...] = jnp.zeros_like(table_msg)
    spread[...] = jnp.zeros_like(spread)

    def make_selectors(b, carry):
        lane = lax.broadcasted_iota(jnp.int32, (BAND, TOKENS), 0)
        query = lax.broadcasted_iota(jnp.int32, (BAND, TOKENS), 1)
        picked = (query // WIN_LON) * SLOT + query % WIN_LON + WIN_LON - 1 - b
        spreader[b] = (lane == picked).astype(F32).astype(BF16)
        lane = lax.broadcasted_iota(jnp.int32, (TOKENS, BAND), 1)
        query = lax.broadcasted_iota(jnp.int32, (TOKENS, BAND), 0)
        picked = (query // WIN_LON) * SLOT + query % WIN_LON + WIN_LON - 1 - b
        gatherer[b] = (lane == picked).astype(F32).astype(BF16)
        return carry

    lax.fori_loop(0, WIN_LON, make_selectors, 0)
    loads[3].wait()
    loads[4].wait()
    loads[5].wait()
    loads[6].wait()
    w_t[...] = w_in[...].astype(F32).T.astype(BF16)
    total_rows = lat_size * WIN_LAT
    key_band = (lax.broadcasted_iota(jnp.int32, (TOKENS, TOKENS), 0) // WIN_LON) % WIN_LAT
    query_band = (lax.broadcasted_iota(jnp.int32, (TOKENS, TOKENS), 1) // WIN_LON) % WIN_LAT

    def back_copy_big(kind, slot):
        return remote(
            res_big.at[kind, slot, 1 - slot],
            back_big.at[kind, 1 - slot],
            back_send.at[kind, slot, 0],
            back_recv.at[kind, 1 - slot],
            (jnp.where(slot == 0, dn, up), lon),
        )

    def back_copy_small(kind, slot, half):
        owner = lax.rem(lat + half - slot + lat_size, lat_size)
        return remote(
            res_small.at[kind, slot, half],
            back_small.at[kind, half],
            back_send.at[kind, slot, 1 + half],
            back_recv.at[kind, 2 + half],
            (owner, rt),
        )

    def give_back(kind, slot, tokens):
        for w in range(WINDOWS):
            cells[w * CELLS : (w + 1) * CELLS, 0:WIDTH] = tokens[w][0:CELLS]
            cells[w * CELLS : (w + 1) * CELLS, WIDTH:] = tokens[w][CELLS:]
        for half in range(2):
            base, side = half * 88, 64 + half * 88
            tmp[base : base + 36, :] = cells[36 * half : 36 * half + 36, :]
            for r in range(RIM_R):
                row = CELLS + (RIM_R * half + r) * 12
                tmp[base + 36 + r * 6 : base + 42 + r * 6, :] = cells[row : row + 6, :]
                tmp[side + r * 6 : side + 6 + r * 6, :] = cells[row + 6 : row + 12, :]
            res_big[kind, slot, half] = tmp[base : base + BIG, :].astype(BF16)
            res_small[kind, slot, half] = tmp[side : side + SMALL, :].astype(BF16)
        for half in range(2):
            back_copy_small(kind, slot, half).start()
        back_copy_big(kind, slot).start()
        back_big[kind, slot] = res_big[kind, slot, slot]

    def table_pass(slot, s):
        target = column_peer(s)
        return remote(
            table_msg.at[slot, pl.ds(target * RUN, RUN)],
            table_mid.at[slot, column],
            table_xsend.at[slot, s],
            table_xrecv.at[slot, column],
            (lat, target * RUN + inside),
        )

    def table_passed(slot, s):
        source = column_peer(s)
        return remote(
            table_msg.at[slot, pl.ds(source * RUN, RUN)],
            table_mid.at[slot, source],
            table_xsend.at[slot, s],
            table_xrecv.at[slot, source],
            (lat, lon),
        )

    def table_copy(slot, s):
        peer = lax.rem(inside + s, RUN)
        return remote(
            table_out.at[slot, peer],
            table_recv.at[inside],
            table_send.at[slot, s],
            table_rsem.at[inside],
            (lat, run_peer(s)),
        )

    def table_arrival(s):
        source = lax.rem(inside + s, RUN)
        return remote(
            table_out.at[0, source],
            table_recv.at[source],
            table_send.at[0, s],
            table_rsem.at[source],
            (lat, run_peer(s)),
        )

    def table_far(j):
        return remote(
            far_msg.at[j],
            far_recv.at[lon],
            far_send.at[j],
            table_rsem.at[lon],
            (up, j),
        )

    def near_table():
        summed = table_msg[0, pl.ds(column * RUN, RUN)]
        for s in range(1, steps):
            table_passed(0, s).wait_recv()
        for s in range(1, steps):
            summed = summed + table_mid[0, column_peer(s)]
        table_out[0] = summed

        def send_table(s, inner):
            table_copy(0, s).start()
            return inner

        lax.fori_loop(1, RUN, send_table, 0)
        table_recv[inside] = table_out[0, inside]

    def window_row(slot, carry):
        def wait_bias(s, inner):
            bias_arrival(slot, s).wait_recv()
            return inner

        lax.fori_loop(1 - slot, RUN, wait_bias, 0)
        for s in range(1, steps):
            bias_pass(slot, s).start()
        gain = gain_ref[...]
        wait_halo(0, slot)
        unpack_in(0, slot)
        for w in range(WINDOWS):
            block = xw[w * CELLS : (w + 1) * CELLS, :]
            x = jnp.concatenate([block[:, :WIDTH], block[:, WIDTH:]], axis=0)
            xtok[w] = x
            center = x - jnp.mean(x, axis=1, keepdims=True)
            inverse = lax.rsqrt(jnp.mean(center * center, axis=1, keepdims=True) + EPS)
            normed = center * inverse
            xhat[w] = normed
            spread_inv[w] = inverse
            x_n = (normed * gain).astype(BF16)
            proj_t[w] = dot_nt(w_t[...], x_n).astype(BF16)
            kv = dot_nn(x_n, w_in[:, WIDTH:]).astype(BF16)
            for h in range(HEADS):
                k_nat[w, h] = kv[:, h * HEAD_DIM : (h + 1) * HEAD_DIM]
                v_nat[w, h] = kv[:, WIDTH + h * HEAD_DIM : WIDTH + (h + 1) * HEAD_DIM]
        wait_halo(1, slot)
        unpack_in(1, slot)
        for w in range(WINDOWS):
            block = xw[w * CELLS : (w + 1) * CELLS, :]
            c = jnp.concatenate([block[:, :WIDTH], block[:, WIDTH:]], axis=0)
            ctok[w] = c
            gmix_t[w] = dot_nt(wo_in[...], c.astype(BF16)).astype(BF16)

        def rows_of(part, h):
            return pl.ds(part * WIDTH + h * HEAD_DIM, HEAD_DIM)

        for h in range(HEADS):
            for w in range(WINDOWS):
                score_buf[w, h] = dot_nn(k_nat[w, h], proj_t[w, rows_of(0, h), :]) * SCALE
                gw_buf[w, h] = dot_nn(v_nat[w, h], gmix_t[w, rows_of(0, h), :])
        first_row = jnp.where(slot == 0, lat, up) * WIN_LAT + RIM_R
        key_row = lax.rem(first_row + key_band, total_rows)
        query_row = lax.rem(first_row + query_band, total_rows)
        real = jnp.zeros((TOKENS, TOKENS), jnp.int32)
        for a in range(WIN_LAT):
            real = jnp.where(key_band == a, pad_ref[lax.rem(first_row + a, total_rows)], real)
        allowed = (jnp.abs(query_row - key_row) < WIN_LAT) & (real == 1)

        for s in range(1, steps):
            bias_passed(slot, s).wait_recv()
        for p in range(PAIRS):
            owner, r = p // pairs_here, p % pairs_here
            zq, zt = p // ZONE, p % ZONE
            spread[zt * 8 : zt * 8 + 8, zq * SLOT : (zq + 1) * SLOT] = bias_recv[
                slot, owner, :, r * SLOT : (r + 1) * SLOT
            ]
        table = spread[...]
        high = table.astype(BF16)
        rest = table - high.astype(F32)
        middle = rest.astype(BF16)
        low = (rest - middle.astype(F32)).astype(BF16)
        rows = ZONE * 8
        stacked = jnp.concatenate([high, middle, low], axis=0)
        for b in range(WIN_LON):
            three = dot_nn(stacked, spreader[b])
            wide = three[0:rows] + (three[rows : 2 * rows] + three[2 * rows :])
            for zt in range(ZONE):
                row = (zt * WIN_LON + b) * 8
                bias_flat[0, row : row + 8, :] = wide[zt * 8 : zt * 8 + 8, 0:128]
                bias_flat[1, row : row + 8, 0 : TOKENS - 128] = wide[
                    zt * 8 : zt * 8 + 8, 128:TOKENS
                ]
        for h in range(HEADS):
            left = bias_flat[0, pl.ds(h, TOKENS, stride=8), :]
            right = bias_flat[1, pl.ds(h, TOKENS, stride=8), :]
            whole = jnp.concatenate([left, right[:, 0 : TOKENS - 128]], axis=1)
            bias_full[h] = jnp.where(allowed, whole, MASKED)

        for h in range(HEADS):
            summed = None
            for w in range(WINDOWS):
                scores = score_buf[w, h] + bias_full[h]
                raised = jnp.exp(scores - jnp.max(scores, axis=0, keepdims=True))
                weights = raised * (1.0 / jnp.sum(raised, axis=0, keepdims=True))
                p_low[w, h] = weights.astype(BF16)
                grad_w = gw_buf[w, h]
                grad_s = weights * (grad_w - jnp.sum(weights * grad_w, axis=0, keepdims=True))
                d_low[w, h] = grad_s.astype(BF16)
                summed = grad_s if summed is None else summed + grad_s
            gflat[0, pl.ds(h, TOKENS, stride=8), :] = summed[:, 0:128]
            gflat[1, pl.ds(h, TOKENS, stride=8), 0 : TOKENS - 128] = summed[:, 128:TOKENS]
        @pl.when(slot == 1)
        def _():
            near_table()

        for h in range(HEADS):
            for w in range(WINDOWS):
                q_t = proj_t[w, rows_of(0, h), :]
                g_t = gmix_t[w, rows_of(0, h), :]
                weights_low = p_low[w, h]
                grad_low = d_low[w, h]
                mixed_t[w, rows_of(0, h), :] = dot_nn(
                    proj_t[w, rows_of(2, h), :], weights_low
                ).astype(BF16)
                gproj_t[w, rows_of(0, h), :] = (
                    dot_nn(proj_t[w, rows_of(1, h), :], grad_low) * SCALE
                ).astype(BF16)
                gproj_t[w, rows_of(1, h), :] = (dot_nt(q_t, grad_low) * SCALE).astype(BF16)
                gproj_t[w, rows_of(2, h), :] = dot_nt(g_t, weights_low).astype(BF16)

        give_back(
            0, slot, [xtok[w] + dot_tn(mixed_t[w], wo_in[...]) for w in range(WINDOWS)]
        )
        grads = []
        for w in range(WINDOWS):
            scaled = dot_tn(gproj_t[w], w_t[...]) * gain
            normed = xhat[w]
            centered = (
                scaled
                - jnp.mean(scaled, axis=1, keepdims=True)
                - normed * jnp.mean(scaled * normed, axis=1, keepdims=True)
            )
            grads.append(ctok[w] + spread_inv[w] * centered)
        give_back(1, slot, grads)

        total = jnp.zeros((ZONE * 8, BAND), F32)
        for b in range(WIN_LON):
            picked_rows = []
            for zt in range(ZONE):
                row = (zt * WIN_LON + b) * 8
                picked_rows.append(
                    jnp.concatenate(
                        [
                            gflat[0, row : row + 8, :],
                            gflat[1, row : row + 8, 0 : TOKENS - 128],
                        ],
                        axis=1,
                    )
                )
            part = jnp.concatenate(picked_rows, axis=0).astype(BF16)
            total = total + dot_nn(part, gatherer[b])
        spread[...] = total
        for p in range(PAIRS):
            owner, r = p // pairs_here, p % pairs_here
            zq, zt = p // ZONE, p % ZONE
            table_msg[slot, owner, :, r * SLOT : (r + 1) * SLOT] = spread[
                zt * 8 : zt * 8 + 8, zq * SLOT : (zq + 1) * SLOT
            ]

        @pl.when(slot == 0)
        def _():
            for s in range(1, steps):
                table_pass(0, s).start()

        @pl.when(slot == 1)
        def _():
            far_msg[...] = table_msg[1].astype(BF16)
            pl.semaphore_wait(alive_sem, lon_size)

            def send_far(j, inner):
                table_far(j).start()
                return inner

            lax.fori_loop(0, lon_size, send_far, 0)

        return carry

    rows_here = 1 + one_if_first - one_if_last
    lax.fori_loop(0, rows_here, window_row, 0)

    def take_back(kind, dst):
        def arrived_big(half):
            remote(
                res_big.at[kind, 0, half],
                back_big.at[kind, half],
                back_send.at[kind, 0, 0],
                back_recv.at[kind, half],
                (dn, lon),
            ).wait_recv()

        @pl.when(is_last)
        def _():
            arrived_big(0)

        @pl.when(jnp.logical_not(is_first))
        def _():
            arrived_big(1)

        for half in range(2):
            remote(
                res_small.at[kind, 0, half],
                back_small.at[kind, half],
                back_send.at[kind, 0, 1],
                back_recv.at[kind, 2 + half],
                (dn, rt),
            ).wait_recv()
        for half, first in ((0, RIM_R), (1, 0)):
            base, side = half * 88, 64 + half * 88
            tmp[base : base + BIG, :] = back_big[kind, half].astype(F32)
            tmp[side : side + SMALL, :] = back_small[kind, half].astype(F32)
            for r in range(RIM_R):
                row = (first + r) * COLS
                raw[row + 6 : row + 18, :] = tmp[base + r * 12 : base + r * 12 + 12, :]
                raw[row + 18 : row + 24, :] = tmp[base + 36 + r * 6 : base + 42 + r * 6, :]
                raw[row : row + 6, :] = tmp[side + r * 6 : side + 6 + r * 6, :]
        for r in range(WIN_LAT):
            dst[r] = raw[r * COLS : (r + 1) * COLS, :].astype(BF16)

    @pl.when(jnp.logical_not(is_first | is_last))
    def _():
        near_table()

    take_back(0, out_ref)
    take_back(1, grads_ref)

    def wait_table(s, carry):
        table_arrival(s).wait_recv()
        return carry

    def wait_far(j, carry):
        remote(
            far_msg.at[j],
            far_recv.at[j],
            far_send.at[j],
            table_rsem.at[j],
            (up, j),
        ).wait_recv()
        return carry

    @pl.when(is_last)
    def _():
        lax.fori_loop(0, lon_size, wait_far, 0)
        table_recv[...] = far_recv[...].astype(F32)

    @pl.when(jnp.logical_not(is_last))
    def _():
        lax.fori_loop(1, RUN, wait_table, 0)
        table_recv[RUN:lon_size] = jnp.zeros_like(table_recv[RUN:lon_size])

    added = table_recv[0]
    for j in range(1, lon_size):
        added = added + table_recv[j]
    for r in range(pairs_here):
        piece = added[:, r * SLOT : r * SLOT + OFFSETS]
        for h in range(HEADS):
            table_ref[h, r] = piece[h : h + 1, :]

    for kind in range(2):

        @pl.when(is_last)
        def _():
            big_last(kind).wait_send()

        @pl.when(jnp.logical_not(is_first))
        def _():
            big_up(kind).wait_send()

        small_low(kind).wait_send()
        small_top(kind).wait_send()

    def drain_bias(s, carry):
        bias_copy(s).wait_send()
        return carry

    lax.fori_loop(1 - one_if_last, RUN, drain_bias, 0)

    def drain_row(slot, carry):
        for kind in range(2):
            back_copy_big(kind, slot).wait_send()
            for half in range(2):
                back_copy_small(kind, slot, half).wait_send()

        for s in range(1, steps):
            bias_pass(slot, s).wait_send()

        @pl.when(slot == 0)
        def _():
            for s in range(1, steps):
                table_pass(0, s).wait_send()
            for s in range(1, RUN):
                table_copy(0, s).wait_send()

        @pl.when(slot == 1)
        def _():
            def drain_far(j, inner):
                table_far(j).wait_send()
                return inner

            lax.fori_loop(0, lon_size, drain_far, 0)

        return carry

    lax.fori_loop(0, rows_here, drain_row, 0)


def place_out(*refs):
    sources, targets, sem = refs[:3], refs[3:6], refs[6]
    copies = [
        pltpu.make_async_copy(src, dst, sem.at[n])
        for n, (src, dst) in enumerate(zip(sources, targets))
    ]
    for copy in copies:
        copy.start()
    for copy in copies:
        copy.wait()


def solution(mesh):
    lat_size, lon_size = mesh.shape["lat"], mesh.shape["lon"]
    pairs_here = PAIRS // lon_size
    lanes = -(-pairs_here * SLOT // 128) * 128

    def per_device(fields, norm_gain, project_in, project_out, bias_table, pad_rows, cotangent):
        hbm_spec = pl.BlockSpec(memory_space=pltpu.HBM)
        vmem_spec = pl.BlockSpec(memory_space=pltpu.VMEM)
        out_fields, field_grads, table_grads = pl.pallas_call(
            functools.partial(kernel, lat_size, lon_size, pairs_here),
            out_shape=(
                jax.ShapeDtypeStruct(fields.shape, BF16),
                jax.ShapeDtypeStruct(fields.shape, BF16),
                jax.ShapeDtypeStruct((HEADS, pairs_here, 1, OFFSETS), F32),
            ),
            in_specs=[hbm_spec] * 7,
            out_specs=(vmem_spec, vmem_spec, vmem_spec),
            scratch_shapes=[
                pltpu.VMEM(fields.shape, BF16),
                pltpu.VMEM(fields.shape, BF16),
                pltpu.VMEM(project_in.shape, BF16),
                pltpu.VMEM(project_out.shape, BF16),
                pltpu.VMEM((HEADS, pairs_here, 1, OFFSETS), F32),
                pltpu.VMEM((1, WIDTH), F32),
                pltpu.SMEM(pad_rows.shape, jnp.int32),
                pltpu.VMEM((WIN_LAT * COLS, FEATS), F32),
                pltpu.VMEM((WINDOWS * CELLS, FEATS), F32),
                pltpu.VMEM((176, FEATS), F32),
                pltpu.VMEM((2, 2, BIG, FEATS), BF16),
                pltpu.VMEM((2, 2, SMALL, FEATS), BF16),
                pltpu.VMEM((2, 2, 2, BIG, FEATS), BF16),
                pltpu.VMEM((2, 2, 2, SMALL, FEATS), BF16),
                pltpu.VMEM((2, 2, 2, BIG, FEATS), BF16),
                pltpu.VMEM((2, 2, 2, SMALL, FEATS), BF16),
                pltpu.VMEM((2, 2, BIG, FEATS), BF16),
                pltpu.VMEM((2, 2, SMALL, FEATS), BF16),
                pltpu.VMEM((8, lanes), F32),
                pltpu.VMEM((2, lon_size, 8, lanes), F32),
                pltpu.VMEM((ZONE * 8, BAND), F32),
                pltpu.VMEM((2, TOKENS * 8, 128), F32),
                pltpu.VMEM((HEADS, TOKENS, TOKENS), F32),
                pltpu.VMEM((3 * WIDTH, WIDTH), BF16),
                pltpu.VMEM((WINDOWS, TOKENS, WIDTH), F32),
                pltpu.VMEM((WINDOWS, TOKENS, WIDTH), F32),
                pltpu.VMEM((WINDOWS, TOKENS, WIDTH), F32),
                pltpu.VMEM((WINDOWS, TOKENS, 1), F32),
                pltpu.VMEM((WINDOWS, 3 * WIDTH, TOKENS), BF16),
                pltpu.VMEM((WINDOWS, HEADS, TOKENS, HEAD_DIM), BF16),
                pltpu.VMEM((WINDOWS, HEADS, TOKENS, HEAD_DIM), BF16),
                pltpu.VMEM((WINDOWS, WIDTH, TOKENS), BF16),
                pltpu.VMEM((WINDOWS, WIDTH, TOKENS), BF16),
                pltpu.VMEM((WINDOWS, 3 * WIDTH, TOKENS), BF16),
                pltpu.VMEM((2, TOKENS * 8, 128), F32),
                pltpu.VMEM((WINDOWS * CELLS, FEATS), F32),
                pltpu.VMEM((2, lon_size, 8, lanes), F32),
                pltpu.VMEM((2, lon_size // RUN, RUN, 8, lanes), F32),
                pltpu.VMEM((2, RUN, 8, lanes), F32),
                pltpu.VMEM((lon_size, 8, lanes), BF16),
                pltpu.VMEM((lon_size, 8, lanes), BF16),
                pltpu.VMEM((lon_size, 8, lanes), F32),
                pltpu.VMEM((WIN_LON, BAND, TOKENS), BF16),
                pltpu.VMEM((WIN_LON, TOKENS, BAND), BF16),
                pltpu.VMEM((WINDOWS, HEADS, TOKENS, TOKENS), F32),
                pltpu.VMEM((WINDOWS, HEADS, TOKENS, TOKENS), F32),
                pltpu.VMEM((WINDOWS, HEADS, TOKENS, TOKENS), BF16),
                pltpu.VMEM((WINDOWS, HEADS, TOKENS, TOKENS), BF16),
                pltpu.SemaphoreType.DMA((7,)),
                pltpu.SemaphoreType.DMA((2, 4)),
                pltpu.SemaphoreType.DMA((2, 2, 3)),
                pltpu.SemaphoreType.DMA((2, 2, 3)),
                pltpu.SemaphoreType.DMA((2, 4)),
                pltpu.SemaphoreType.DMA((RUN,)),
                pltpu.SemaphoreType.DMA((2, lon_size)),
                pltpu.SemaphoreType.DMA((2, lon_size // RUN)),
                pltpu.SemaphoreType.DMA((2, lon_size // RUN)),
                pltpu.SemaphoreType.DMA((2, lon_size // RUN)),
                pltpu.SemaphoreType.DMA((2, lon_size // RUN)),
                pltpu.SemaphoreType.DMA((2, RUN)),
                pltpu.SemaphoreType.DMA((lon_size,)),
                pltpu.SemaphoreType.DMA((lon_size,)),
                pltpu.SemaphoreType.REGULAR,
                pltpu.SemaphoreType.REGULAR,
            ],
            compiler_params=pltpu.CompilerParams(
                collective_id=0, has_side_effects=True, vmem_limit_bytes=48 << 20
            ),
        )(
            *(
                pltpu.with_memory_space_constraint(x, pltpu.HBM)
                for x in (
                    fields,
                    norm_gain.reshape(1, WIDTH),
                    project_in,
                    project_out,
                    bias_table.reshape(HEADS, pairs_here, 1, OFFSETS),
                    pad_rows,
                    cotangent,
                )
            )
        )
        parts = (out_fields, field_grads, table_grads)
        any_spec = pl.BlockSpec(memory_space=pl.ANY)
        out_fields, field_grads, table_grads = pl.pallas_call(
            place_out,
            out_shape=tuple(jax.ShapeDtypeStruct(x.shape, x.dtype) for x in parts),
            in_specs=[any_spec] * 3,
            out_specs=(hbm_spec,) * 3,
            scratch_shapes=[pltpu.SemaphoreType.DMA((3,))],
            compiler_params=pltpu.CompilerParams(vmem_limit_bytes=1 << 20),
        )(*parts)
        return out_fields, field_grads, table_grads.reshape(bias_table.shape)

    in_specs = (
        P("lat", "lon", None),
        P(),
        P(),
        P(),
        P("lat", None, "lon", None),
        P(),
        P("lat", "lon", None),
    )
    out_specs = (P("lat", "lon", None), P("lat", "lon", None), P("lat", None, "lon", None))
    return jax.shard_map(
        per_device, mesh=mesh, in_specs=in_specs, out_specs=out_specs, check_vma=False
    )
```
